32 devices in a mesh: groups: 2 (over x), tgt: 16 (over z, y, core).
Axes of the slice: x: 2, y: 2, z: 4, core: 2. Of those that a mesh axis runs over, the one named last changes fastest.
Arguments:
- source_feats: bfloat16 [4096, 1024], P(('groups', 'tgt')), parts along dimension 0, may hold values from -18 to 18
- target_feats: bfloat16 [16384, 1024], P(('groups', 'tgt')), parts along dimension 0, may hold values from -18 to 18
- source_logits: float32 [4096], P('groups'), parts along dimension 0, may hold values from -1.2 to 1.2
- target_logits: float32 [16384], P(('groups', 'tgt')), parts along dimension 0, may hold values from -1 to 3.4
Outputs:
- grad_source: float32 [4096, 1024], P(('groups', 'tgt')), parts along dimension 0
- grad_target: float32 [16384, 1024], P(('groups', 'tgt')), parts along dimension 0
- potential_src: float32 [4096], P('groups'), parts along dimension 0
- potential_tgt: float32 [16384], P(('groups', 'tgt')), parts along dimension 0
The draws below stay inside these ranges and needn't reach their ends.
There are 2 independent parts, one for each index of `groups`. The reference program is written for one: setup_inputs(seed, part) draws one part's arguments, and reference() takes and returns one part's arrays. A program takes and returns all parts, laid end to end along the dimension named above; each array names one. Nothing has to cross between parts.
All inputs are finite; a program needn't handle non-finite values.
Results may differ from the reference program's by a relative error of at most 0.0033.
Values may be sent and summed in bfloat16 or wider, within the bound.
No kernel may reach another device: no remote copies, remote signals or barrier semaphores. Data moves between devices by JAX's collectives and lax.ppermute only.
A program may use at most 64 MiB of HBM per device.

```python
import math
import jax
import jax.numpy as jnp
from jax import lax

D = 1024
S = 2048
ITERS = 3
NT = 8192


def feature_pair(key):
    base = jax.random.fold_in(key, 7)
    key_src, key_tgt = jax.random.split(base, 2)
    source = jax.random.normal(key_src, (S, D), jnp.float32)
    target = jax.random.normal(key_tgt, (NT, D), jnp.float32)
    return (jnp.clip(source, -18.0, 18.0), jnp.clip(target, -18.0, 18.0))


def draw_source_feats(key, part):
    return feature_pair(key)[0].astype(jnp.bfloat16)


def draw_target_feats(key, part):
    return feature_pair(key)[1].astype(jnp.bfloat16)


def draw_target_logits(key, part):
    spread = jax.random.uniform(jax.random.fold_in(key, 11), (NT,), jnp.float32, -1.0, 1.0)
    ramp = jnp.arange(NT, dtype=jnp.float32) / NT
    return spread + 1.2 * ramp


def setup_inputs(seed: int = 0, part: int = 0) -> dict:
    streams_of = jax.random.split(jax.random.key(seed), 5)
    own_keys = jax.random.split(jax.random.fold_in(streams_of[4], part), 5)
    return {
        "source_feats": draw_source_feats(jax.random.fold_in(jax.random.fold_in(streams_of[4], part), 71), part),
        "target_feats": draw_target_feats(jax.random.fold_in(jax.random.fold_in(streams_of[4], part), 71), part),
        "source_logits": jnp.clip(jax.random.uniform(own_keys[2], (S,), jnp.float32, -1.2, 1.2), -1.2, 1.2),
        "target_logits": draw_target_logits(jax.random.fold_in(jax.random.fold_in(streams_of[4], part), 71), part),
    }


def reference(source_feats, target_feats, source_logits, target_logits):
    log_source = source_logits - jnp.log(jnp.sum(jnp.exp(source_logits)))
    log_target = target_logits - jnp.log(jnp.sum(jnp.exp(target_logits)))
    source_sq = lax.optimization_barrier(jnp.sum(jnp.square(source_feats.astype(jnp.float32)), axis=1))
    target_sq = lax.optimization_barrier(jnp.sum(jnp.square(target_feats.astype(jnp.float32)), axis=1))
    cross = lax.dot_general(source_feats, target_feats, (((1,), (1,)), ((), ())), preferred_element_type=jnp.float32)
    cost = (source_sq[:, None] + target_sq[None, :] - 2.0 * cross) * (1.0 / math.sqrt(D))
    potential_tgt = jnp.zeros((NT,), jnp.float32)
    potential_src = jnp.zeros((S,), jnp.float32)
    for step in range(ITERS):
        potential_src = -jax.nn.logsumexp((log_target + potential_tgt)[None, :] - cost, axis=1)
        potential_tgt = -jax.nn.logsumexp((log_source + potential_src)[:, None] - cost, axis=0)
    plan = jnp.exp(math.log(S) + (log_source + potential_src)[:, None] + (log_target + potential_tgt)[None, :] - cost).astype(jnp.bfloat16)
    row_part = jnp.dot(plan, target_feats, preferred_element_type=jnp.float32)
    row_mass = lax.optimization_barrier(jnp.sum(plan.astype(jnp.float32), axis=1))
    grad_source = row_mass[:, None] * source_feats.astype(jnp.float32) - row_part
    col_part = lax.dot_general(plan, source_feats, (((0,), (0,)), ((), ())), preferred_element_type=jnp.float32)
    col_mass = lax.optimization_barrier(jnp.sum(plan.astype(jnp.float32), axis=0))
    grad_target = NT / S * (col_mass[:, None] * target_feats.astype(jnp.float32) - col_part)
    return (grad_source, grad_target, potential_src, potential_tgt)
```

```python
import functools
import math

import jax
import jax.numpy as jnp
from jax import lax
from jax.experimental import pallas as pl
from jax.experimental.pallas import tpu as pltpu
from jax.sharding import PartitionSpec as P

ITERS = 3
AXIS = "tgt"
VMEM = pl.BlockSpec(memory_space=pltpu.VMEM)
F32 = jnp.float32
BF16 = jnp.bfloat16


def params(mib):
    return pltpu.CompilerParams(vmem_limit_bytes=mib << 20)


def swap(value, mask):
    count = lax.axis_size(AXIS)
    return lax.ppermute(value, AXIS, [(i, i ^ mask) for i in range(count)])


def tree_levels(count):
    levels, step = [], 1
    while step < count:
        if step * 4 <= count:
            levels.append((step, 2 * step, 3 * step))
            step *= 4
        else:
            levels.append((step,))
            step *= 2
    return levels


def flip_blocks(value, mask, count):
    lead = value.shape[:-1]
    width = value.shape[-1] // count
    blocks = [value[..., (r ^ mask) * width : ((r ^ mask) + 1) * width] for r in range(count)]
    return jnp.concatenate(blocks, axis=-1)


def cost_kernel(scale, blocks, *refs):
    x_refs = refs[:blocks]
    y_ref, u_ref, s_ref, top_ref, sum_ref, x_out = refs[blocks:]
    rows = x_refs[0].shape[0]
    for q in range(blocks):
        x_out[q * rows : (q + 1) * rows, :] = x_refs[q][...]
    s = scale * lax.dot_general(
        y_ref[...], x_out[...], (((1,), (1,)), ((), ())), preferred_element_type=F32
    )
    s_ref[...] = s
    shifted = s + u_ref[...]
    top = jnp.max(shifted, axis=0, keepdims=True)
    top_ref[...] = top
    sum_ref[...] = jnp.sum(jnp.exp(shifted - top), axis=0, keepdims=True)


def first_column_kernel(chunks, *refs):
    s_refs = refs[:chunks]
    q_ref, w_ref, p_ref, row_ref, g_ref = refs[chunks:]
    width = s_refs[0].shape[1]
    q = q_ref[...]
    parts = [s_refs[k][...] + q[:, k * width : (k + 1) * width] for k in range(chunks)]
    top = functools.reduce(
        jnp.maximum, [jnp.max(part, axis=1, keepdims=True) for part in parts]
    )
    parts = [jnp.exp(part - top) for part in parts]
    total = functools.reduce(
        jnp.add, [jnp.sum(part, axis=1, keepdims=True) for part in parts]
    )
    g_ref[...] = -(top + jnp.log(total))
    inverse = 1.0 / total

    @pl.when(pl.program_id(0) == 0)
    def _():
        row_ref[...] = jnp.zeros_like(row_ref)

    for k in range(chunks):
        p = parts[k] * inverse
        p_ref[:, k * width : (k + 1) * width] = p
        row_ref[:, k * width : (k + 1) * width] += jnp.sum(
            p * w_ref[...], axis=0, keepdims=True
        )


def step_kernel(p_ref, a_ref, w_ref, row_ref):
    p = p_ref[...]
    c = jnp.sum(p * a_ref[...], axis=1, keepdims=True)

    @pl.when(pl.program_id(0) == 0)
    def _():
        row_ref[...] = jnp.zeros_like(row_ref)

    row_ref[...] += jnp.sum(p * (w_ref[...] / c), axis=0, keepdims=True)


def plan_kernel(chunks, p_ref, a_ref, w_ref, *refs):
    plan_refs = refs[:chunks]
    logb_ref, col_ref, row_ref = refs[chunks:]
    p = p_ref[...] * a_ref[...]
    c = jnp.sum(p, axis=1, keepdims=True)
    logb_ref[...] = -jnp.log(c)
    plan = (p * (w_ref[...] / c)).astype(BF16)
    width = plan_refs[0].shape[1]
    for k in range(chunks):
        plan_refs[k][...] = plan[:, k * width : (k + 1) * width]
    wide = plan.astype(F32)
    col_ref[...] = jnp.sum(wide, axis=1, keepdims=True)

    @pl.when(pl.program_id(0) == 0)
    def _():
        row_ref[...] = jnp.zeros_like(row_ref)

    row_ref[...] += jnp.sum(wide, axis=0, keepdims=True)


def all_sum(vector, count):
    for level in tree_levels(count):
        vector = vector + sum(
            flip_blocks(swap(vector, mask), mask, count) for mask in level
        )
    return vector


def all_lse(top, total, extra, count):
    for level in tree_levels(count):
        packed = jnp.concatenate([top, total, extra], axis=1)
        width = top.shape[1]
        tops, totals, extras = [top], [total], [extra]
        for mask in level:
            other = swap(packed, mask)
            tops.append(flip_blocks(other[:, :width], mask, count))
            totals.append(flip_blocks(other[:, width : 2 * width], mask, count))
            extras.append(other[:, 2 * width :])
        top = functools.reduce(jnp.maximum, tops)
        total = sum(t * jnp.exp(m - top) for m, t in zip(tops, totals))
        extra = sum(extras)
    return top, total, extra


def per_device(source_feats, target_feats, source_logits, target_logits):
    count = lax.axis_size(AXIS)
    me = lax.axis_index(AXIS)
    rows, width = source_feats.shape
    cols = target_feats.shape[0]
    source_count = rows * count
    target_count = cols * count
    scale = 1.0 / math.sqrt(width)
    direct = count == 16
    chunks = 4
    chunk = source_count // chunks
    order = jnp.bitwise_xor(me, jnp.arange(count))

    by_chunk = []
    if direct:
        for k in range(chunks):
            block = source_feats if k == 0 else swap(source_feats, 4 * k)
            pair = [block, swap(block, 2)]
            by_chunk.append([pair[0], swap(pair[0], 1), pair[1], swap(pair[1], 1)])
    else:
        gathered = lax.all_gather(source_feats, AXIS, axis=0)[order]
        gathered = gathered.reshape(chunks, chunk, width)
        by_chunk = [[gathered[k]] for k in range(chunks)]

    target_weight = jnp.exp(target_logits)[:, None]
    target_sq = scale * jnp.sum(jnp.square(target_feats.astype(F32)), axis=1, keepdims=True)
    lift = target_logits[:, None] - target_sq

    cost_call = pl.pallas_call(
        functools.partial(cost_kernel, 2.0 * scale, len(by_chunk[0])),
        name="cost",
        out_shape=(
            jax.ShapeDtypeStruct((cols, chunk), F32),
            jax.ShapeDtypeStruct((1, chunk), F32),
            jax.ShapeDtypeStruct((1, chunk), F32),
            jax.ShapeDtypeStruct((chunk, width), BF16),
        ),
        in_specs=[VMEM] * (len(by_chunk[0]) + 2),
        out_specs=(VMEM,) * 4,
        compiler_params=params(24),
        cost_estimate=pl.CostEstimate(
            flops=2 * cols * chunk * width, bytes_accessed=5 << 20, transcendentals=cols * chunk
        ),
    )
    scores, tops, sums, feats = zip(
        *[cost_call(*blocks, target_feats, lift) for blocks in by_chunk]
    )

    source_rel = source_logits.reshape(count, rows)[order].reshape(1, source_count)
    source_log = source_rel - jnp.log(jnp.sum(jnp.exp(source_logits)))
    source_mass = jnp.exp(source_log)

    local_total = jnp.broadcast_to(jnp.sum(target_weight), (1, 128))
    top, total, target_total = all_lse(
        jnp.concatenate(tops, axis=1), jnp.concatenate(sums, axis=1), local_total, count
    )
    target_total = target_total[:, :1]
    f1 = jnp.log(target_total) - (top + jnp.log(total))

    tile = 64
    grid = (cols // tile,)
    tall = pl.BlockSpec((tile, source_count), lambda j: (j, 0))
    thin = pl.BlockSpec((tile, 1), lambda j: (j, 0))
    flat = pl.BlockSpec((1, source_count), lambda j: (0, 0))
    part = pl.BlockSpec((tile, chunk), lambda j: (j, 0))
    thin_shape = jax.ShapeDtypeStruct((cols, 1), F32)
    flat_shape = jax.ShapeDtypeStruct((1, source_count), F32)

    p1, row, g1 = pl.pallas_call(
        functools.partial(first_column_kernel, chunks),
        name="first_column",
        grid=grid,
        out_shape=(jax.ShapeDtypeStruct((cols, source_count), F32), flat_shape, thin_shape),
        in_specs=[part] * chunks + [flat, thin],
        out_specs=(tall, flat, thin),
        compiler_params=params(24),
    )(*scores, source_log + f1, target_weight)

    scaled_mass = source_mass * target_total
    for _ in range(ITERS - 2):
        ratio = scaled_mass / all_sum(row, count)
        row = pl.pallas_call(
            step_kernel,
            name="step",
            grid=grid,
            out_shape=flat_shape,
            in_specs=[tall, flat, thin],
            out_specs=flat,
            compiler_params=params(24),
        )(p1, ratio, target_weight)
    ratio = scaled_mass / all_sum(row, count)

    *plans, logb, col_mass, row_mass = pl.pallas_call(
        functools.partial(plan_kernel, chunks),
        name="plan",
        grid=grid,
        out_shape=[jax.ShapeDtypeStruct((cols, chunk), BF16)] * chunks
        + [thin_shape, thin_shape, flat_shape],
        in_specs=[tall, flat, thin],
        out_specs=[part] * chunks + [thin, thin, flat],
        compiler_params=params(24),
    )(p1, ratio, target_weight * (source_count / target_total))

    row_part = None
    if not direct:
        full = lax.dot_general(
            jnp.concatenate(plans, axis=1),
            target_feats,
            (((0,), (0,)), ((), ())),
            preferred_element_type=F32,
        ).reshape(count, rows, width)[order]
        row_part = lax.psum_scatter(full, AXIS, scatter_dimension=0)
    for k in [3, 2, 1, 0] if direct else []:
        full = lax.dot_general(
            plans[k], target_feats, (((0,), (0,)), ((), ())), preferred_element_type=F32
        ).reshape(2, 2, rows, width)
        chip = full[:, 0] + swap(full[:, 1], 1)
        line = chip[0] + swap(chip[1].astype(BF16), 2).astype(F32)
        if k:
            line = swap(line.astype(BF16), 4 * k).astype(F32)
        row_part = line if row_part is None else row_part + line

    mass = all_sum(row_mass, count)[0, :rows]
    grad_source = mass[:, None] * source_feats.astype(F32) - row_part

    col_part = sum(
        lax.dot_general(plans[k], feats[k], (((1,), (0,)), ((), ())), preferred_element_type=F32)
        for k in range(chunks)
    )
    grad_target = (target_count / source_count) * (
        col_mass * target_feats.astype(F32) - col_part
    )

    source_sq = scale * jnp.concatenate(
        [jnp.sum(jnp.square(x.astype(F32)), axis=1) for x in feats]
    )
    potential_src = (f1 + jnp.log(ratio)).reshape(source_count) + source_sq
    potential_src = potential_src.reshape(count, rows)[order].reshape(source_count)
    potential_tgt = (g1 + logb + target_sq).reshape(cols)
    return (grad_source, grad_target, potential_src, potential_tgt)


def solution(mesh):
    return jax.shard_map(
        per_device,
        mesh=mesh,
        in_specs=(
            P(("groups", "tgt"), None),
            P(("groups", "tgt"), None),
            P("groups"),
            P(("groups", "tgt")),
        ),
        out_specs=(
            P(("groups", "tgt"), None),
            P(("groups", "tgt"), None),
            P("groups"),
            P(("groups", "tgt")),
        ),
        check_vma=False,
    )
```

```python
import functools
import math

import jax
import jax.numpy as jnp
from jax import lax
from jax.experimental import pallas as pl
from jax.experimental.pallas import tpu as pltpu
from jax.sharding import PartitionSpec as P

ITERS = 3
AXIS = "tgt"
F32 = jnp.float32
BF16 = jnp.bfloat16
TAIL = 8


def call(body, name, ins, outs, grid=(), in_specs=None, out_specs=None, flops=0, **kw):
    def whole(a):
        return pl.BlockSpec(a.shape, lambda *_: (0,) * len(a.shape))

    size = sum(math.prod(a.shape) * jnp.dtype(a.dtype).itemsize for a in [*ins, *outs])
    return pl.pallas_call(
        body,
        name=name,
        grid=grid,
        out_shape=outs,
        in_specs=in_specs or [whole(a) for a in ins],
        out_specs=out_specs or [whole(a) for a in outs],
        compiler_params=pltpu.CompilerParams(vmem_limit_bytes=56 << 20),
        cost_estimate=pl.CostEstimate(flops=flops, bytes_accessed=size, transcendentals=0),
        **kw,
    )(*ins)


def shape(dims, dtype=F32):
    return jax.ShapeDtypeStruct(dims, dtype)


def swap(value, mask):
    count = lax.axis_size(AXIS)
    return lax.ppermute(value, AXIS, [(i, i ^ mask) for i in range(count)])


def tree_levels(count):
    levels, step = [], 1
    while step < count:
        if step * 4 <= count:
            levels.append((step, 2 * step, 3 * step))
            step *= 4
        else:
            levels.append((step,))
            step *= 2
    return levels


def flip(value, mask, count):
    width = value.shape[-1] // count
    blocks = [value[..., (r ^ mask) * width : ((r ^ mask) + 1) * width] for r in range(count)]
    return jnp.concatenate(blocks, axis=-1)


def cost_kernel(scale, blocks, chunk_index, *refs):
    x_refs = refs[:blocks]
    y_ref, u_ref, w_ref, pack_ref, s_ref, x_out, pack_out = refs[blocks:]
    rows = x_refs[0].shape[0]
    chunk = rows * blocks
    for q in range(blocks):
        x_out[q * rows : (q + 1) * rows, :] = x_refs[q][...]
    s = scale * lax.dot_general(
        y_ref[...], x_out[...], (((1,), (1,)), ((), ())), preferred_element_type=F32
    )
    s_ref[...] = s
    shifted = s + u_ref[...]
    top = jnp.max(shifted, axis=0, keepdims=True)
    half = (pack_ref.shape[1] - 128) // 2
    pack_out[...] = pack_ref[...]
    start = chunk_index * chunk
    pack_out[:, start : start + chunk] = top
    pack_out[:, half + start : half + start + chunk] = jnp.sum(
        jnp.exp(shifted - top), axis=0, keepdims=True
    )
    total = jnp.sum(w_ref[...], axis=0, keepdims=True)
    pack_out[:, 2 * half :] = jnp.broadcast_to(total, (1, 128))


def merge(packs, masks, count):
    half = (packs[0].shape[1] - 128) // 2
    tops = [flip(p[:, :half], m, count) for p, m in zip(packs, masks)]
    sums = [flip(p[:, half : 2 * half], m, count) for p, m in zip(packs, masks)]
    top = functools.reduce(jnp.maximum, tops)
    total = sum(s * jnp.exp(t - top) for t, s in zip(tops, sums))
    return top, total, sum(p[:, 2 * half :] for p in packs)


def merge_kernel(masks, count, *refs):
    top, total, mass = merge([r[...] for r in refs[:-1]], masks, count)
    half = top.shape[1]
    refs[-1][:, :half] = top
    refs[-1][:, half : 2 * half] = total
    refs[-1][:, 2 * half :] = mass


def first_kernel(chunks, masks, count, source_count, *refs):
    s_refs, refs = refs[:chunks], refs[chunks:]
    pack_refs, refs = refs[: len(masks)], refs[len(masks) :]
    logit_ref, w_ref, q_ref, h_ref, row_ref, g_ref, share_ref = refs
    width = s_refs[0].shape[1]

    @pl.when(pl.program_id(0) == 0)
    def _():
        top, total, mass = merge([r[...] for r in pack_refs], masks, count)
        logit = logit_ref[...]
        h = logit - jnp.log(jnp.sum(jnp.exp(logit))) + jnp.log(mass[:, :1])
        h_ref[...] = h
        q_ref[...] = h - top - jnp.log(total)
        row_ref[...] = jnp.zeros_like(row_ref)

    mass = sum(r[:, r.shape[1] - 1 :] for r in pack_refs)
    w = w_ref[...]
    share_ref[...] = w * (source_count / mass)
    q = q_ref[...]
    parts = [s_refs[k][...] + q[:, k * width : (k + 1) * width] for k in range(chunks)]
    top = functools.reduce(jnp.maximum, [jnp.max(p, axis=1, keepdims=True) for p in parts])
    parts = [jnp.exp(p - top) for p in parts]
    total = sum(jnp.sum(p, axis=1, keepdims=True) for p in parts)
    g_ref[...] = -(top + jnp.log(total))
    w = w / total
    for k in range(chunks):
        row_ref[:, k * width : (k + 1) * width] += jnp.sum(parts[k] * w, axis=0, keepdims=True)


def advance(sum_refs, masks, count, q_ref, h_ref, q_out):
    total = sum(flip(r[...], m, count) for r, m in zip(sum_refs, masks))
    q_out[...] = q_ref[...] + h_ref[...] - jnp.log(total)


def step_kernel(chunks, masks, count, *refs):
    s_refs, refs = refs[:chunks], refs[chunks:]
    sum_refs, refs = refs[: len(masks)], refs[len(masks) :]
    q_ref, h_ref, w_ref, g_ref, q_out, row_ref = refs
    width = s_refs[0].shape[1]

    @pl.when(pl.program_id(0) == 0)
    def _():
        advance(sum_refs, masks, count, q_ref, h_ref, q_out)
        row_ref[...] = jnp.zeros_like(row_ref)

    q, g = q_out[...], g_ref[...]
    parts = [
        jnp.exp(s_refs[k][...] + q[:, k * width : (k + 1) * width] + g) for k in range(chunks)
    ]
    w = w_ref[...] / sum(jnp.sum(p, axis=1, keepdims=True) for p in parts)
    for k in range(chunks):
        row_ref[:, k * width : (k + 1) * width] += jnp.sum(parts[k] * w, axis=0, keepdims=True)


def plan_kernel(chunks, masks, count, *refs):
    s_refs, refs = refs[:chunks], refs[chunks:]
    sum_refs, refs = refs[: len(masks)], refs[len(masks) :]
    q_ref, h_ref, w_ref, g_ref = refs[:4]
    plan_refs = refs[4 : 4 + chunks]
    q_out, logb_ref, col_ref, row_ref = refs[4 + chunks :]
    width = s_refs[0].shape[1]

    @pl.when(pl.program_id(0) == 0)
    def _():
        advance(sum_refs, masks, count, q_ref, h_ref, q_out)
        row_ref[...] = jnp.zeros_like(row_ref)

    q, g = q_out[...], g_ref[...]
    parts = [
        jnp.exp(s_refs[k][...] + q[:, k * width : (k + 1) * width] + g) for k in range(chunks)
    ]
    total = sum(jnp.sum(p, axis=1, keepdims=True) for p in parts)
    logb_ref[...] = -jnp.log(total)
    w = w_ref[...] / total
    col = jnp.zeros_like(total)
    for k in range(chunks):
        plan = (parts[k] * w).astype(BF16)
        plan_refs[k][...] = plan
        wide = plan.astype(F32)
        col = col + jnp.sum(wide, axis=1, keepdims=True)
        row_ref[:, k * width : (k + 1) * width] += jnp.sum(wide, axis=0, keepdims=True)
    col_ref[...] = col


def row_part_kernel(plan_ref, y_ref, mass_ref, keep_ref, send_ref):
    rows = keep_ref.shape[1] - TAIL
    part = lax.dot_general(
        plan_ref[...], y_ref[...], (((0,), (0,)), ((), ())), preferred_element_type=F32
    )
    for block in range(4):
        ref = send_ref if block % 2 else keep_ref
        half = block // 2
        ref[half, :rows, :] = part[block * rows : (block + 1) * rows, :]
        ref[half, rows:, :] = jnp.zeros((TAIL, ref.shape[2]), F32)
        ref[half, rows : rows + 1, :rows] = mass_ref[:, block * rows : (block + 1) * rows]


def split_mass(mass):
    high = mass.astype(BF16).astype(F32)
    rest = mass - high
    middle = rest.astype(BF16).astype(F32)
    row = lax.broadcasted_iota(jnp.int32, (TAIL, mass.shape[1]), 0)
    out = jnp.where(row == 0, high, jnp.where(row == 1, middle, rest - middle))
    return jnp.where(row < 3, out, 0.0).astype(BF16)


def chip_kernel(keep_ref, other_ref, own_ref, send_ref):
    rows = own_ref.shape[0] - TAIL
    own_ref[...] = keep_ref[0] + other_ref[0]
    send_ref[:rows, :] = (keep_ref[1, :rows, :] + other_ref[1, :rows, :]).astype(BF16)
    send_ref[rows:, :] = split_mass(
        keep_ref[1, rows : rows + 1, :] + other_ref[1, rows : rows + 1, :]
    )


def gathered_sum(own_ref, other_refs):
    rows = own_ref.shape[0] - TAIL
    part = own_ref[:rows, :]
    mass = own_ref[rows : rows + 1, :]
    for ref in other_refs:
        part = part + ref[:rows, :].astype(F32)
        mass = mass + jnp.sum(ref[rows:, :].astype(F32), axis=0, keepdims=True)
    return part, mass


def line_kernel(own_ref, *refs):
    part, mass = gathered_sum(own_ref, refs[:-1])
    rows = part.shape[0]
    refs[-1][:rows, :] = part.astype(BF16)
    refs[-1][rows:, :] = split_mass(mass)


def last_kernel(own_ref, *refs):
    *others, x_ref, out_ref = refs
    part, mass = gathered_sum(own_ref, others)
    rows = part.shape[0]
    wide = jnp.broadcast_to(mass[:, :rows], (rows, rows))
    same = lax.broadcasted_iota(jnp.int32, (rows, rows), 0) == lax.broadcasted_iota(
        jnp.int32, (rows, rows), 1
    )
    column = jnp.sum(jnp.where(same, wide, 0.0), axis=1, keepdims=True)
    out_ref[...] = column * x_ref[...].astype(F32) - part


def column_kernel(chunks, factor, *refs):
    plan_refs, x_refs = refs[:chunks], refs[chunks : 2 * chunks]
    y_ref, mass_ref, out_ref = refs[2 * chunks :]
    part = sum(
        jnp.dot(plan_refs[k][...], x_refs[k][...], preferred_element_type=F32)
        for k in range(chunks)
    )
    out_ref[...] = factor * (mass_ref[...] * y_ref[...].astype(F32) - part)


def per_device(source_feats, target_feats, source_logits, target_logits):
    count = lax.axis_size(AXIS)
    me = lax.axis_index(AXIS)
    rows, width = source_feats.shape
    cols = target_feats.shape[0]
    source_count = rows * count
    target_count = cols * count
    scale = 1.0 / math.sqrt(width)
    direct = count == 16
    chunks = 4
    chunk = source_count // chunks
    order = jnp.bitwise_xor(me, jnp.arange(count))

    if direct:
        far = swap(source_feats, 8)
        line = [source_feats, swap(source_feats, 4), far, swap(far, 4)]
        by_chunk = []
        for block in line:
            other = swap(block, 2)
            by_chunk.append([block, swap(block, 1), other, swap(other, 1)])
    else:
        gathered = lax.all_gather(source_feats, AXIS, axis=0)[order]
        gathered = gathered.reshape(chunks, chunk, width)
        by_chunk = [[gathered[k]] for k in range(chunks)]

    weight = jnp.exp(target_logits)[:, None]
    target_sq = scale * jnp.sum(jnp.square(target_feats.astype(F32)), axis=1, keepdims=True)
    lift = target_logits[:, None] - target_sq
    logits = source_logits.reshape(count, rows)[order].reshape(1, source_count)
    weight, lift, logits = lax.optimization_barrier((weight, lift, logits))

    pack = jnp.zeros((1, 2 * source_count + 128), F32)
    scores, feats = [None] * chunks, [None] * chunks
    for k in (0, 1, 2, 3):
        scores[k], feats[k], pack = call(
            functools.partial(cost_kernel, 2.0 * scale, len(by_chunk[k]), k),
            "cost",
            [*by_chunk[k], target_feats, lift, weight, pack],
            [shape((cols, chunk)), shape((chunk, width), BF16), shape(pack.shape)],
            flops=2 * cols * chunk * width,
        )

    *levels, last = tree_levels(count)
    masks = (0, *last)
    for level in levels:
        packs = [pack] + [swap(pack, m) for m in level]
        (pack,) = call(
            functools.partial(merge_kernel, (0, *level), count),
            "merge",
            packs,
            [shape(pack.shape)],
        )
    packs = [pack] + [swap(pack, m) for m in last]

    tile = 128
    grid = (cols // tile,)
    thin = pl.BlockSpec((tile, 1), lambda j: (j, 0))
    flat = pl.BlockSpec((1, source_count), lambda j: (0, 0))
    part = pl.BlockSpec((tile, chunk), lambda j: (j, 0))
    packed = pl.BlockSpec(pack.shape, lambda j: (0, 0))
    thin_shape, flat_shape = shape((cols, 1)), shape((1, source_count))

    q, h, row, g, share = call(
        functools.partial(first_kernel, chunks, masks, count, source_count),
        "first",
        [*scores, *packs, logits, weight],
        [flat_shape, flat_shape, flat_shape, thin_shape, thin_shape],
        grid=grid,
        in_specs=[part] * chunks + [packed] * len(masks) + [flat, thin],
        out_specs=[flat, flat, flat, thin, thin],
    )

    def row_sums(row):
        for level in levels:
            row = row + sum(flip(swap(row, m), m, count) for m in level)
        return [row] + [swap(row, m) for m in last]

    for _ in range(ITERS - 2):
        q, row = call(
            functools.partial(step_kernel, chunks, masks, count),
            "step",
            [*scores, *row_sums(row), q, h, weight, g],
            [flat_shape, flat_shape],
            grid=grid,
            in_specs=[part] * chunks + [flat] * (len(masks) + 2) + [thin, thin],
            out_specs=[flat, flat],
        )

    *plans, q, logb, col_mass, row_mass = call(
        functools.partial(plan_kernel, chunks, masks, count),
        "plan",
        [*scores, *row_sums(row), q, h, share, g],
        [shape((cols, chunk), BF16)] * chunks + [flat_shape, thin_shape, thin_shape, flat_shape],
        grid=grid,
        in_specs=[part] * chunks + [flat] * (len(masks) + 2) + [thin, thin],
        out_specs=[part] * chunks + [flat, thin, thin, flat],
    )

    block = shape((rows + TAIL, width))
    block_out = shape((rows + TAIL, width), BF16)

    def line_sum(own, *others):
        return call(line_kernel, "line", [own, *others], [block_out])[0]

    gate = row_mass
    if direct:
        own, crossed = {}, {}
        for k in (3, 2, 1, 0):
            plan, _ = lax.optimization_barrier((plans[k], gate))
            pair = shape((2, rows + TAIL, width))
            keep, send = call(
                row_part_kernel,
                "row_part",
                [plan, target_feats, row_mass[:, k * chunk : (k + 1) * chunk]],
                [pair, pair],
                flops=2 * cols * chunk * width,
            )
            gate = send
            own[k], out = call(
                chip_kernel, "chip", [keep, swap(send, 1)], [block, block_out]
            )
            crossed[k] = swap(out, 2)
        near = swap(line_sum(own[3], crossed[3]), 4)
        far = swap(line_sum(own[2], crossed[2], near), 8)
        near = swap(line_sum(own[1], crossed[1]), 4)
        grad_source = call(
            last_kernel,
            "last",
            [own[0], crossed[0], near, far, source_feats],
            [shape((rows, width))],
        )[0]
        gate = out
    else:
        full = lax.dot_general(
            jnp.concatenate(plans, axis=1),
            target_feats,
            (((0,), (0,)), ((), ())),
            preferred_element_type=F32,
        ).reshape(count, rows, width)[order]
        mass = row_mass.reshape(count, rows)[order]
        grad_source = lax.psum_scatter(mass, AXIS, scatter_dimension=0)[:, None] * (
            source_feats.astype(F32)
        ) - lax.psum_scatter(full, AXIS, scatter_dimension=0)

    *plans, _ = lax.optimization_barrier((*plans, gate))
    (grad_target,) = call(
        functools.partial(column_kernel, chunks, target_count / source_count),
        "column",
        [*plans, *feats, target_feats, col_mass],
        [shape((cols, width))],
        flops=2 * cols * source_count * width,
    )

    source_sq = scale * jnp.concatenate(
        [jnp.sum(jnp.square(x.astype(F32)), axis=1) for x in feats]
    )
    log_total = jnp.log(jnp.sum(jnp.exp(source_logits)))
    potential_src = (q - logits + log_total).reshape(source_count) + source_sq
    potential_src = potential_src.reshape(count, rows)[order].reshape(source_count)
    potential_tgt = (g + logb + target_sq).reshape(cols)
    return (grad_source, grad_target, potential_src, potential_tgt)


def solution(mesh):
    return jax.shard_map(
        per_device,
        mesh=mesh,
        in_specs=(
            P(("groups", "tgt"), None),
            P(("groups", "tgt"), None),
            P("groups"),
            P(("groups", "tgt")),
        ),
        out_specs=(
            P(("groups", "tgt"), None),
            P(("groups", "tgt"), None),
            P("groups"),
            P(("groups", "tgt")),
        ),
        check_vma=False,
    )
```

```python
import functools
import math

import jax
import jax.numpy as jnp
from jax import lax
from jax.experimental import pallas as pl
from jax.experimental.pallas import tpu as pltpu
from jax.sharding import PartitionSpec as P

ITERS = 3
AXIS = "tgt"
F32 = jnp.float32
BF16 = jnp.bfloat16
TAIL = 8
LOW = -1e30
ANY = pl.BlockSpec(memory_space=pl.ANY)


def whole(a):
    return pl.BlockSpec(a.shape, lambda *_: (0,) * len(a.shape))


def call(body, name, ins, outs, grid=(1,), in_specs=None, out_specs=None, flops=0, **kw):
    size = sum(math.prod(a.shape) * jnp.dtype(a.dtype).itemsize for a in [*ins, *outs])
    return pl.pallas_call(
        body,
        name=name,
        grid=grid,
        out_shape=outs,
        in_specs=in_specs or [whole(a) for a in ins],
        out_specs=out_specs or [whole(a) for a in outs],
        compiler_params=pltpu.CompilerParams(vmem_limit_bytes=60 << 20),
        cost_estimate=pl.CostEstimate(flops=flops, bytes_accessed=size, transcendentals=0),
        **kw,
    )(*ins)


def shape(dims, dtype=F32):
    return jax.ShapeDtypeStruct(dims, dtype)


def swap(value, mask):
    count = lax.axis_size(AXIS)
    return lax.ppermute(value, AXIS, [(i, i ^ mask) for i in range(count)])


def row_levels(count):
    levels, step = [(1,)], 4
    while step < count:
        if step * 4 <= count:
            levels.append((step, 2 * step, 3 * step))
            step *= 4
        else:
            levels.append((step,))
            step *= 2
    return levels


def flip(value, mask, blocks):
    move = (mask & 1) * (blocks // 2) + (mask >> 2)
    if not move:
        return value
    width = value.shape[-1] // blocks
    parts = [value[..., (r ^ move) * width : ((r ^ move) + 1) * width] for r in range(blocks)]
    return jnp.concatenate(parts, axis=-1)


def diagonal():
    return lax.broadcasted_iota(jnp.int32, (128, 128), 0) == lax.broadcasted_iota(
        jnp.int32, (128, 128), 1
    )


def to_column(row):
    same = diagonal()
    parts = [
        jnp.sum(
            jnp.where(same, jnp.broadcast_to(row[:, i : i + 128], (128, 128)), 0.0),
            axis=1,
            keepdims=True,
        )
        for i in range(0, row.shape[1], 128)
    ]
    return jnp.concatenate(parts, axis=0)


def to_row(column):
    same = diagonal()
    parts = [
        jnp.sum(
            jnp.where(same, jnp.broadcast_to(column[i : i + 128, :], (128, 128)), 0.0),
            axis=0,
            keepdims=True,
        )
        for i in range(0, column.shape[0], 128)
    ]
    return jnp.concatenate(parts, axis=1)


def cost_kernel(scale, copy, add_mass, offsets, *refs):
    x_refs, y_ref, logit_ref, pack_ref = refs[:2], refs[2], refs[3], refs[4]
    outs = refs[-5:] if copy else refs[-3:]
    s_outs, pack_out = outs[:2], outs[-1]
    y = y_ref[...]
    wide = y.astype(F32)
    logit = logit_ref[...]
    lift = to_column(logit) - scale * jnp.sum(wide * wide, axis=1, keepdims=True)
    pack_out[...] = pack_ref[...]
    if add_mass:
        pack_out[2:3, :] = pack_ref[2:3, :] + jnp.sum(jnp.exp(logit), axis=1, keepdims=True)
    for c in range(2):
        x = x_refs[c][...]
        if copy:
            outs[2 + c][...] = x
        s = (2.0 * scale) * lax.dot_general(
            y, x, (((1,), (1,)), ((), ())), preferred_element_type=F32
        )
        s_outs[c][...] = s
        s = s + lift
        lanes = slice(offsets[c], offsets[c] + s.shape[1])
        old = pack_ref[0:1, lanes]
        top = jnp.maximum(old, jnp.max(s, axis=0, keepdims=True))
        pack_out[0:1, lanes] = top
        pack_out[1:2, lanes] = pack_ref[1:2, lanes] * jnp.exp(old - top) + jnp.sum(
            jnp.exp(s - top), axis=0, keepdims=True
        )


def merge(packs, masks, blocks):
    packs = [flip(p, m, blocks) for p, m in zip(packs, masks)]
    top = functools.reduce(jnp.maximum, [p[0:1] for p in packs])
    total = sum(p[1:2] * jnp.exp(p[0:1] - top) for p in packs)
    return top, total, sum(p[2:3] for p in packs)


def merge_kernel(masks, blocks, *refs):
    top, total, mass = merge([r[...] for r in refs[:-1]], masks, blocks)
    refs[-1][0:1, :] = top
    refs[-1][1:2, :] = total
    refs[-1][2:3, :] = mass


def first_kernel(masks, blocks, *refs):
    pack_refs, refs = refs[: len(masks)], refs[len(masks) :]
    s_refs, refs = refs[:2], refs[2:]
    logit_ref, total_ref, e_ref, col_ref, q_ref, h_ref = refs

    @pl.when(pl.program_id(0) == 0)
    def _():
        top, total, mass = merge([r[...] for r in pack_refs], masks, blocks)
        h = logit_ref[...] - total_ref[...] + jnp.log(mass)
        h_ref[0:1, :] = h
        h_ref[1:2, :] = mass
        q_ref[...] = h - top - jnp.log(total)

    half = s_refs[0].shape[1]
    parts = [s_refs[c][...] + q_ref[:, c * half : (c + 1) * half] for c in range(2)]
    top = jnp.maximum(*[jnp.max(p, axis=1, keepdims=True) for p in parts])
    total = jnp.zeros_like(top)
    for c in range(2):
        e = jnp.exp(parts[c] - top)
        e_ref[:, c * half : (c + 1) * half] = e
        total = total + jnp.sum(e, axis=1, keepdims=True)
    col_ref[0:1, :] = to_row(top)
    col_ref[1:2, :] = to_row(total)


def weighted_rows(e_ref, weight, row_ref):
    @pl.when(pl.program_id(0) == 0)
    def _():
        row_ref[...] = jnp.zeros_like(row_ref)

    row_ref[...] += jnp.sum(e_ref[...] * to_column(weight), axis=0, keepdims=True)


def first_row_kernel(e_ref, own_ref, other_ref, logit_ref, row_ref, phi_ref, g_ref):
    tops = own_ref[0:1, :], other_ref[0:1, :]
    top = jnp.maximum(*tops)
    total = own_ref[1:2, :] * jnp.exp(tops[0] - top) + other_ref[1:2, :] * jnp.exp(tops[1] - top)
    g_ref[...] = -(top + jnp.log(total))
    phi = jnp.exp(tops[0] - top) / total
    phi_ref[...] = phi
    weighted_rows(e_ref, jnp.exp(logit_ref[...]) * phi, row_ref)


def row_kernel(e_ref, own_ref, other_ref, logit_ref, phi_ref, row_ref):
    weight = jnp.exp(logit_ref[...]) * phi_ref[...] / (own_ref[...] + other_ref[...])
    weighted_rows(e_ref, weight, row_ref)


def column_kernel(masks, blocks, *refs):
    sum_refs, refs = refs[: len(masks)], refs[len(masks) :]
    e_ref, h_ref, phi_ref, col_ref, a_ref = refs

    @pl.when(pl.program_id(0) == 0)
    def _():
        total = sum(flip(r[...], m, blocks) for r, m in zip(sum_refs, masks))
        a_ref[...] = jnp.exp(h_ref[0:1, :]) / total

    total = jnp.sum(e_ref[...] * a_ref[...], axis=1, keepdims=True)
    col_ref[...] = to_row(total) * phi_ref[...]


def plan_kernel(source_count, *refs):
    e_ref, a_ref, h_ref, own_ref, other_ref, logit_ref, phi_ref = refs[:7]
    keep_ref, send_ref, mass_ref, logb_ref = refs[7:]
    c = own_ref[...] + other_ref[...]
    logb_ref[...] = -jnp.log(c)
    mass = h_ref[1:2, : c.shape[1]]
    share = to_column(jnp.exp(logit_ref[...]) * phi_ref[...] * (source_count / mass) / c)
    plan = ((e_ref[...] * a_ref[...]) * share).astype(BF16)
    half = keep_ref.shape[1]
    keep_ref[...] = plan[:, :half]
    send_ref[...] = plan[:, half:]
    mass_ref[...] = to_row(jnp.sum(plan.astype(F32), axis=1, keepdims=True))


def split_mass(mass, width):
    mass = jnp.concatenate([mass, jnp.zeros((1, width - mass.shape[1]), F32)], axis=1)
    high = mass.astype(BF16).astype(F32)
    rest = mass - high
    middle = rest.astype(BF16).astype(F32)
    row = lax.broadcasted_iota(jnp.int32, (TAIL, width), 0)
    out = jnp.where(row == 0, high, jnp.where(row == 1, middle, rest - middle))
    return jnp.where(row < 3, out, 0.0).astype(BF16)


def joined_mass(ref, width):
    return jnp.sum(ref[ref.shape[0] - TAIL :, :width].astype(F32), axis=0, keepdims=True)


def row_part_kernel(keep_ref, other_ref, *refs):
    y_refs, (own_ref, out_ref) = refs[:-2], refs[-2:]
    group = len(y_refs) // 2
    part = mass = 0.0
    for plan_ref, ys in ((keep_ref, y_refs[:group]), (other_ref, y_refs[group:])):
        start = 0
        for y in ys:
            block = plan_ref[start : start + y.shape[0], :]
            start += y.shape[0]
            part = part + lax.dot_general(
                block, y[...], (((0,), (0,)), ((), ())), preferred_element_type=F32
            )
            mass = mass + jnp.sum(block.astype(F32), axis=0, keepdims=True)
    rows = own_ref.shape[0] - TAIL
    width = own_ref.shape[1]
    own_ref[:rows, :] = part[:rows, :]
    own_ref[rows:, :] = jnp.concatenate(
        [jnp.broadcast_to(mass[:, :rows], (TAIL, rows)), jnp.zeros((TAIL, width - rows), F32)],
        axis=1,
    )
    out_ref[:rows, :] = part[rows:, :].astype(BF16)
    out_ref[rows:, :] = split_mass(mass[:, rows:], width)


def line_kernel(own_ref, other_ref, out_ref):
    rows, width = out_ref.shape[0] - TAIL, out_ref.shape[1]
    out_ref[:rows, :] = (own_ref[:rows, :] + other_ref[:rows, :].astype(F32)).astype(BF16)
    mass = own_ref[rows : rows + 1, :rows] + joined_mass(other_ref, rows)
    out_ref[rows:, :] = split_mass(mass, width)


def source_kernel(own_ref, near_ref, far_ref, x_ref, out_ref):
    rows = out_ref.shape[0]
    part = own_ref[:rows, :] + near_ref[:rows, :].astype(F32) + far_ref[:rows, :].astype(F32)
    mass = own_ref[rows : rows + 1, :rows] + joined_mass(near_ref, rows)
    mass = mass + joined_mass(far_ref, rows)
    out_ref[...] = to_column(mass) * x_ref[...].astype(F32) - part


def col_part(keep_ref, send_ref, x_refs):
    return jnp.dot(keep_ref[...], x_refs[0][...], preferred_element_type=F32) + jnp.dot(
        send_ref[...], x_refs[1][...], preferred_element_type=F32
    )


def col_send_kernel(keep_ref, send_ref, x0_ref, x1_ref, mass_ref, *out_refs):
    part = col_part(keep_ref, send_ref, (x0_ref, x1_ref))
    width = part.shape[1]
    cols = part.shape[0] // len(out_refs)
    for p, ref in enumerate(out_refs):
        ref[:cols, :] = part[p * cols : (p + 1) * cols, :].astype(BF16)
        ref[cols:, :] = split_mass(mass_ref[:, p * cols : (p + 1) * cols], width)


def col_keep_kernel(keep_ref, send_ref, x0_ref, x1_ref, out_ref):
    out_ref[...] = col_part(keep_ref, send_ref, (x0_ref, x1_ref))


def target_kernel(factor, own_ref, other_ref, mass_ref, y_ref, *refs):
    cols = own_ref.shape[0]
    part = own_ref[...] + other_ref[:cols, :].astype(F32)
    mass = to_column(mass_ref[...] + joined_mass(other_ref, cols))
    refs[-1][...] = factor * (mass * y_ref[...].astype(F32) - part)


def per_device(source_feats, target_feats, source_logits, target_logits):
    count = lax.axis_size(AXIS)
    me = lax.axis_index(AXIS)
    rows, width = source_feats.shape
    cols = target_feats.shape[0]
    source_count = rows * count
    target_count = cols * count
    scale = 1.0 / math.sqrt(width)
    direct = count == 16
    blocks = count // 2
    lines = blocks // 2
    mine = source_count // 2
    half = mine // 2
    part = cols // 2
    masks = [4 * k + c for c in range(2) for k in range(lines)]
    order = jnp.bitwise_xor(me, jnp.array(masks))

    y_pieces = [target_feats[:part], target_feats[part:]]
    if direct:
        far = swap(source_feats, 8)
        line = [source_feats, swap(source_feats, 4), far]
    crossed = [swap(y, 2) for y in y_pieces]
    logits_here = target_logits.reshape(1, cols)
    logits_there = swap(logits_here, 2)
    logits = jnp.concatenate([logits_here, logits_there], axis=1)
    source_rel = source_logits.reshape(count, rows)[order].reshape(1, mine)
    source_total = jnp.log(jnp.sum(jnp.exp(source_logits))).reshape(1, 1)
    logits_here, source_rel, source_total = lax.optimization_barrier(
        (logits_here, source_rel, source_total)
    )
    pack = jnp.concatenate([jnp.full((1, mine), LOW, F32), jnp.zeros((2, mine), F32)])

    s_shape, x_shape = shape((2 * cols, half)), shape((half, width), BF16)
    store = None
    if direct:
        gate = None
        for k in range(lines):
            x = source_feats if k == 0 else line[k]
            if k:
                x, _ = lax.optimization_barrier((x, gate))
            pair = [x, swap(x, 1)]
            ins = [*pair, target_feats, logits_here, pack]
            column = pl.BlockSpec((cols, rows), lambda _, k=k: (0, k))
            block = pl.BlockSpec((rows, width), lambda _, k=k: (k, 0))
            *store, pack = call(
                functools.partial(
                    cost_kernel, scale, True, k == 0, (k * rows, half + k * rows)
                ),
                "cost",
                ins + (store or []),
                [s_shape, s_shape, x_shape, x_shape, shape(pack.shape)],
                in_specs=[whole(a) for a in ins] + [ANY] * len(store or []),
                out_specs=[column, column, block, block, whole(pack)],
                flops=4 * cols * rows * width,
                input_output_aliases={5 + i: i for i in range(4)} if store else {},
            )
            gate = pack
            if k == 0:
                far_gated, _ = lax.optimization_barrier((far, gate))
                line.append(swap(far_gated, 4))
        s0, s1, x0, x1 = store
    else:
        gathered = lax.all_gather(source_feats, AXIS, axis=0)[order].reshape(2, half, width)
        x0, x1 = gathered[0], gathered[1]

    def cost_piece(y, logit, index, height, store, pack):
        ins = [x0, x1, y, logit, pack]
        block = pl.BlockSpec((height, half), lambda _: (index, 0))
        return call(
            functools.partial(cost_kernel, scale, False, True, (0, half)),
            "cost",
            ins + store,
            [s_shape, s_shape, shape(pack.shape)],
            in_specs=[whole(a) for a in ins] + [ANY] * len(store),
            out_specs=[block, block, whole(pack)],
            flops=2 * height * mine * width,
            input_output_aliases={5 + i: i for i in range(len(store))},
        )

    if not direct:
        s0, s1, pack = cost_piece(target_feats, logits_here, 0, cols, [], pack)
    for p in range(2):
        s0, s1, pack = cost_piece(
            crossed[p], logits_there[:, p * part : (p + 1) * part], 2 + p, part, [s0, s1], pack
        )

    *levels, last = row_levels(count)
    last_masks = (0, *last)
    for level in levels:
        packs = [pack] + [swap(pack, m) for m in level]
        (pack,) = call(
            functools.partial(merge_kernel, (0, *level), blocks),
            "merge",
            packs,
            [shape(pack.shape)],
        )
    packs = [pack] + [swap(pack, m) for m in last]

    tile = part
    tiles = 2 * cols // tile
    grid = (tiles,)
    turn = tiles // 2
    tall = pl.BlockSpec((tile, mine), lambda j: (j, 0))
    tall_half = pl.BlockSpec((tile, half), lambda j: (j, 0))
    flat = pl.BlockSpec((1, mine), lambda j: (0, 0))
    flat2 = pl.BlockSpec((2, mine), lambda j: (0, 0))
    lane = pl.BlockSpec((1, tile), lambda j: (0, j))
    lane2 = pl.BlockSpec((2, tile), lambda j: (0, j))
    lane_other = pl.BlockSpec((1, tile), lambda j: (0, (j + turn) % tiles))
    lane2_other = pl.BlockSpec((2, tile), lambda j: (0, (j + turn) % tiles))
    flat_shape, lane_shape = shape((1, mine)), shape((1, 2 * cols))
    e_shape = shape((2 * cols, mine))

    e, col, q, h = call(
        functools.partial(first_kernel, last_masks, blocks),
        "first",
        [*packs, s0, s1, source_rel, source_total],
        [e_shape, shape((2, 2 * cols)), flat_shape, shape((2, mine))],
        grid=grid,
        in_specs=[pl.BlockSpec(pack.shape, lambda j: (0, 0))] * len(packs)
        + [tall_half, tall_half, flat, pl.BlockSpec((1, 1), lambda j: (0, 0))],
        out_specs=[tall, lane2, flat, flat2],
    )
    row, phi, g = call(
        first_row_kernel,
        "first_row",
        [e, col, swap(col, 2), logits],
        [flat_shape, lane_shape, lane_shape],
        grid=grid,
        in_specs=[tall, lane2, lane2_other, lane],
        out_specs=[flat, lane, lane],
    )

    def columns(row):
        for level in levels:
            row = row + sum(flip(swap(row, m), m, blocks) for m in level)
        sums = [row] + [swap(row, m) for m in last]
        return call(
            functools.partial(column_kernel, last_masks, blocks),
            "column",
            [*sums, e, h, phi],
            [lane_shape, flat_shape],
            grid=grid,
            in_specs=[flat] * len(sums) + [tall, flat2, lane],
            out_specs=[lane, flat],
        )

    for _ in range(ITERS - 2):
        col, a = columns(row)
        (row,) = call(
            row_kernel,
            "row",
            [e, col, swap(col, 2), logits, phi],
            [flat_shape],
            grid=grid,
            in_specs=[tall, lane, lane_other, lane, lane],
            out_specs=[flat],
        )
    col, a = columns(row)
    keep, send, mass, logb = call(
        functools.partial(plan_kernel, source_count),
        "plan",
        [e, a, h, col, swap(col, 2), logits, phi],
        [shape((2 * cols, half), BF16)] * 2 + [lane_shape, lane_shape],
        grid=grid,
        in_specs=[tall, flat, flat2, lane, lane_other, lane, lane],
        out_specs=[tall_half, tall_half, lane, lane],
    )

    upper = pl.BlockSpec((cols, half), lambda _: (0, 0))
    lower = pl.BlockSpec((cols, half), lambda _: (1, 0))
    feats = pl.BlockSpec((half, width), lambda _: (0, 0))
    outs = call(
        col_send_kernel,
        "col_send",
        [keep, send, x0, x1, mass],
        [shape((part + TAIL, width), BF16)] * 2,
        in_specs=[lower, lower, feats, feats, pl.BlockSpec((1, cols), lambda _: (0, 1))],
        flops=2 * cols * mine * width,
    )
    back = [swap(o, 2) for o in outs]
    gate = outs[1]
    if direct:
        other_plan = swap(send, 1)
        ys = [target_feats, *crossed]
        ys = ys + [swap(y, 1) for y in ys]
        block, block_out = shape((rows + TAIL, width)), shape((rows + TAIL, width), BF16)

        def row_parts(pair, gate):
            plan, other, _ = lax.optimization_barrier((keep, other_plan, gate))
            lanes = pl.BlockSpec((2 * cols, 2 * rows), lambda _: (0, pair))
            return call(
                row_part_kernel,
                "row_part",
                [plan, other, *ys],
                [block, block_out],
                in_specs=[lanes, lanes] + [whole(y) for y in ys],
                flops=8 * cols * 2 * rows * width,
            )

        own2, out3 = row_parts(1, gate)
        own0, out1 = row_parts(0, out3)
        near3 = swap(out3, 4)
        near1 = swap(out1, 4)
        (out2,) = call(line_kernel, "line", [own2, near3], [block_out])
        far2 = swap(out2, 8)
        (grad_source,) = call(
            source_kernel,
            "source",
            [own0, near1, far2, source_feats],
            [shape((rows, width))],
        )
        gate = out1
    else:
        plan = jnp.concatenate([keep, send], axis=1)
        both = jnp.concatenate([target_feats, *crossed], axis=0)
        full = lax.dot_general(
            plan, both, (((0,), (0,)), ((), ())), preferred_element_type=F32
        ).reshape(blocks, rows, width)
        row_mass = jnp.sum(plan.astype(F32), axis=0).reshape(blocks, rows)
        full = jnp.zeros((count, rows, width), F32).at[order].set(full)
        row_mass = jnp.zeros((count, rows), F32).at[order].set(row_mass)
        grad_source = lax.psum_scatter(row_mass, AXIS, scatter_dimension=0)[:, None] * (
            source_feats.astype(F32)
        ) - lax.psum_scatter(full, AXIS, scatter_dimension=0)

    keep_later, _ = lax.optimization_barrier((keep, gate))
    (own_col,) = call(
        col_keep_kernel,
        "col_keep",
        [keep_later, send, x0, x1],
        [shape((cols, width))],
        in_specs=[upper, upper, feats, feats],
        flops=2 * cols * mine * width,
    )
    grad_target = None
    for p in range(2):
        piece = pl.BlockSpec((part, width), lambda _, p=p: (p, 0))
        done = [] if grad_target is None else [grad_target]
        (grad_target,) = call(
            functools.partial(target_kernel, target_count / source_count),
            "target",
            [own_col, back[p], mass, target_feats, *done],
            [shape((cols, width))],
            in_specs=[
                piece,
                whole(back[p]),
                pl.BlockSpec((1, part), lambda _, p=p: (0, p)),
                piece,
            ]
            + [ANY] * len(done),
            out_specs=[piece],
            input_output_aliases={4: 0} if done else {},
        )

    source_sq = scale * jnp.concatenate(
        [jnp.sum(jnp.square(x.astype(F32)), axis=1) for x in (x0, x1)]
    )
    potential = (q + jnp.log(a) - source_rel + source_total).reshape(mine) + source_sq
    potential = potential.reshape(1, mine)
    pair = [v.reshape(2, lines, rows) for v in (potential, swap(potential, 2))]
    potential_src = jnp.stack(pair).transpose(2, 0, 1, 3).reshape(count, rows)
    everyone = jnp.bitwise_xor(me, jnp.arange(count))
    potential_src = potential_src[everyone].reshape(source_count)
    target_sq = scale * jnp.sum(jnp.square(target_feats.astype(F32)), axis=1)
    potential_tgt = (g + logb)[0, :cols] + target_sq
    return (grad_source, grad_target, potential_src, potential_tgt)


def solution(mesh):
    return jax.shard_map(
        per_device,
        mesh=mesh,
        in_specs=(
            P(("groups", "tgt"), None),
            P(("groups", "tgt"), None),
            P("groups"),
            P(("groups", "tgt")),
        ),
        out_specs=(
            P(("groups", "tgt"), None),
            P(("groups", "tgt"), None),
            P("groups"),
            P(("groups", "tgt")),
        ),
        check_vma=False,
    )
```

```python
import functools
import math

import jax
import jax.numpy as jnp
from jax import lax
from jax.experimental import pallas as pl
from jax.experimental.pallas import tpu as pltpu
from jax.sharding import PartitionSpec as P

ITERS = 3
AXIS = "tgt"
F32 = jnp.float32
BF16 = jnp.bfloat16
TAIL = 8
LOW = -1e30
ANY = pl.BlockSpec(memory_space=pl.ANY)


def whole(a):
    return pl.BlockSpec(a.shape, lambda *_: (0,) * len(a.shape))


def call(body, name, ins, outs, grid=(1,), in_specs=None, out_specs=None, size=1, **kw):
    return pl.pallas_call(
        body,
        name=name,
        grid=grid,
        out_shape=outs,
        in_specs=in_specs or [whole(a) for a in ins],
        out_specs=out_specs or [whole(a) for a in outs],
        compiler_params=pltpu.CompilerParams(vmem_limit_bytes=16 << 20),
        cost_estimate=pl.CostEstimate(flops=1, bytes_accessed=size, transcendentals=0),
        **kw,
    )(*ins)


def shape(dims, dtype=F32):
    return jax.ShapeDtypeStruct(dims, dtype)


def swap(value, mask):
    count = lax.axis_size(AXIS)
    return lax.ppermute(value, AXIS, [(i, i ^ mask) for i in range(count)])


def row_levels(count):
    levels, step = [(1,)], 4
    while step < count:
        if step * 4 <= count:
            levels.append((step, 2 * step, 3 * step))
            step *= 4
        else:
            levels.append((step,))
            step *= 2
    return levels


def flip(value, mask, blocks):
    move = (mask & 1) * (blocks // 2) + (mask >> 2)
    if not move:
        return value
    width = value.shape[-1] // blocks
    parts = [value[..., (r ^ move) * width : ((r ^ move) + 1) * width] for r in range(blocks)]
    return jnp.concatenate(parts, axis=-1)


def diagonal():
    return lax.broadcasted_iota(jnp.int32, (128, 128), 0) == lax.broadcasted_iota(
        jnp.int32, (128, 128), 1
    )


def to_column(row):
    same = diagonal()
    parts = [
        jnp.sum(
            jnp.where(same, jnp.broadcast_to(row[:, i : i + 128], (128, 128)), 0.0),
            axis=1,
            keepdims=True,
        )
        for i in range(0, row.shape[1], 128)
    ]
    return jnp.concatenate(parts, axis=0)


def to_row(column):
    same = diagonal()
    parts = [
        jnp.sum(
            jnp.where(same, jnp.broadcast_to(column[i : i + 128, :], (128, 128)), 0.0),
            axis=0,
            keepdims=True,
        )
        for i in range(0, column.shape[0], 128)
    ]
    return jnp.concatenate(parts, axis=1)


def cost_kernel(scale, copy, add_mass, offsets, *refs):
    x_refs, y_ref, logit_ref, pack_ref = refs[:2], refs[2], refs[3], refs[4]
    outs = refs[-5:] if copy else refs[-3:]
    s_outs, pack_out = outs[:2], outs[-1]
    y = y_ref[...]
    wide = y.astype(F32)
    logit = logit_ref[...]
    lift = to_column(logit) - scale * jnp.sum(wide * wide, axis=1, keepdims=True)
    pack_out[...] = pack_ref[...]
    if add_mass:
        pack_out[2:3, :] = pack_ref[2:3, :] + jnp.sum(jnp.exp(logit), axis=1, keepdims=True)
    for c in range(2):
        x = x_refs[c][...]
        if copy:
            outs[2 + c][...] = x
        s = (2.0 * scale) * lax.dot_general(
            y, x, (((1,), (1,)), ((), ())), preferred_element_type=F32
        )
        s_outs[c][...] = s
        s = s + lift
        lanes = slice(offsets[c], offsets[c] + s.shape[1])
        old = pack_ref[0:1, lanes]
        top = jnp.maximum(old, jnp.max(s, axis=0, keepdims=True))
        pack_out[0:1, lanes] = top
        pack_out[1:2, lanes] = pack_ref[1:2, lanes] * jnp.exp(old - top) + jnp.sum(
            jnp.exp(s - top), axis=0, keepdims=True
        )


def merge(packs, masks, blocks):
    packs = [flip(p, m, blocks) for p, m in zip(packs, masks)]
    top = functools.reduce(jnp.maximum, [p[0:1] for p in packs])
    total = sum(p[1:2] * jnp.exp(p[0:1] - top) for p in packs)
    return top, total, sum(p[2:3] for p in packs)


def merge_kernel(masks, blocks, *refs):
    top, total, mass = merge([r[...] for r in refs[:-1]], masks, blocks)
    refs[-1][0:1, :] = top
    refs[-1][1:2, :] = total
    refs[-1][2:3, :] = mass


def first_kernel(masks, blocks, *refs):
    pack_refs, refs = refs[: len(masks)], refs[len(masks) :]
    s_refs, refs = refs[:2], refs[2:]
    logit_ref, total_ref, e_ref, col_ref, q_ref, h_ref = refs

    @pl.when(pl.program_id(0) == 0)
    def _():
        top, total, mass = merge([r[...] for r in pack_refs], masks, blocks)
        h = logit_ref[...] - total_ref[...] + jnp.log(mass)
        h_ref[0:1, :] = h
        h_ref[1:2, :] = mass
        q_ref[...] = h - top - jnp.log(total)

    half = s_refs[0].shape[1]
    parts = [s_refs[c][...] + q_ref[:, c * half : (c + 1) * half] for c in range(2)]
    top = jnp.maximum(*[jnp.max(p, axis=1, keepdims=True) for p in parts])
    total = jnp.zeros_like(top)
    for c in range(2):
        e = jnp.exp(parts[c] - top)
        e_ref[:, c * half : (c + 1) * half] = e
        total = total + jnp.sum(e, axis=1, keepdims=True)
    col_ref[0:1, :] = to_row(top)
    col_ref[1:2, :] = to_row(total)


def weighted_rows(e_ref, weight, row_ref):
    @pl.when(pl.program_id(0) == 0)
    def _():
        row_ref[...] = jnp.zeros_like(row_ref)

    row_ref[...] += jnp.sum(e_ref[...] * to_column(weight), axis=0, keepdims=True)


def first_row_kernel(e_ref, own_ref, other_ref, logit_ref, row_ref, phi_ref, g_ref):
    tops = own_ref[0:1, :], other_ref[0:1, :]
    top = jnp.maximum(*tops)
    total = own_ref[1:2, :] * jnp.exp(tops[0] - top) + other_ref[1:2, :] * jnp.exp(tops[1] - top)
    g_ref[...] = -(top + jnp.log(total))
    phi = jnp.exp(tops[0] - top) / total
    phi_ref[...] = phi
    weighted_rows(e_ref, jnp.exp(logit_ref[...]) * phi, row_ref)


def row_kernel(e_ref, own_ref, other_ref, logit_ref, phi_ref, row_ref):
    weight = jnp.exp(logit_ref[...]) * phi_ref[...] / (own_ref[...] + other_ref[...])
    weighted_rows(e_ref, weight, row_ref)


def column_kernel(masks, blocks, *refs):
    sum_refs, refs = refs[: len(masks)], refs[len(masks) :]
    e_ref, h_ref, phi_ref, col_ref, a_ref = refs

    @pl.when(pl.program_id(0) == 0)
    def _():
        total = sum(flip(r[...], m, blocks) for r, m in zip(sum_refs, masks))
        a_ref[...] = jnp.exp(h_ref[0:1, :]) / total

    total = jnp.sum(e_ref[...] * a_ref[...], axis=1, keepdims=True)
    col_ref[...] = to_row(total) * phi_ref[...]


def plan_kernel(source_count, *refs):
    e_ref, a_ref, h_ref, own_ref, other_ref, logit_ref, phi_ref = refs[:7]
    keep_ref, send_ref, mass_ref, logb_ref = refs[7:]
    c = own_ref[...] + other_ref[...]
    logb_ref[...] = -jnp.log(c)
    mass = h_ref[1:2, : c.shape[1]]
    share = to_column(jnp.exp(logit_ref[...]) * phi_ref[...] * (source_count / mass) / c)
    plan = ((e_ref[...] * a_ref[...]) * share).astype(BF16)
    half = keep_ref.shape[1]
    keep_ref[...] = plan[:, :half]
    send_ref[...] = plan[:, half:]
    mass_ref[...] = to_row(jnp.sum(plan.astype(F32), axis=1, keepdims=True))


def split_mass(mass, width):
    mass = jnp.concatenate([mass, jnp.zeros((1, width - mass.shape[1]), F32)], axis=1)
    high = mass.astype(BF16).astype(F32)
    rest = mass - high
    middle = rest.astype(BF16).astype(F32)
    row = lax.broadcasted_iota(jnp.int32, (TAIL, width), 0)
    out = jnp.where(row == 0, high, jnp.where(row == 1, middle, rest - middle))
    return jnp.where(row < 3, out, 0.0).astype(BF16)


def joined_mass(ref, width):
    return jnp.sum(ref[ref.shape[0] - TAIL :, :width].astype(F32), axis=0, keepdims=True)


def row_part_kernel(keep_ref, other_ref, *refs):
    y_refs, (own_ref, out_ref) = refs[:-2], refs[-2:]
    group = len(y_refs) // 2
    part = mass = 0.0
    for plan_ref, ys in ((keep_ref, y_refs[:group]), (other_ref, y_refs[group:])):
        start = 0
        for y in ys:
            block = plan_ref[start : start + y.shape[0], :]
            start += y.shape[0]
            part = part + lax.dot_general(
                block, y[...], (((0,), (0,)), ((), ())), preferred_element_type=F32
            )
            mass = mass + jnp.sum(block.astype(F32), axis=0, keepdims=True)
    rows = own_ref.shape[0] - TAIL
    width = own_ref.shape[1]
    own_ref[:rows, :] = part[:rows, :]
    own_ref[rows:, :] = jnp.concatenate(
        [jnp.broadcast_to(mass[:, :rows], (TAIL, rows)), jnp.zeros((TAIL, width - rows), F32)],
        axis=1,
    )
    out_ref[:rows, :] = part[rows:, :].astype(BF16)
    out_ref[rows:, :] = split_mass(mass[:, rows:], width)


def line_kernel(own_ref, other_ref, out_ref):
    rows, width = out_ref.shape[0] - TAIL, out_ref.shape[1]
    out_ref[:rows, :] = (own_ref[:rows, :] + other_ref[:rows, :].astype(F32)).astype(BF16)
    mass = own_ref[rows : rows + 1, :rows] + joined_mass(other_ref, rows)
    out_ref[rows:, :] = split_mass(mass, width)


def source_kernel(own_ref, near_ref, far_ref, x_ref, out_ref):
    rows = out_ref.shape[0]
    part = own_ref[:rows, :] + near_ref[:rows, :].astype(F32) + far_ref[:rows, :].astype(F32)
    mass = own_ref[rows : rows + 1, :rows] + joined_mass(near_ref, rows)
    mass = mass + joined_mass(far_ref, rows)
    out_ref[...] = to_column(mass) * x_ref[...].astype(F32) - part


def col_part(keep_ref, send_ref, x_refs):
    return jnp.dot(keep_ref[...], x_refs[0][...], preferred_element_type=F32) + jnp.dot(
        send_ref[...], x_refs[1][...], preferred_element_type=F32
    )


def col_send_kernel(keep_ref, send_ref, x0_ref, x1_ref, mass_ref, *out_refs):
    part = col_part(keep_ref, send_ref, (x0_ref, x1_ref))
    width = part.shape[1]
    cols = part.shape[0] // len(out_refs)
    for p, ref in enumerate(out_refs):
        ref[:cols, :] = part[p * cols : (p + 1) * cols, :].astype(BF16)
        ref[cols:, :] = split_mass(mass_ref[:, p * cols : (p + 1) * cols], width)


def col_keep_kernel(keep_ref, send_ref, x0_ref, x1_ref, out_ref):
    out_ref[...] = col_part(keep_ref, send_ref, (x0_ref, x1_ref))


def target_kernel(factor, own_ref, other_ref, mass_ref, y_ref, *refs):
    cols = own_ref.shape[0]
    part = own_ref[...] + other_ref[:cols, :].astype(F32)
    mass = to_column(mass_ref[...] + joined_mass(other_ref, cols))
    refs[-1][...] = factor * (mass * y_ref[...].astype(F32) - part)


def per_device(source_feats, target_feats, source_logits, target_logits):
    count = lax.axis_size(AXIS)
    me = lax.axis_index(AXIS)
    rows, width = source_feats.shape
    cols = target_feats.shape[0]
    source_count = rows * count
    target_count = cols * count
    scale = 1.0 / math.sqrt(width)
    direct = count == 16
    blocks = count // 2
    lines = blocks // 2
    mine = source_count // 2
    half = mine // 2
    part = cols // 2
    masks = [4 * k + c for c in range(2) for k in range(lines)]
    order = jnp.bitwise_xor(me, jnp.array(masks))

    if direct:
        far = swap(source_feats, 8)
        line = [source_feats, swap(source_feats, 4), far]
    crossed = [swap(target_feats, 2)]
    if direct:
        ys = [target_feats, swap(target_feats, 1)]
    logits_here = target_logits.reshape(1, cols)
    logits_there = swap(logits_here, 2)
    logits = jnp.concatenate([logits_here, logits_there], axis=1)
    source_rel = source_logits.reshape(count, rows)[order].reshape(1, mine)
    source_total = jnp.log(jnp.sum(jnp.exp(source_logits))).reshape(1, 1)
    logits_here, source_rel, source_total = lax.optimization_barrier(
        (logits_here, source_rel, source_total)
    )
    pack = jnp.concatenate([jnp.full((1, mine), LOW, F32), jnp.zeros((2, mine), F32)])

    s_shape, x_shape = shape((2 * cols, half)), shape((half, width), BF16)
    store = None
    if direct:
        for k in range(lines):
            x = line[k]
            if k == 3:
                x, _ = lax.optimization_barrier((x, pack))
            pair = [x, swap(x, 1)]
            ins = [*pair, target_feats, logits_here, pack]
            column = pl.BlockSpec((cols, rows), lambda _, k=k: (0, k))
            block = pl.BlockSpec((rows, width), lambda _, k=k: (k, 0))
            *store, pack = call(
                functools.partial(
                    cost_kernel, scale, True, k == 0, (k * rows, half + k * rows)
                ),
                "cost",
                ins + (store or []),
                [s_shape, s_shape, x_shape, x_shape, shape(pack.shape)],
                in_specs=[whole(a) for a in ins] + [ANY] * len(store or []),
                out_specs=[column, column, block, block, whole(pack)],
                input_output_aliases={5 + i: i for i in range(4)} if store else {},
            )
            if k == 0:
                line[1:], _ = lax.optimization_barrier((line[1:], pack))
                line.append(swap(line[2], 4))
        s0, s1, x0, x1 = store
    else:
        gathered = lax.all_gather(source_feats, AXIS, axis=0)[order].reshape(2, half, width)
        x0, x1 = gathered[0], gathered[1]

    def cost_piece(y, logit, index, height, store, pack):
        ins = [x0, x1, y, logit, pack]
        block = pl.BlockSpec((height, half), lambda _: (index, 0))
        return call(
            functools.partial(cost_kernel, scale, False, True, (0, half)),
            "cost",
            ins + store,
            [s_shape, s_shape, shape(pack.shape)],
            in_specs=[whole(a) for a in ins] + [ANY] * len(store),
            out_specs=[block, block, whole(pack)],
            input_output_aliases={5 + i: i for i in range(len(store))},
        )

    if not direct:
        s0, s1, pack = cost_piece(target_feats, logits_here, 0, cols, [], pack)
    s0, s1, pack = cost_piece(crossed[0], logits_there, 1, cols, [s0, s1], pack)

    *levels, last = row_levels(count)
    last_masks = (0, *last)
    for level in levels:
        packs = [pack] + [swap(pack, m) for m in level]
        (pack,) = call(
            functools.partial(merge_kernel, (0, *level), blocks),
            "merge",
            packs,
            [shape(pack.shape)],
        )
    packs = [pack] + [swap(pack, m) for m in last]

    tile = part
    tiles = 2 * cols // tile
    grid = (tiles,)
    turn = tiles // 2
    tall = pl.BlockSpec((tile, mine), lambda j: (j, 0))
    tall_half = pl.BlockSpec((tile, half), lambda j: (j, 0))
    flat = pl.BlockSpec((1, mine), lambda j: (0, 0))
    flat2 = pl.BlockSpec((2, mine), lambda j: (0, 0))
    lane = pl.BlockSpec((1, tile), lambda j: (0, j))
    lane2 = pl.BlockSpec((2, tile), lambda j: (0, j))
    lane_other = pl.BlockSpec((1, tile), lambda j: (0, (j + turn) % tiles))
    lane2_other = pl.BlockSpec((2, tile), lambda j: (0, (j + turn) % tiles))
    flat_shape, lane_shape = shape((1, mine)), shape((1, 2 * cols))
    e_shape = shape((2 * cols, mine))

    e, col, q, h = call(
        functools.partial(first_kernel, last_masks, blocks),
        "first",
        [*packs, s0, s1, source_rel, source_total],
        [e_shape, shape((2, 2 * cols)), flat_shape, shape((2, mine))],
        grid=grid,
        in_specs=[pl.BlockSpec(pack.shape, lambda j: (0, 0))] * len(packs)
        + [tall_half, tall_half, flat, pl.BlockSpec((1, 1), lambda j: (0, 0))],
        out_specs=[tall, lane2, flat, flat2],
    )
    col_other = swap(col, 2)
    if direct:
        crossed, _ = lax.optimization_barrier((crossed, pack))
        ys = [ys[0], crossed[0], ys[1], swap(crossed[0], 1)]
        col_other, *ys = lax.optimization_barrier((col_other, *ys))
    row, phi, g = call(
        first_row_kernel,
        "first_row",
        [e, col, col_other, logits],
        [flat_shape, lane_shape, lane_shape],
        grid=grid,
        in_specs=[tall, lane2, lane2_other, lane],
        out_specs=[flat, lane, lane],
    )

    def columns(row):
        for level in levels:
            row = row + sum(flip(swap(row, m), m, blocks) for m in level)
        sums = [row] + [swap(row, m) for m in last]
        return call(
            functools.partial(column_kernel, last_masks, blocks),
            "column",
            [*sums, e, h, phi],
            [lane_shape, flat_shape],
            grid=grid,
            in_specs=[flat] * len(sums) + [tall, flat2, lane],
            out_specs=[lane, flat],
        )

    for _ in range(ITERS - 2):
        col, a = columns(row)
        (row,) = call(
            row_kernel,
            "row",
            [e, col, swap(col, 2), logits, phi],
            [flat_shape],
            grid=grid,
            in_specs=[tall, lane, lane_other, lane, lane],
            out_specs=[flat],
        )
    col, a = columns(row)
    keep, send, mass, logb = call(
        functools.partial(plan_kernel, source_count),
        "plan",
        [e, a, h, col, swap(col, 2), logits, phi],
        [shape((2 * cols, half), BF16)] * 2 + [lane_shape, lane_shape],
        grid=grid,
        in_specs=[tall, flat, flat2, lane, lane_other, lane, lane],
        out_specs=[tall_half, tall_half, lane, lane],
    )

    feats = pl.BlockSpec((half, width), lambda _: (0, 0))

    def col_send(p, keep):
        piece = pl.BlockSpec((part, half), lambda _: (2 + p, 0))
        (out,) = call(
            col_send_kernel,
            "col_send",
            [keep, send, x0, x1, mass],
            [shape((part + TAIL, width), BF16)],
            in_specs=[piece, piece, feats, feats, pl.BlockSpec((1, part), lambda _: (0, 2 + p))],
        )
        return out

    out = col_send(0, keep)
    back = [swap(out, 2)]
    if direct:
        other_plan = swap(send, 1)
        block, block_out = shape((rows + TAIL, width)), shape((rows + TAIL, width), BF16)

        def row_parts(pair, gate):
            plan, other, _ = lax.optimization_barrier((keep, other_plan, gate))
            lanes = pl.BlockSpec((2 * cols, 2 * rows), lambda _: (0, pair))
            return call(
                row_part_kernel,
                "row_part",
                [plan, other, *ys],
                [block, block_out],
                in_specs=[lanes, lanes] + [whole(y) for y in ys],
            )

        own2, out3 = row_parts(1, out)
        near3 = swap(out3, 4)
        keep_gated, _ = lax.optimization_barrier((keep, out3))
        out = col_send(1, keep_gated)
        back.append(swap(out, 2))
        own0, out1 = row_parts(0, out)
        near1 = swap(out1, 4)
        (out2,) = call(line_kernel, "line", [own2, near3], [block_out])
        far2 = swap(out2, 8)
        (grad_source,) = call(
            source_kernel,
            "source",
            [own0, near1, far2, source_feats],
            [shape((rows, width))],
        )
        gate = out1
    else:
        out = col_send(1, keep)
        back.append(swap(out, 2))
        gate = out
        plan = jnp.concatenate([keep, send], axis=1)
        both = jnp.concatenate([target_feats, *crossed], axis=0)
        full = lax.dot_general(
            plan, both, (((0,), (0,)), ((), ())), preferred_element_type=F32
        ).reshape(blocks, rows, width)
        row_mass = jnp.sum(plan.astype(F32), axis=0).reshape(blocks, rows)
        full = jnp.zeros((count, rows, width), F32).at[order].set(full)
        row_mass = jnp.zeros((count, rows), F32).at[order].set(row_mass)
        grad_source = lax.psum_scatter(row_mass, AXIS, scatter_dimension=0)[:, None] * (
            source_feats.astype(F32)
        ) - lax.psum_scatter(full, AXIS, scatter_dimension=0)

    upper = pl.BlockSpec((cols, half), lambda _: (0, 0))
    keep_later, x0, x1, a, q, _ = lax.optimization_barrier((keep, x0, x1, a, q, gate))
    (own_col,) = call(
        col_keep_kernel,
        "col_keep",
        [keep_later, send, x0, x1],
        [shape((cols, width))],
        in_specs=[upper, upper, feats, feats],
    )
    grad_target = None
    for p in range(2):
        piece = pl.BlockSpec((part, width), lambda _, p=p: (p, 0))
        done = [] if grad_target is None else [grad_target]
        (grad_target,) = call(
            functools.partial(target_kernel, target_count / source_count),
            "target",
            [own_col, back[p], mass, target_feats, *done],
            [shape((cols, width))],
            in_specs=[
                piece,
                whole(back[p]),
                pl.BlockSpec((1, part), lambda _, p=p: (0, p)),
                piece,
            ]
            + [ANY] * len(done),
            out_specs=[piece],
            size=7 * part * width,
            input_output_aliases={4: 0} if done else {},
        )

    source_sq = scale * jnp.concatenate(
        [jnp.sum(jnp.square(x.astype(F32)), axis=1) for x in (x0, x1)]
    )
    potential = (q + jnp.log(a) - source_rel + source_total).reshape(mine) + source_sq
    potential = potential.reshape(1, mine)
    pair = [v.reshape(2, lines, rows) for v in (potential, swap(potential, 2))]
    potential_src = jnp.stack(pair).transpose(2, 0, 1, 3).reshape(count, rows)
    everyone = jnp.bitwise_xor(me, jnp.arange(count))
    potential_src = potential_src[everyone].reshape(source_count)
    target_sq = scale * jnp.sum(jnp.square(target_feats.astype(F32)), axis=1)
    potential_tgt = (g + logb)[0, :cols] + target_sq
    return (grad_source, grad_target, potential_src, potential_tgt)


def solution(mesh):
    return jax.shard_map(
        per_device,
        mesh=mesh,
        in_specs=(
            P(("groups", "tgt"), None),
            P(("groups", "tgt"), None),
            P("groups"),
            P(("groups", "tgt")),
        ),
        out_specs=(
            P(("groups", "tgt"), None),
            P(("groups", "tgt"), None),
            P("groups"),
            P(("groups", "tgt")),
        ),
        check_vma=False,
    )
```

```python
import functools
import math

import jax
import jax.numpy as jnp
from jax import lax
from jax.experimental import pallas as pl
from jax.experimental.pallas import tpu as pltpu
from jax.sharding import PartitionSpec as P

ITERS = 3
AXIS = "tgt"
F32 = jnp.float32
BF16 = jnp.bfloat16
TAIL = 8
LOW = -1e30


def call(body, name, ins, outs, size=1, in_hbm=(), out_hbm=False, scalar=False, **kw):
    held, away = pl.BlockSpec(memory_space=pltpu.VMEM), pl.BlockSpec(memory_space=pl.ANY)
    specs = [away if i in in_hbm else held for i in range(len(ins))]
    if scalar:
        specs[0] = pl.BlockSpec(memory_space=pltpu.SMEM)
    return pl.pallas_call(
        body,
        name=name,
        out_shape=outs,
        in_specs=specs,
        out_specs=[away if out_hbm else held] * len(outs),
        compiler_params=pltpu.CompilerParams(vmem_limit_bytes=12 << 20),
        cost_estimate=pl.CostEstimate(flops=1, bytes_accessed=size, transcendentals=0),
        **kw,
    )(*ins)


def tiles(count):
    step = min(count, 256)
    return [slice(i, i + step) for i in range(0, count, step)]


def shape(dims, dtype=F32):
    return jax.ShapeDtypeStruct(dims, dtype)


def swap(value, mask):
    count = lax.axis_size(AXIS)
    return lax.ppermute(value, AXIS, [(i, i ^ mask) for i in range(count)])


def row_levels(count):
    levels, step = [(1,)], 4
    while step < count:
        if step * 4 <= count:
            levels.append((3 * step, 2 * step, step))
            step *= 4
        else:
            levels.append((step,))
            step *= 2
    return levels


def flip(value, mask, blocks):
    move = (mask & 1) * (blocks // 2) + (mask >> 2)
    if not move:
        return value
    width = value.shape[-1] // blocks
    parts = [value[..., (r ^ move) * width : ((r ^ move) + 1) * width] for r in range(blocks)]
    return jnp.concatenate(parts, axis=-1)


def by_index(value, me, blocks):
    width = value.shape[1] // blocks
    bit = 1
    while bit < blocks:
        parts = [value[:, (r ^ bit) * width : ((r ^ bit) + 1) * width] for r in range(blocks)]
        value = jnp.where((me & bit) != 0, jnp.concatenate(parts, axis=1), value)
        bit *= 2
    return value


def prep_kernel(count, me_ref, logit_ref, rel_ref, total_ref):
    logit = logit_ref[...]
    total_ref[...] = jnp.log(jnp.sum(jnp.exp(logit), axis=1, keepdims=True))
    value = by_index(logit, me_ref[0, 0], count)
    rows = logit.shape[1] // count
    lines = count // 4
    for c in range(2):
        for k in range(lines):
            here, there = (c * lines + k) * rows, (4 * k + c) * rows
            rel_ref[:, here : here + rows] = value[:, there : there + rows]


def potential_kernel(
    count, scale, me_ref, own_ref, other_ref, g_ref, logb_ref, y_ref, source_ref, target_ref
):
    rows = source_ref.shape[1] // count
    lines = count // 4
    parts = []
    for r in range(count):
        start = ((r & 1) * lines + (r >> 2)) * rows
        ref = other_ref if r & 2 else own_ref
        parts.append(ref[1:2, start : start + rows])
    source_ref[...] = by_index(jnp.concatenate(parts, axis=1), me_ref[0, 0], count)
    cols = target_ref.shape[1]
    wide = y_ref[...].astype(F32)
    square = to_row(jnp.sum(wide * wide, axis=1, keepdims=True))
    target_ref[...] = g_ref[:, :cols] + logb_ref[:, :cols] + scale * square


def diagonal():
    return lax.broadcasted_iota(jnp.int32, (128, 128), 0) == lax.broadcasted_iota(
        jnp.int32, (128, 128), 1
    )


def to_column(row):
    same = diagonal()
    parts = [
        jnp.sum(
            jnp.where(same, jnp.broadcast_to(row[:, i : i + 128], (128, 128)), 0.0),
            axis=1,
            keepdims=True,
        )
        for i in range(0, row.shape[1], 128)
    ]
    return jnp.concatenate(parts, axis=0)


def to_row(column):
    same = diagonal()
    parts = [
        jnp.sum(
            jnp.where(same, jnp.broadcast_to(column[i : i + 128, :], (128, 128)), 0.0),
            axis=0,
            keepdims=True,
        )
        for i in range(0, column.shape[0], 128)
    ]
    return jnp.concatenate(parts, axis=1)


def cost_kernel(scale, copy, add_mass, cols, line, *refs):
    x_refs, y_ref, logit_ref, pack_ref = refs[:2], refs[2], refs[3], refs[4]
    outs = refs[-5:] if copy else refs[-3:]
    s_outs, pack_out = outs[:2], outs[-1]
    half = s_outs[0].shape[1]
    y = y_ref[...]
    wide = y.astype(F32)
    logit = logit_ref[...]
    lift = to_column(logit) - scale * jnp.sum(wide * wide, axis=1, keepdims=True)
    pack_out[...] = pack_ref[...]
    if add_mass:
        pack_out[2:3, :] = pack_ref[2:3, :] + jnp.sum(jnp.exp(logit), axis=1, keepdims=True)
    for c in range(2):
        x = x_refs[c][...] if copy else x_refs[c][line, :]
        if copy:
            outs[2 + c][line, :] = x
        s = (2.0 * scale) * lax.dot_general(
            y, x, (((1,), (1,)), ((), ())), preferred_element_type=F32
        )
        s_outs[c][cols, line] = s
        s = s + lift
        lanes = slice(c * half + line.start, c * half + line.stop)
        old = pack_ref[0:1, lanes]
        top = jnp.maximum(old, jnp.max(s, axis=0, keepdims=True))
        pack_out[0:1, lanes] = top
        pack_out[1:2, lanes] = pack_ref[1:2, lanes] * jnp.exp(old - top) + jnp.sum(
            jnp.exp(s - top), axis=0, keepdims=True
        )


def merge(packs, masks, blocks):
    packs = [flip(p, m, blocks) for p, m in zip(packs, masks)]
    top = functools.reduce(jnp.maximum, [p[0:1] for p in packs])
    total = sum(p[1:2] * jnp.exp(p[0:1] - top) for p in packs)
    return top, total, sum(p[2:3] for p in packs)


def merge_kernel(masks, blocks, *refs):
    top, total, mass = merge([r[...] for r in refs[:-1]], masks, blocks)
    refs[-1][0:1, :] = top
    refs[-1][1:2, :] = total
    refs[-1][2:3, :] = mass


def first_kernel(masks, blocks, *refs):
    pack_refs, refs = refs[: len(masks)], refs[len(masks) :]
    s_refs, refs = refs[:2], refs[2:]
    logit_ref, total_ref, e_ref, col_ref, q_ref, h_ref = refs
    top, total, mass = merge([r[...] for r in pack_refs], masks, blocks)
    h = logit_ref[...] - total_ref[...] + jnp.log(mass)
    h_ref[0:1, :] = h
    h_ref[1:2, :] = mass
    q = h - top - jnp.log(total)
    q_ref[...] = q
    half = s_refs[0].shape[1]
    for t in tiles(e_ref.shape[0]):
        parts = [s_refs[c][t, :] + q[:, c * half : (c + 1) * half] for c in range(2)]
        top = jnp.maximum(*[jnp.max(p, axis=1, keepdims=True) for p in parts])
        total = jnp.zeros_like(top)
        for c in range(2):
            e = jnp.exp(parts[c] - top)
            e_ref[t, c * half : (c + 1) * half] = e
            total = total + jnp.sum(e, axis=1, keepdims=True)
        col_ref[0:1, t] = to_row(top)
        col_ref[1:2, t] = to_row(total)


def turn(value):
    half = value.shape[1] // 2
    return jnp.concatenate([value[:, half:], value[:, :half]], axis=1)


def weighted_rows(e_ref, weight):
    return sum(
        jnp.sum(e_ref[t, :] * to_column(weight[:, t]), axis=0, keepdims=True)
        for t in tiles(e_ref.shape[0])
    )


def first_row_kernel(e_ref, own_ref, other_ref, logit_ref, row_ref, phi_ref, g_ref):
    own, other = own_ref[...], turn(other_ref[...])
    top = jnp.maximum(own[0:1, :], other[0:1, :])
    total = own[1:2, :] * jnp.exp(own[0:1, :] - top) + other[1:2, :] * jnp.exp(other[0:1, :] - top)
    g_ref[...] = -(top + jnp.log(total))
    phi = jnp.exp(own[0:1, :] - top) / total
    phi_ref[...] = phi
    row_ref[...] = weighted_rows(e_ref, jnp.exp(logit_ref[...]) * phi)


def row_kernel(e_ref, own_ref, other_ref, logit_ref, phi_ref, row_ref):
    c = own_ref[...] + turn(other_ref[...])
    row_ref[...] = weighted_rows(e_ref, jnp.exp(logit_ref[...]) * phi_ref[...] / c)


def column_kernel(masks, blocks, *refs):
    sum_refs, refs = refs[: len(masks)], refs[len(masks) :]
    e_ref, h_ref, phi_ref, *base_ref, col_ref, a_ref = refs
    total = sum(flip(r[...], m, blocks) for r, m in zip(sum_refs, masks))
    a = jnp.exp(h_ref[0:1, :]) / total
    a_ref[...] = a
    for t in tiles(e_ref.shape[0]):
        total = jnp.sum(e_ref[t, :] * a, axis=1, keepdims=True)
        col_ref[0:1, t] = to_row(total) * phi_ref[:, t]
    if base_ref:
        col_ref[1:2, :] = base_ref[0][...] + jnp.log(a)


def plan_kernel(source_count, *refs):
    e_ref, a_ref, h_ref, own_ref, other_ref, logit_ref, phi_ref = refs[:7]
    keep_ref, near_ref, far_ref, mass_ref, logb_ref = refs[7:]
    c = own_ref[0:1, :] + turn(other_ref[0:1, :])
    logb_ref[...] = -jnp.log(c)
    share = jnp.exp(logit_ref[...]) * phi_ref[...] * (source_count / h_ref[1:2, :1]) / c
    half = keep_ref.shape[1]
    a = a_ref[...]
    for t in tiles(e_ref.shape[0]):
        plan = ((e_ref[t, :] * a) * to_column(share[:, t])).astype(BF16)
        keep_ref[t, :] = plan[:, :half]
        near_ref[t, :] = plan[:, half : half + half // 2]
        far_ref[t, :] = plan[:, half + half // 2 :]
        mass_ref[:, t] = to_row(jnp.sum(plan.astype(F32), axis=1, keepdims=True))


def split_mass(mass, width):
    mass = jnp.concatenate([mass, jnp.zeros((1, width - mass.shape[1]), F32)], axis=1)
    high = mass.astype(BF16).astype(F32)
    rest = mass - high
    middle = rest.astype(BF16).astype(F32)
    row = lax.broadcasted_iota(jnp.int32, (TAIL, width), 0)
    out = jnp.where(row == 0, high, jnp.where(row == 1, middle, rest - middle))
    return jnp.where(row < 3, out, 0.0).astype(BF16)


def joined_mass(ref, width):
    return jnp.sum(ref[ref.shape[0] - TAIL :, :width].astype(F32), axis=0, keepdims=True)


def row_part_kernel(lanes, keep_ref, other_ref, *refs):
    y_refs, (own_ref, out_ref) = refs[:-2], refs[-2:]
    group = len(y_refs) // 2
    part = mass = 0.0
    for plan_ref, part_lanes, ys in (
        (keep_ref, lanes, y_refs[:group]),
        (other_ref, slice(None), y_refs[group:]),
    ):
        start = 0
        for y in ys:
            block = plan_ref[start : start + y.shape[0], part_lanes]
            start += y.shape[0]
            part = part + lax.dot_general(
                block, y[...], (((0,), (0,)), ((), ())), preferred_element_type=F32
            )
            mass = mass + jnp.sum(block.astype(F32), axis=0, keepdims=True)
    rows = own_ref.shape[0] - TAIL
    width = own_ref.shape[1]
    own_ref[:rows, :] = part[:rows, :]
    own_ref[rows:, :] = jnp.concatenate(
        [jnp.broadcast_to(mass[:, :rows], (TAIL, rows)), jnp.zeros((TAIL, width - rows), F32)],
        axis=1,
    )
    out_ref[:rows, :] = part[rows:, :].astype(BF16)
    out_ref[rows:, :] = split_mass(mass[:, rows:], width)


def line_kernel(own_ref, other_ref, out_ref):
    rows, width = out_ref.shape[0] - TAIL, out_ref.shape[1]
    out_ref[:rows, :] = (own_ref[:rows, :] + other_ref[:rows, :].astype(F32)).astype(BF16)
    mass = own_ref[rows : rows + 1, :rows] + joined_mass(other_ref, rows)
    out_ref[rows:, :] = split_mass(mass, width)


def source_kernel(own_ref, near_ref, far_ref, x_ref, out_ref):
    rows = out_ref.shape[0]
    part = own_ref[:rows, :] + near_ref[:rows, :].astype(F32) + far_ref[:rows, :].astype(F32)
    mass = own_ref[rows : rows + 1, :rows] + joined_mass(near_ref, rows)
    mass = mass + joined_mass(far_ref, rows)
    out_ref[...] = to_column(mass) * x_ref[:rows, :].astype(F32) - part


def col_part(keep_ref, near_ref, far_ref, x0_ref, x1_ref, cols):
    half = near_ref.shape[1]
    part = jnp.dot(keep_ref[cols, :], x0_ref[...], preferred_element_type=F32)
    part = part + jnp.dot(near_ref[cols, :], x1_ref[:half, :], preferred_element_type=F32)
    return part + jnp.dot(far_ref[cols, :], x1_ref[half:, :], preferred_element_type=F32)


def col_send_kernel(cols, *refs):
    *refs, mass_ref, out_ref = refs
    part = col_part(*refs, cols)
    out_ref[: part.shape[0], :] = part.astype(BF16)
    out_ref[part.shape[0] :, :] = split_mass(mass_ref[:, cols], part.shape[1])


def col_keep_kernel(*refs):
    *refs, out_ref = refs
    out_ref[...] = col_part(*refs, slice(0, out_ref.shape[0]))


def target_rows(factor, cols, own_ref, other_ref, mass_ref, y_ref, out_ref, held_ref, sem_ref):
    count = cols.stop - cols.start
    mass = mass_ref[:, cols] + joined_mass(other_ref, count)
    copies = []
    for n, t in enumerate(slice(i, i + 128) for i in range(0, count, 128)):
        here = slice(cols.start + t.start, cols.start + t.stop)
        part = own_ref[here, :] + other_ref[t, :].astype(F32)
        held_ref[t, :] = factor * (to_column(mass[:, t]) * y_ref[here, :].astype(F32) - part)
        copies.append(pltpu.make_async_copy(held_ref.at[t], out_ref.at[here], sem_ref.at[n]))
        copies[-1].start()
    return copies


def target_kernel(factor, cols, *refs):
    for copy in target_rows(factor, cols, *refs):
        copy.wait()


def last_kernel(factor, cols, *refs):
    target_ins, (_, own_ref, near_ref, far_ref, x_ref), refs = refs[:4], refs[4:9], refs[9:]
    target_out, source_out, held_target, sem_target, held_source, sem_source = refs
    source_kernel(own_ref, near_ref, far_ref, x_ref, held_source)
    first = pltpu.make_async_copy(held_source, source_out, sem_source)
    first.start()
    copies = target_rows(factor, cols, *target_ins, target_out, held_target, sem_target)
    for copy in [first, *copies]:
        copy.wait()


def per_device(source_feats, target_feats, source_logits, target_logits):
    count = lax.axis_size(AXIS)
    me = lax.axis_index(AXIS)
    rows, width = source_feats.shape
    cols = target_feats.shape[0]
    source_count = rows * count
    target_count = cols * count
    scale = 1.0 / math.sqrt(width)
    direct = count == 16
    blocks = count // 2
    lines = blocks // 2
    mine = source_count // 2
    half = mine // 2
    parts = [slice(0, cols * 3 // 4), slice(cols * 3 // 4, cols)]
    masks = [4 * k + c for c in range(2) for k in range(lines)]
    order = jnp.bitwise_xor(me, jnp.array(masks))

    if direct:
        far = swap(source_feats, 8)
        line = [source_feats, swap(source_feats, 4), far]
    crossed = [swap(target_feats, 2)]
    logits_here = target_logits.reshape(1, cols)
    logits_there = swap(logits_here, 2)
    logits = jnp.concatenate([logits_here, logits_there], axis=1)
    here = me.astype(jnp.int32).reshape(1, 1)
    source_rel, source_total = call(
        functools.partial(prep_kernel, count),
        "prep",
        [here, source_logits.reshape(1, source_count)],
        [shape((1, mine)), shape((1, 1))],
        scalar=True,
    )
    logits_here, source_rel, source_total = lax.optimization_barrier(
        (logits_here, source_rel, source_total)
    )
    pack = jnp.concatenate([jnp.full((1, mine), LOW, F32), jnp.zeros((2, mine), F32)])

    s_shape, x_shape = shape((2 * cols, half)), shape((half, width), BF16)
    store = None

    def cost_piece(y, logit, start, line, xs, store, pack, first=True):
        return call(
            functools.partial(cost_kernel, scale, False, first, slice(start, start + cols), line),
            "cost",
            [*xs, y, logit, pack, *store],
            [s_shape, s_shape, shape(pack.shape)],
            input_output_aliases={5 + i: i for i in range(len(store))},
        )

    if direct:
        for k in range(lines):
            x = line[k]
            if k == 3:
                x, *_ = lax.optimization_barrier((x, logits_there, pack))
                s0, s1, pack = cost_piece(
                    crossed[0], logits_there, cols, slice(0, k * rows), store[2:], store[:2], pack
                )
                store = [s0, s1, *store[2:]]
            pair = [x, swap(x, 1)]
            ins = [*pair, target_feats, logits_here, pack]
            *store, pack = call(
                functools.partial(
                    cost_kernel,
                    scale,
                    True,
                    k == 0,
                    slice(0, cols),
                    slice(k * rows, (k + 1) * rows),
                ),
                "cost",
                ins + (store or []),
                [s_shape, s_shape, x_shape, x_shape, shape(pack.shape)],
                input_output_aliases={5 + i: i for i in range(4)} if store else {},
            )
            if k == 0:
                *line[1:], y, _ = lax.optimization_barrier((*line[1:], target_feats, pack))
                line.append(swap(line[2], 4))
                ys = [target_feats, swap(y, 1)]
        s0, s1, x0, x1 = store
        s0, s1, pack = cost_piece(
            crossed[0],
            logits_there,
            cols,
            slice(3 * rows, half),
            [x0, x1],
            [s0, s1],
            pack,
            first=False,
        )
    else:
        gathered = lax.all_gather(source_feats, AXIS, axis=0)[order].reshape(2, half, width)
        x0, x1 = gathered[0], gathered[1]
        full = slice(0, half)
        s0, s1, pack = cost_piece(target_feats, logits_here, 0, full, [x0, x1], [], pack)
        s0, s1, pack = cost_piece(crossed[0], logits_there, cols, full, [x0, x1], [s0, s1], pack)

    *levels, last = row_levels(count)
    last_masks = (0, *last)
    for level in levels:
        packs = [pack] + [swap(pack, m) for m in level]
        (pack,) = call(
            functools.partial(merge_kernel, (0, *level), blocks),
            "merge",
            packs,
            [shape(pack.shape)],
        )
    packs = [pack] + [swap(pack, m) for m in last]

    flat_shape, lane_shape = shape((1, mine)), shape((1, 2 * cols))
    e_shape = shape((2 * cols, mine))

    e, col, q, h = call(
        functools.partial(first_kernel, last_masks, blocks),
        "first",
        [*packs, s0, s1, source_rel, source_total],
        [e_shape, shape((2, 2 * cols)), flat_shape, shape((2, mine))],
    )
    col_other = swap(col, 2)
    if direct:
        crossed, _ = lax.optimization_barrier((crossed, pack))
        ys = [ys[0], crossed[0], ys[1], swap(crossed[0], 1)]
        col_other, *ys = lax.optimization_barrier((col_other, *ys))
    row, phi, g = call(
        first_row_kernel,
        "first_row",
        [e, col, col_other, logits],
        [flat_shape, lane_shape, lane_shape],
    )

    def columns(row, *base):
        for level in levels:
            row = row + sum(flip(swap(row, m), m, blocks) for m in level)
        sums = [row] + [swap(row, m) for m in last]
        return call(
            functools.partial(column_kernel, last_masks, blocks),
            "column",
            [*sums, e, h, phi, *base],
            [shape((1 + len(base), 2 * cols)), flat_shape],
        )

    for _ in range(ITERS - 2):
        col, a = columns(row)
        (row,) = call(
            row_kernel,
            "row",
            [e, col, swap(col, 2), logits, phi],
            [flat_shape],
        )
    assert mine == 2 * cols
    source_sq = scale * jnp.concatenate(
        [jnp.sum(jnp.square(x.astype(F32)), axis=1) for x in (x0, x1)]
    )
    base = q - source_rel + source_total + source_sq.reshape(1, mine)
    col, a = columns(row, base)
    col_other = swap(col, 2)
    keep, *sends, mass, logb = call(
        functools.partial(plan_kernel, source_count),
        "plan",
        [e, a, h, col, col_other, logits, phi],
        [shape((2 * cols, half), BF16)]
        + [shape((2 * cols, half // 2), BF16)] * 2
        + [lane_shape, lane_shape],
    )

    def col_send(p, keep):
        piece = slice(cols + parts[p].start, cols + parts[p].stop)
        (out,) = call(
            functools.partial(col_send_kernel, piece),
            "col_send",
            [keep, *sends, x0, x1, mass],
            [shape((parts[p].stop - parts[p].start + TAIL, width), BF16)],
        )
        return out

    out = col_send(0, keep)
    back = [swap(out, 2)]
    if direct:
        others = [None, swap(sends[1], 1)]
        others[0] = swap(sends[0], 1)
        block, block_out = shape((rows + TAIL, width)), shape((rows + TAIL, width), BF16)

        def row_parts(pair, gate):
            plan, other, _ = lax.optimization_barrier((keep, others[pair], gate))
            lanes = slice(2 * pair * rows, 2 * (pair + 1) * rows)
            return call(
                functools.partial(row_part_kernel, lanes),
                "row_part",
                [plan, other, *ys],
                [block, block_out],
            )

        own2, out3 = row_parts(1, out)
        near3 = swap(out3, 4)
        keep_gated, _ = lax.optimization_barrier((keep, out3))
        out = col_send(1, keep_gated)
        back.append(swap(out, 2))
        own0, out1 = row_parts(0, out)
        near1 = swap(out1, 4)
        (out2,) = call(line_kernel, "line", [own2, near3], [block_out])
        far2 = swap(out2, 8)
        ends = [own0, near1, far2, x0]
        gate = out1
    else:
        out = col_send(1, keep)
        back.append(swap(out, 2))
        gate = out
        plan = jnp.concatenate([keep, *sends], axis=1)
        both = jnp.concatenate([target_feats, *crossed], axis=0)
        full = lax.dot_general(
            plan, both, (((0,), (0,)), ((), ())), preferred_element_type=F32
        ).reshape(blocks, rows, width)
        row_mass = jnp.sum(plan.astype(F32), axis=0).reshape(blocks, rows)
        full = jnp.zeros((count, rows, width), F32).at[order].set(full)
        row_mass = jnp.zeros((count, rows), F32).at[order].set(row_mass)
        grad_source = lax.psum_scatter(row_mass, AXIS, scatter_dimension=0)[:, None] * (
            source_feats.astype(F32)
        ) - lax.psum_scatter(full, AXIS, scatter_dimension=0)

    logb, _ = lax.optimization_barrier((logb, gate))
    potential_src, potential_tgt = call(
        functools.partial(potential_kernel, count, scale),
        "potential",
        [here, col, col_other, g, logb, target_feats],
        [shape((1, source_count)), shape((1, cols))],
        scalar=True,
    )
    keep_later, _ = lax.optimization_barrier((keep, potential_tgt))
    (own_col,) = call(
        col_keep_kernel,
        "col_keep",
        [keep_later, *sends, x0, x1],
        [shape((cols, width))],
    )
    factor = target_count / source_count

    def held(p):
        size = parts[p].stop - parts[p].start
        return [pltpu.VMEM((size, width), F32), pltpu.SemaphoreType.DMA((size // 128,))]

    ins = [own_col, back[0], mass, target_feats]
    (grad_target,) = call(
        functools.partial(target_kernel, factor, parts[0]),
        "target",
        ins,
        [shape((cols, width))],
        size=4 * cols * width,
        out_hbm=True,
        scratch_shapes=held(0),
    )
    ins = [own_col, back[1], mass, target_feats, grad_target]
    kw = dict(size=cols * width, in_hbm=(4,), out_hbm=True, input_output_aliases={4: 0})
    if direct:
        grad_target, grad_source = call(
            functools.partial(last_kernel, factor, parts[1]),
            "last",
            ins + ends,
            [shape((cols, width)), shape((rows, width))],
            scratch_shapes=held(1) + [pltpu.VMEM((rows, width), F32), pltpu.SemaphoreType.DMA],
            **kw,
        )
    else:
        (grad_target,) = call(
            lambda *refs: target_kernel(factor, parts[1], *refs[:4], *refs[5:]),
            "target",
            ins,
            [shape((cols, width))],
            scratch_shapes=held(1),
            **kw,
        )

    potential_src = potential_src.reshape(source_count)
    potential_tgt = potential_tgt.reshape(cols)
    return (grad_source, grad_target, potential_src, potential_tgt)


def solution(mesh):
    return jax.shard_map(
        per_device,
        mesh=mesh,
        in_specs=(
            P(("groups", "tgt"), None),
            P(("groups", "tgt"), None),
            P("groups"),
            P(("groups", "tgt")),
        ),
        out_specs=(
            P(("groups", "tgt"), None),
            P(("groups", "tgt"), None),
            P("groups"),
            P(("groups", "tgt")),
        ),
        check_vma=False,
    )
```

```python
import functools
import math

import jax
import jax.numpy as jnp
from jax import lax
from jax.experimental import pallas as pl
from jax.experimental.pallas import tpu as pltpu
from jax.sharding import PartitionSpec as P

ITERS = 3
AXIS = "tgt"
F32 = jnp.float32
BF16 = jnp.bfloat16
TAIL = 8
LOW = -1e30


def call(body, name, ins, outs, size=1, in_hbm=(), out_hbm=False, scalar=False, **kw):
    held, away = pl.BlockSpec(memory_space=pltpu.VMEM), pl.BlockSpec(memory_space=pl.ANY)
    specs = [away if i in in_hbm else held for i in range(len(ins))]
    if scalar:
        specs[0] = pl.BlockSpec(memory_space=pltpu.SMEM)
    return pl.pallas_call(
        body,
        name=name,
        out_shape=outs,
        in_specs=specs,
        out_specs=[away if out_hbm else held] * len(outs),
        compiler_params=pltpu.CompilerParams(vmem_limit_bytes=12 << 20),
        cost_estimate=pl.CostEstimate(flops=1, bytes_accessed=size, transcendentals=0),
        **kw,
    )(*ins)


def tiles(count):
    step = min(count, 128)
    return [slice(i, i + step) for i in range(0, count, step)]


def shape(dims, dtype=F32):
    return jax.ShapeDtypeStruct(dims, dtype)


def swap(value, mask):
    count = lax.axis_size(AXIS)
    return lax.ppermute(value, AXIS, [(i, i ^ mask) for i in range(count)])


def row_levels(count):
    levels, step = [(1,)], 4
    while step < count:
        if step * 4 <= count:
            levels.append((3 * step, 2 * step, step))
            step *= 4
        else:
            levels.append((step,))
            step *= 2
    return levels


def flip(value, mask, blocks):
    move = (mask & 1) * (blocks // 2) + (mask >> 2)
    if not move:
        return value
    width = value.shape[-1] // blocks
    parts = [value[..., (r ^ move) * width : ((r ^ move) + 1) * width] for r in range(blocks)]
    return jnp.concatenate(parts, axis=-1)


def by_index(value, me, blocks):
    width = value.shape[1] // blocks
    bit = 1
    while bit < blocks:
        parts = [value[:, (r ^ bit) * width : ((r ^ bit) + 1) * width] for r in range(blocks)]
        value = jnp.where((me & bit) != 0, jnp.concatenate(parts, axis=1), value)
        bit *= 2
    return value


def prep_kernel(count, me_ref, logit_ref, rel_ref):
    logit = logit_ref[...]
    logit = logit - jnp.log(jnp.sum(jnp.exp(logit), axis=1, keepdims=True))
    value = by_index(logit, me_ref[0, 0], count)
    rows = logit.shape[1] // count
    lines = count // 4
    for c in range(2):
        for k in range(lines):
            here, there = (c * lines + k) * rows, (4 * k + c) * rows
            rel_ref[:, here : here + rows] = value[:, there : there + rows]


def potential_kernel(
    count, scale, me_ref, own_ref, other_ref, g_ref, logb_ref, y_ref, source_ref, target_ref
):
    rows = source_ref.shape[1] // count
    lines = count // 4
    parts = []
    for r in range(count):
        start = ((r & 1) * lines + (r >> 2)) * rows
        ref = other_ref if r & 2 else own_ref
        parts.append(ref[1:2, start : start + rows])
    source_ref[...] = by_index(jnp.concatenate(parts, axis=1), me_ref[0, 0], count)
    cols = target_ref.shape[1]
    wide = y_ref[...].astype(F32)
    square = to_row(jnp.sum(wide * wide, axis=1, keepdims=True))
    target_ref[...] = g_ref[:, :cols] + logb_ref[:, :cols] + scale * square


def diagonal():
    return lax.broadcasted_iota(jnp.int32, (128, 128), 0) == lax.broadcasted_iota(
        jnp.int32, (128, 128), 1
    )


def to_column(row):
    same = diagonal()
    parts = [
        jnp.sum(
            jnp.where(same, jnp.broadcast_to(row[:, i : i + 128], (128, 128)), 0.0),
            axis=1,
            keepdims=True,
        )
        for i in range(0, row.shape[1], 128)
    ]
    return jnp.concatenate(parts, axis=0)


def to_row(column):
    same = diagonal()
    parts = [
        jnp.sum(
            jnp.where(same, jnp.broadcast_to(column[i : i + 128, :], (128, 128)), 0.0),
            axis=0,
            keepdims=True,
        )
        for i in range(0, column.shape[0], 128)
    ]
    return jnp.concatenate(parts, axis=1)


def cost_kernel(scale, copy, fresh, add_mass, cols, line, *refs):
    count = len(cols)
    x_refs, y_refs, side_refs = refs[:2], refs[2 : 2 + count], refs[2 + count : 2 + 2 * count]
    pack_ref = refs[2 + 2 * count]
    outs = refs[-(3 + 2 * copy + fresh) :]
    s_outs, pack_out = outs[:2], outs[2 + 2 * copy]
    half = s_outs[0].shape[1]
    pack_out[...] = pack_ref[...]
    lifts = [side[...] for side in side_refs]
    if fresh:
        logit = lifts[0]
        wide = y_refs[0][...].astype(F32)
        lifts = [to_column(logit) - scale * jnp.sum(wide * wide, axis=1, keepdims=True)]
        outs[-1][...] = lifts[0]
        if add_mass:
            mass = jnp.sum(jnp.exp(logit), axis=1, keepdims=True)
            pack_out[2:3, :] = pack_ref[2:3, :] + mass
    for c in range(2):
        x = x_refs[c][...] if copy else x_refs[c][line, :]
        if copy:
            outs[2 + c][line, :] = x
        lanes = slice(c * half + line.start, c * half + line.stop)
        top, total = pack_ref[0:1, lanes], pack_ref[1:2, lanes]
        for y_ref, lift, here in zip(y_refs, lifts, cols):
            s = (2.0 * scale) * lax.dot_general(
                y_ref[...], x, (((1,), (1,)), ((), ())), preferred_element_type=F32
            )
            s_outs[c][here, line] = s
            s = s + lift
            old, top = top, jnp.maximum(top, jnp.max(s, axis=0, keepdims=True))
            total = total * jnp.exp(old - top) + jnp.sum(jnp.exp(s - top), axis=0, keepdims=True)
        pack_out[0:1, lanes] = top
        pack_out[1:2, lanes] = total


def merge(packs, masks, blocks):
    packs = [flip(p, m, blocks) for p, m in zip(packs, masks)]
    top = functools.reduce(jnp.maximum, [p[0:1] for p in packs])
    total = sum(p[1:2] * jnp.exp(p[0:1] - top) for p in packs)
    return top, total, sum(p[2:3] for p in packs)


def merge_kernel(masks, blocks, *refs):
    top, total, mass = merge([r[...] for r in refs[:-1]], masks, blocks)
    refs[-1][0:1, :] = top
    refs[-1][1:2, :] = total
    refs[-1][2:3, :] = mass


def first_kernel(masks, blocks, *refs):
    pack_refs, refs = refs[: len(masks)], refs[len(masks) :]
    s_refs, refs = refs[:2], refs[2:]
    log_ref, e_ref, col_ref, q_ref, h_ref = refs
    top, total, mass = merge([r[...] for r in pack_refs], masks, blocks)
    h = log_ref[...] + jnp.log(mass)
    h_ref[0:1, :] = h
    h_ref[1:2, :] = mass
    q = h - top - jnp.log(total)
    q_ref[...] = q
    half = s_refs[0].shape[1]
    for t in tiles(e_ref.shape[0]):
        parts = [s_refs[c][t, :] + q[:, c * half : (c + 1) * half] for c in range(2)]
        top = jnp.maximum(*[jnp.max(p, axis=1, keepdims=True) for p in parts])
        total = jnp.zeros_like(top)
        for c in range(2):
            e = jnp.exp(parts[c] - top)
            e_ref[t, c * half : (c + 1) * half] = e
            total = total + jnp.sum(e, axis=1, keepdims=True)
        col_ref[0:1, t] = to_row(top)
        col_ref[1:2, t] = to_row(total)


def turn(value):
    half = value.shape[1] // 2
    return jnp.concatenate([value[:, half:], value[:, :half]], axis=1)


def weighted_rows(e_ref, weight):
    return sum(
        jnp.sum(e_ref[t, :] * to_column(weight[:, t]), axis=0, keepdims=True)
        for t in tiles(e_ref.shape[0])
    )


def first_row_kernel(e_ref, own_ref, other_ref, logit_ref, row_ref, phi_ref, g_ref):
    own, other = own_ref[...], turn(other_ref[...])
    top = jnp.maximum(own[0:1, :], other[0:1, :])
    total = own[1:2, :] * jnp.exp(own[0:1, :] - top) + other[1:2, :] * jnp.exp(other[0:1, :] - top)
    g_ref[...] = -(top + jnp.log(total))
    phi = jnp.exp(own[0:1, :] - top) / total
    phi_ref[...] = phi
    row_ref[...] = weighted_rows(e_ref, jnp.exp(logit_ref[...]) * phi)


def row_kernel(e_ref, own_ref, other_ref, logit_ref, phi_ref, row_ref):
    c = own_ref[...] + turn(other_ref[...])
    row_ref[...] = weighted_rows(e_ref, jnp.exp(logit_ref[...]) * phi_ref[...] / c)


def column_kernel(masks, blocks, *refs):
    sum_refs, refs = refs[: len(masks)], refs[len(masks) :]
    (e_ref, h_ref, phi_ref), rest = refs[:3], refs[3:]
    col_ref = rest[-2] if len(rest) > 1 else rest[0]
    total = sum(flip(r[...], m, blocks) for r, m in zip(sum_refs, masks))
    a = jnp.exp(h_ref[0:1, :]) / total
    for t in tiles(e_ref.shape[0]):
        total = jnp.sum(e_ref[t, :] * a, axis=1, keepdims=True)
        col_ref[0:1, t] = to_row(total) * phi_ref[:, t]
    if len(rest) > 1:
        rest[-1][...] = a
        col_ref[1:2, :] = rest[0][...] + jnp.log(a)


def plan_kernel(source_count, *refs):
    e_ref, a_ref, h_ref, own_ref, other_ref, logit_ref, phi_ref = refs[:7]
    keep_ref, near_ref, far_ref, mass_ref, logb_ref = refs[7:]
    c = own_ref[0:1, :] + turn(other_ref[0:1, :])
    logb_ref[...] = -jnp.log(c)
    share = jnp.exp(logit_ref[...]) * phi_ref[...] * (source_count / h_ref[1:2, :1]) / c
    half = keep_ref.shape[1]
    a = a_ref[...]
    for t in tiles(e_ref.shape[0]):
        plan = ((e_ref[t, :] * a) * to_column(share[:, t])).astype(BF16)
        keep_ref[t, :] = plan[:, :half]
        near_ref[t, :] = plan[:, half : half + half // 2]
        far_ref[t, :] = plan[:, half + half // 2 :]
        mass_ref[:, t] = to_row(jnp.sum(plan.astype(F32), axis=1, keepdims=True))


def split_mass(mass, width):
    mass = jnp.concatenate([mass, jnp.zeros((1, width - mass.shape[1]), F32)], axis=1)
    high = mass.astype(BF16).astype(F32)
    rest = mass - high
    middle = rest.astype(BF16).astype(F32)
    row = lax.broadcasted_iota(jnp.int32, (TAIL, width), 0)
    out = jnp.where(row == 0, high, jnp.where(row == 1, middle, rest - middle))
    return jnp.where(row < 3, out, 0.0).astype(BF16)


def joined_mass(ref, width):
    return jnp.sum(ref[ref.shape[0] - TAIL :, :width].astype(F32), axis=0, keepdims=True)


def row_part_kernel(lanes, keep_ref, other_ref, *refs):
    y_refs, (own_ref, out_ref) = refs[:-2], refs[-2:]
    group = len(y_refs) // 2
    part = mass = 0.0
    for plan_ref, part_lanes, ys in (
        (keep_ref, lanes, y_refs[:group]),
        (other_ref, slice(None), y_refs[group:]),
    ):
        start = 0
        for y in ys:
            block = plan_ref[start : start + y.shape[0], part_lanes]
            start += y.shape[0]
            part = part + lax.dot_general(
                block, y[...], (((0,), (0,)), ((), ())), preferred_element_type=F32
            )
            mass = mass + jnp.sum(block.astype(F32), axis=0, keepdims=True)
    rows = own_ref.shape[0] - TAIL
    width = own_ref.shape[1]
    own_ref[:rows, :] = part[:rows, :]
    own_ref[rows:, :] = jnp.concatenate(
        [jnp.broadcast_to(mass[:, :rows], (TAIL, rows)), jnp.zeros((TAIL, width - rows), F32)],
        axis=1,
    )
    out_ref[:rows, :] = part[rows:, :].astype(BF16)
    out_ref[rows:, :] = split_mass(mass[:, rows:], width)


def line_kernel(own_ref, other_ref, out_ref):
    rows, width = out_ref.shape[0] - TAIL, out_ref.shape[1]
    out_ref[:rows, :] = (own_ref[:rows, :] + other_ref[:rows, :].astype(F32)).astype(BF16)
    mass = own_ref[rows : rows + 1, :rows] + joined_mass(other_ref, rows)
    out_ref[rows:, :] = split_mass(mass, width)


def source_kernel(own_ref, near_ref, far_ref, x_ref, out_ref):
    rows = out_ref.shape[0]
    part = own_ref[:rows, :] + near_ref[:rows, :].astype(F32) + far_ref[:rows, :].astype(F32)
    mass = own_ref[rows : rows + 1, :rows] + joined_mass(near_ref, rows)
    mass = mass + joined_mass(far_ref, rows)
    out_ref[...] = to_column(mass) * x_ref[:rows, :].astype(F32) - part


def col_part(keep_ref, near_ref, far_ref, x0_ref, x1_ref, cols):
    half = near_ref.shape[1]
    part = jnp.dot(keep_ref[cols, :], x0_ref[...], preferred_element_type=F32)
    part = part + jnp.dot(near_ref[cols, :], x1_ref[:half, :], preferred_element_type=F32)
    return part + jnp.dot(far_ref[cols, :], x1_ref[half:, :], preferred_element_type=F32)


def col_send_kernel(cols, *refs):
    *refs, mass_ref, out_ref = refs
    part = col_part(*refs, cols)
    out_ref[: part.shape[0], :] = part.astype(BF16)
    out_ref[part.shape[0] :, :] = split_mass(mass_ref[:, cols], part.shape[1])


def col_keep_kernel(*refs):
    *refs, out_ref = refs
    out_ref[...] = col_part(*refs, slice(0, out_ref.shape[0]))


def target_rows(factor, cols, own_ref, other_ref, mass_ref, y_ref, out_ref, held_ref, sem_ref):
    count = cols.stop - cols.start
    mass = mass_ref[:, cols] + joined_mass(other_ref, count)
    copies = []
    for n, t in enumerate(slice(i, i + 128) for i in range(0, count, 128)):
        here = slice(cols.start + t.start, cols.start + t.stop)
        part = own_ref[here, :] + other_ref[t, :].astype(F32)
        held_ref[t, :] = factor * (to_column(mass[:, t]) * y_ref[here, :].astype(F32) - part)
        copies.append(pltpu.make_async_copy(held_ref.at[t], out_ref.at[here], sem_ref.at[n]))
        copies[-1].start()
    return copies


def target_kernel(factor, cols, *refs):
    for copy in target_rows(factor, cols, *refs):
        copy.wait()


def last_kernel(factor, cols, *refs):
    target_ins, (_, own_ref, near_ref, far_ref, x_ref), refs = refs[:4], refs[4:9], refs[9:]
    target_out, source_out, held_target, sem_target, held_source, sem_source = refs
    source_kernel(own_ref, near_ref, far_ref, x_ref, held_source)
    first = pltpu.make_async_copy(held_source, source_out, sem_source)
    first.start()
    copies = target_rows(factor, cols, *target_ins, target_out, held_target, sem_target)
    for copy in [first, *copies]:
        copy.wait()


def per_device(source_feats, target_feats, source_logits, target_logits):
    count = lax.axis_size(AXIS)
    me = lax.axis_index(AXIS)
    rows, width = source_feats.shape
    cols = target_feats.shape[0]
    source_count = rows * count
    target_count = cols * count
    scale = 1.0 / math.sqrt(width)
    direct = count == 16
    blocks = count // 2
    lines = blocks // 2
    mine = source_count // 2
    half = mine // 2
    parts = [slice(0, cols * 3 // 4), slice(cols * 3 // 4, cols)]
    masks = [4 * k + c for c in range(2) for k in range(lines)]
    order = jnp.bitwise_xor(me, jnp.array(masks))

    if direct:
        far = swap(source_feats, 8)
        line = [source_feats, swap(source_feats, 4), far]
    crossed = [swap(target_feats, 2)]
    logits_here = target_logits.reshape(1, cols)
    logits_there = swap(logits_here, 2)
    logits = jnp.concatenate([logits_here, logits_there], axis=1)
    here = me.astype(jnp.int32).reshape(1, 1)
    (source_log,) = call(
        functools.partial(prep_kernel, count),
        "prep",
        [here, source_logits.reshape(1, source_count)],
        [shape((1, mine))],
        scalar=True,
    )
    logits_here, source_log = lax.optimization_barrier((logits_here, source_log))
    pack = jnp.concatenate([jnp.full((1, mine), LOW, F32), jnp.zeros((2, mine), F32)])

    s_shape, x_shape = shape((2 * cols, half)), shape((half, width), BF16)
    here_cols, there_cols = slice(0, cols), slice(cols, 2 * cols)
    lift_shape = shape((cols, 1))

    def cost(xs, ys, sides, where, line, store, pack, copy=False, fresh=False):
        ins = [*xs, *ys, *sides, pack]
        return call(
            functools.partial(cost_kernel, scale, copy, fresh, fresh, where, line),
            "cost",
            ins + store,
            [s_shape] * 2 + [x_shape] * 2 * copy + [shape(pack.shape)] + [lift_shape] * fresh,
            input_output_aliases={len(ins) + i: i for i in range(len(store))},
        )

    if direct:
        store = []
        for k in (0, 2, 1, 3):
            x, ours, sides, where = line[k], [target_feats], [], [here_cols]
            if k == 0:
                sides = [logits_here]
            if k == 3:
                x, *_ = lax.optimization_barrier((x, logits_there, pack))
                s0, s1, pack, lift_there = cost(
                    store[2:],
                    crossed,
                    [logits_there],
                    [there_cols],
                    slice(0, k * rows),
                    store[:2],
                    pack,
                    fresh=True,
                )
                store = [s0, s1, *store[2:]]
                ours, where = [target_feats, *crossed], [here_cols, there_cols]
                sides = [lift, lift_there]
            *store, pack = cost(
                [x, swap(x, 1)],
                ours,
                sides or [lift],
                where,
                slice(k * rows, (k + 1) * rows),
                store,
                pack,
                copy=True,
                fresh=k == 0,
            )
            if k == 0:
                *store, pack, lift = [*store, pack]
                line[2], y, _ = lax.optimization_barrier((line[2], target_feats, pack))
                line.append(swap(line[2], 4))
                ys = [target_feats, swap(y, 1)]
        s0, s1, x0, x1 = store
    else:
        gathered = lax.all_gather(source_feats, AXIS, axis=0)[order].reshape(2, half, width)
        x0, x1 = gathered[0], gathered[1]
        store = []
        for y, logit, where in (
            (target_feats, logits_here, here_cols),
            (crossed[0], logits_there, there_cols),
        ):
            *store, pack, _ = cost(
                [x0, x1], [y], [logit], [where], slice(0, half), store, pack, fresh=True
            )
        s0, s1 = store

    *levels, last = row_levels(count)
    last_masks = (0, *last)
    for level in levels:
        packs = [pack] + [swap(pack, m) for m in level]
        (pack,) = call(
            functools.partial(merge_kernel, (0, *level), blocks),
            "merge",
            packs,
            [shape(pack.shape)],
        )
    packs = [pack] + [swap(pack, m) for m in last]

    flat_shape, lane_shape = shape((1, mine)), shape((1, 2 * cols))
    e_shape = shape((2 * cols, mine))

    e, col, q, h = call(
        functools.partial(first_kernel, last_masks, blocks),
        "first",
        [*packs, s0, s1, source_log],
        [e_shape, shape((2, 2 * cols)), flat_shape, shape((2, mine))],
    )
    col_other = swap(col, 2)
    if direct:
        crossed, _ = lax.optimization_barrier((crossed, pack))
        ys = [ys[0], crossed[0], ys[1], swap(crossed[0], 1)]
        col_other, *ys = lax.optimization_barrier((col_other, *ys))
    row, phi, g = call(
        first_row_kernel,
        "first_row",
        [e, col, col_other, logits],
        [flat_shape, lane_shape, lane_shape],
    )

    def columns(row, *base):
        for level in levels:
            row = row + sum(flip(swap(row, m), m, blocks) for m in level)
        sums = [row] + [swap(row, m) for m in last]
        return call(
            functools.partial(column_kernel, last_masks, blocks),
            "column",
            [*sums, e, h, phi, *base],
            [shape((1 + len(base), 2 * cols))] + [flat_shape] * len(base),
        )

    for _ in range(ITERS - 2):
        (col,) = columns(row)
        (row,) = call(
            row_kernel,
            "row",
            [e, col, swap(col, 2), logits, phi],
            [flat_shape],
        )
    assert mine == 2 * cols
    source_sq = scale * jnp.concatenate(
        [jnp.sum(jnp.square(x.astype(F32)), axis=1) for x in (x0, x1)]
    )
    base = q - source_log + source_sq.reshape(1, mine)
    col, a = columns(row, base)
    col_other = swap(col, 2)
    keep, *sends, mass, logb = call(
        functools.partial(plan_kernel, source_count),
        "plan",
        [e, a, h, col, col_other, logits, phi],
        [shape((2 * cols, half), BF16)]
        + [shape((2 * cols, half // 2), BF16)] * 2
        + [lane_shape, lane_shape],
    )

    def col_send(p, keep):
        piece = slice(cols + parts[p].start, cols + parts[p].stop)
        (out,) = call(
            functools.partial(col_send_kernel, piece),
            "col_send",
            [keep, *sends, x0, x1, mass],
            [shape((parts[p].stop - parts[p].start + TAIL, width), BF16)],
        )
        return out

    out = col_send(0, keep)
    back = [swap(out, 2)]
    if direct:
        others = [None, swap(sends[1], 1)]
        others[0] = swap(sends[0], 1)
        block, block_out = shape((rows + TAIL, width)), shape((rows + TAIL, width), BF16)

        def row_parts(pair, gate):
            plan, other, _ = lax.optimization_barrier((keep, others[pair], gate))
            lanes = slice(2 * pair * rows, 2 * (pair + 1) * rows)
            return call(
                functools.partial(row_part_kernel, lanes),
                "row_part",
                [plan, other, *ys],
                [block, block_out],
            )

        own2, out3 = row_parts(1, out)
        near3 = swap(out3, 4)
        keep_gated, _ = lax.optimization_barrier((keep, out3))
        out = col_send(1, keep_gated)
        back.append(swap(out, 2))
        own0, out1 = row_parts(0, out)
        near1 = swap(out1, 4)
        (out2,) = call(line_kernel, "line", [own2, near3], [block_out])
        far2 = swap(out2, 8)
        ends = [own0, near1, far2, x0]
        gate = out1
    else:
        out = col_send(1, keep)
        back.append(swap(out, 2))
        gate = out
        plan = jnp.concatenate([keep, *sends], axis=1)
        both = jnp.concatenate([target_feats, *crossed], axis=0)
        full = lax.dot_general(
            plan, both, (((0,), (0,)), ((), ())), preferred_element_type=F32
        ).reshape(blocks, rows, width)
        row_mass = jnp.sum(plan.astype(F32), axis=0).reshape(blocks, rows)
        full = jnp.zeros((count, rows, width), F32).at[order].set(full)
        row_mass = jnp.zeros((count, rows), F32).at[order].set(row_mass)
        grad_source = lax.psum_scatter(row_mass, AXIS, scatter_dimension=0)[:, None] * (
            source_feats.astype(F32)
        ) - lax.psum_scatter(full, AXIS, scatter_dimension=0)

    logb, _ = lax.optimization_barrier((logb, gate))
    potential_src, potential_tgt = call(
        functools.partial(potential_kernel, count, scale),
        "potential",
        [here, col, col_other, g, logb, target_feats],
        [shape((1, source_count)), shape((1, cols))],
        scalar=True,
    )
    keep_later, _ = lax.optimization_barrier((keep, potential_tgt))
    (own_col,) = call(
        col_keep_kernel,
        "col_keep",
        [keep_later, *sends, x0, x1],
        [shape((cols, width))],
    )
    factor = target_count / source_count

    def held(p):
        size = parts[p].stop - parts[p].start
        return [pltpu.VMEM((size, width), F32), pltpu.SemaphoreType.DMA((size // 128,))]

    ins = [own_col, back[0], mass, target_feats]
    (grad_target,) = call(
        functools.partial(target_kernel, factor, parts[0]),
        "target",
        ins,
        [shape((cols, width))],
        size=4 * cols * width,
        out_hbm=True,
        scratch_shapes=held(0),
    )
    ins = [own_col, back[1], mass, target_feats, grad_target]
    kw = dict(size=cols * width, in_hbm=(4,), out_hbm=True, input_output_aliases={4: 0})
    if direct:
        grad_target, grad_source = call(
            functools.partial(last_kernel, factor, parts[1]),
            "last",
            ins + ends,
            [shape((cols, width)), shape((rows, width))],
            scratch_shapes=held(1) + [pltpu.VMEM((rows, width), F32), pltpu.SemaphoreType.DMA],
            **kw,
        )
    else:
        (grad_target,) = call(
            lambda *refs: target_kernel(factor, parts[1], *refs[:4], *refs[5:]),
            "target",
            ins,
            [shape((cols, width))],
            scratch_shapes=held(1),
            **kw,
        )

    potential_src = potential_src.reshape(source_count)
    potential_tgt = potential_tgt.reshape(cols)
    return (grad_source, grad_target, potential_src, potential_tgt)


def solution(mesh):
    return jax.shard_map(
        per_device,
        mesh=mesh,
        in_specs=(
            P(("groups", "tgt"), None),
            P(("groups", "tgt"), None),
            P("groups"),
            P(("groups", "tgt")),
        ),
        out_specs=(
            P(("groups", "tgt"), None),
            P(("groups", "tgt"), None),
            P("groups"),
            P(("groups", "tgt")),
        ),
        check_vma=False,
    )
```

```python
import functools
import math

import jax
import jax.numpy as jnp
from jax import lax
from jax.experimental import pallas as pl
from jax.experimental.pallas import tpu as pltpu
from jax.sharding import PartitionSpec as P

ITERS = 3
AXIS = "tgt"
F32 = jnp.float32
BF16 = jnp.bfloat16
TAIL = 8
LOW = -1e30


def call(body, name, ins, outs, size=1, in_hbm=(), out_hbm=False, scalar=False, **kw):
    held, away = pl.BlockSpec(memory_space=pltpu.VMEM), pl.BlockSpec(memory_space=pl.ANY)
    specs = [away if i in in_hbm else held for i in range(len(ins))]
    if scalar:
        specs[0] = pl.BlockSpec(memory_space=pltpu.SMEM)
    return pl.pallas_call(
        body,
        name=name,
        out_shape=outs,
        in_specs=specs,
        out_specs=[away if out_hbm else held] * len(outs),
        compiler_params=pltpu.CompilerParams(vmem_limit_bytes=12 << 20),
        cost_estimate=pl.CostEstimate(flops=1, bytes_accessed=size, transcendentals=0),
        **kw,
    )(*ins)


def tiles(count):
    step = min(count, 128)
    return [slice(i, i + step) for i in range(0, count, step)]


def shape(dims, dtype=F32):
    return jax.ShapeDtypeStruct(dims, dtype)


def swap(value, mask):
    count = lax.axis_size(AXIS)
    return lax.ppermute(value, AXIS, [(i, i ^ mask) for i in range(count)])


def row_levels(count):
    levels, step = [(1,)], 4
    while step < count:
        if step * 4 <= count:
            levels.append((3 * step, 2 * step, step))
            step *= 4
        else:
            levels.append((step,))
            step *= 2
    return levels


def flip(value, mask, blocks):
    move = (mask & 1) * (blocks // 2) + (mask >> 2)
    if not move:
        return value
    width = value.shape[-1] // blocks
    parts = [value[..., (r ^ move) * width : ((r ^ move) + 1) * width] for r in range(blocks)]
    return jnp.concatenate(parts, axis=-1)


def by_index(value, me, blocks):
    width = value.shape[1] // blocks
    bit = 1
    while bit < blocks:
        parts = [value[:, (r ^ bit) * width : ((r ^ bit) + 1) * width] for r in range(blocks)]
        value = jnp.where((me & bit) != 0, jnp.concatenate(parts, axis=1), value)
        bit *= 2
    return value


def prep_kernel(count, me_ref, logit_ref, rel_ref):
    logit = logit_ref[...]
    logit = logit - jnp.log(jnp.sum(jnp.exp(logit), axis=1, keepdims=True))
    value = by_index(logit, me_ref[0, 0], count)
    rows = logit.shape[1] // count
    lines = count // 4
    for c in range(2):
        for k in range(lines):
            here, there = (c * lines + k) * rows, (4 * k + c) * rows
            rel_ref[:, here : here + rows] = value[:, there : there + rows]


def potential_kernel(
    count, scale, me_ref, own_ref, other_ref, g_ref, logb_ref, y_ref, source_ref, target_ref
):
    rows = source_ref.shape[1] // count
    lines = count // 4
    parts = []
    for r in range(count):
        start = ((r & 1) * lines + (r >> 2)) * rows
        ref = other_ref if r & 2 else own_ref
        parts.append(ref[1:2, start : start + rows])
    source_ref[...] = by_index(jnp.concatenate(parts, axis=1), me_ref[0, 0], count)
    cols = target_ref.shape[1]
    wide = y_ref[...].astype(F32)
    square = to_row(jnp.sum(wide * wide, axis=1, keepdims=True))
    target_ref[...] = g_ref[:, :cols] + logb_ref[:, :cols] + scale * square


def diagonal():
    return lax.broadcasted_iota(jnp.int32, (128, 128), 0) == lax.broadcasted_iota(
        jnp.int32, (128, 128), 1
    )


def to_column(row):
    same = diagonal()
    parts = [
        jnp.sum(
            jnp.where(same, jnp.broadcast_to(row[:, i : i + 128], (128, 128)), 0.0),
            axis=1,
            keepdims=True,
        )
        for i in range(0, row.shape[1], 128)
    ]
    return jnp.concatenate(parts, axis=0)


def to_row(column):
    same = diagonal()
    parts = [
        jnp.sum(
            jnp.where(same, jnp.broadcast_to(column[i : i + 128, :], (128, 128)), 0.0),
            axis=0,
            keepdims=True,
        )
        for i in range(0, column.shape[0], 128)
    ]
    return jnp.concatenate(parts, axis=1)


def cost_kernel(scale, copy, fresh, add_mass, cols, line, *refs):
    count = len(cols)
    x_refs, y_refs, side_refs = refs[:2], refs[2 : 2 + count], refs[2 + count : 2 + 2 * count]
    pack_ref = refs[2 + 2 * count]
    outs = refs[-(3 + 2 * copy + fresh) :]
    s_outs, pack_out = outs[:2], outs[2 + 2 * copy]
    half = s_outs[0].shape[1]
    pack_out[...] = pack_ref[...]
    lifts = [side[...] for side in side_refs]
    if fresh:
        logit = lifts[0]
        wide = y_refs[0][...].astype(F32)
        lifts = [to_column(logit) - scale * jnp.sum(wide * wide, axis=1, keepdims=True)]
        outs[-1][...] = lifts[0]
        if add_mass:
            mass = jnp.sum(jnp.exp(logit), axis=1, keepdims=True)
            pack_out[2:3, :] = pack_ref[2:3, :] + mass
    for c in range(2):
        x = x_refs[c][...] if copy else x_refs[c][line, :]
        if copy:
            outs[2 + c][line, :] = x
        lanes = slice(c * half + line.start, c * half + line.stop)
        top, total = pack_ref[0:1, lanes], pack_ref[1:2, lanes]
        for y_ref, lift, here in zip(y_refs, lifts, cols):
            s = (2.0 * scale) * lax.dot_general(
                y_ref[...], x, (((1,), (1,)), ((), ())), preferred_element_type=F32
            )
            s_outs[c][here, line] = s
            s = s + lift
            old, top = top, jnp.maximum(top, jnp.max(s, axis=0, keepdims=True))
            total = total * jnp.exp(old - top) + jnp.sum(jnp.exp(s - top), axis=0, keepdims=True)
        pack_out[0:1, lanes] = top
        pack_out[1:2, lanes] = total


def merge(packs, masks, blocks):
    packs = [flip(p, m, blocks) for p, m in zip(packs, masks)]
    top = functools.reduce(jnp.maximum, [p[0:1] for p in packs])
    total = sum(p[1:2] * jnp.exp(p[0:1] - top) for p in packs)
    return top, total, sum(p[2:3] for p in packs)


def merge_kernel(masks, blocks, *refs):
    top, total, mass = merge([r[...] for r in refs[:-1]], masks, blocks)
    refs[-1][0:1, :] = top
    refs[-1][1:2, :] = total
    refs[-1][2:3, :] = mass


def first_kernel(masks, blocks, *refs):
    pack_refs, refs = refs[: len(masks)], refs[len(masks) :]
    s_refs, refs = refs[:2], refs[2:]
    log_ref, e_ref, col_ref, q_ref, h_ref = refs
    top, total, mass = merge([r[...] for r in pack_refs], masks, blocks)
    h = log_ref[...] + jnp.log(mass)
    h_ref[0:1, :] = h
    h_ref[1:2, :] = mass
    q = h - top - jnp.log(total)
    q_ref[...] = q
    half = s_refs[0].shape[1]
    for t in tiles(e_ref.shape[0]):
        parts = [s_refs[c][t, :] + q[:, c * half : (c + 1) * half] for c in range(2)]
        top = jnp.maximum(*[jnp.max(p, axis=1, keepdims=True) for p in parts])
        total = jnp.zeros_like(top)
        for c in range(2):
            e = jnp.exp(parts[c] - top)
            e_ref[t, c * half : (c + 1) * half] = e
            total = total + jnp.sum(e, axis=1, keepdims=True)
        col_ref[0:1, t] = to_row(top)
        col_ref[1:2, t] = to_row(total)


def turn(value):
    half = value.shape[1] // 2
    return jnp.concatenate([value[:, half:], value[:, :half]], axis=1)


def weighted_rows(e_ref, weight):
    return sum(
        jnp.sum(e_ref[t, :] * to_column(weight[:, t]), axis=0, keepdims=True)
        for t in tiles(e_ref.shape[0])
    )


def first_row_kernel(e_ref, own_ref, other_ref, logit_ref, row_ref, phi_ref, g_ref):
    own, other = own_ref[...], turn(other_ref[...])
    top = jnp.maximum(own[0:1, :], other[0:1, :])
    total = own[1:2, :] * jnp.exp(own[0:1, :] - top) + other[1:2, :] * jnp.exp(other[0:1, :] - top)
    g_ref[...] = -(top + jnp.log(total))
    phi = jnp.exp(own[0:1, :] - top) / total
    phi_ref[...] = phi
    row_ref[...] = weighted_rows(e_ref, jnp.exp(logit_ref[...]) * phi)


def row_kernel(e_ref, own_ref, other_ref, logit_ref, phi_ref, row_ref):
    c = own_ref[...] + turn(other_ref[...])
    row_ref[...] = weighted_rows(e_ref, jnp.exp(logit_ref[...]) * phi_ref[...] / c)


def column_kernel(masks, blocks, *refs):
    sum_refs, refs = refs[: len(masks)], refs[len(masks) :]
    (e_ref, h_ref, phi_ref), rest = refs[:3], refs[3:]
    col_ref = rest[-2] if len(rest) > 1 else rest[0]
    total = sum(flip(r[...], m, blocks) for r, m in zip(sum_refs, masks))
    a = jnp.exp(h_ref[0:1, :]) / total
    for t in tiles(e_ref.shape[0]):
        total = jnp.sum(e_ref[t, :] * a, axis=1, keepdims=True)
        col_ref[0:1, t] = to_row(total) * phi_ref[:, t]
    if len(rest) > 1:
        rest[-1][...] = a
        col_ref[1:2, :] = rest[0][...] + jnp.log(a)


def plan_kernel(source_count, *refs):
    e_ref, a_ref, h_ref, own_ref, other_ref, logit_ref, phi_ref = refs[:7]
    keep_ref, near_ref, far_ref, mass_ref, logb_ref = refs[7:]
    c = own_ref[0:1, :] + turn(other_ref[0:1, :])
    logb_ref[...] = -jnp.log(c)
    mass = jnp.exp(logit_ref[...]) * (source_count / h_ref[1:2, :1])
    mass_ref[...] = mass
    share = mass * phi_ref[...] / c
    half = keep_ref.shape[1]
    split = half + near_ref.shape[1]
    a = a_ref[...]
    for t in tiles(e_ref.shape[0]):
        plan = ((e_ref[t, :] * a) * to_column(share[:, t])).astype(BF16)
        keep_ref[t, :] = plan[:, :half]
        near_ref[t, :] = plan[:, half:split]
        far_ref[t, :] = plan[:, split:]


def split_mass(mass, width):
    mass = jnp.concatenate([mass, jnp.zeros((1, width - mass.shape[1]), F32)], axis=1)
    high = mass.astype(BF16).astype(F32)
    rest = mass - high
    middle = rest.astype(BF16).astype(F32)
    row = lax.broadcasted_iota(jnp.int32, (TAIL, width), 0)
    out = jnp.where(row == 0, high, jnp.where(row == 1, middle, rest - middle))
    return jnp.where(row < 3, out, 0.0).astype(BF16)


def joined_mass(ref, width):
    return jnp.sum(ref[ref.shape[0] - TAIL :, :width].astype(F32), axis=0, keepdims=True)


def row_part_kernel(lanes, count, keep_ref, other_ref, *refs):
    y_refs, out_refs = refs[:-count], refs[-count:]
    group = len(y_refs) // 2
    part = mass = 0.0
    for plan_ref, part_lanes, ys in (
        (keep_ref, lanes, y_refs[:group]),
        (other_ref, slice(None), y_refs[group:]),
    ):
        start = 0
        for y in ys:
            block = plan_ref[start : start + y.shape[0], part_lanes]
            start += y.shape[0]
            part = part + lax.dot_general(
                block, y[...], (((0,), (0,)), ((), ())), preferred_element_type=F32
            )
            mass = mass + jnp.sum(block.astype(F32), axis=0, keepdims=True)
    rows, width = out_refs[0].shape[0] - TAIL, out_refs[0].shape[1]
    for n, ref in enumerate(out_refs):
        here = slice(n * rows, (n + 1) * rows)
        ref[:rows, :] = part[here, :].astype(ref.dtype)
        if ref.dtype == BF16:
            ref[rows:, :] = split_mass(mass[:, here], width)
        else:
            ref[rows:, :rows] = jnp.broadcast_to(mass[:, here], (TAIL, rows))
            ref[rows:, rows:] = jnp.zeros((TAIL, width - rows), F32)


def line_kernel(own_ref, other_ref, out_ref):
    rows, width = out_ref.shape[0] - TAIL, out_ref.shape[1]
    out_ref[:rows, :] = (own_ref[:rows, :] + other_ref[:rows, :].astype(F32)).astype(BF16)
    mass = own_ref[rows : rows + 1, :rows] + joined_mass(other_ref, rows)
    out_ref[rows:, :] = split_mass(mass, width)


def source_kernel(own_ref, near_ref, far_ref, x_ref, out_ref):
    rows = out_ref.shape[0]
    part = own_ref[:rows, :] + near_ref[:rows, :].astype(F32) + far_ref[:rows, :].astype(F32)
    mass = own_ref[rows : rows + 1, :rows] + joined_mass(near_ref, rows)
    mass = mass + joined_mass(far_ref, rows)
    out_ref[...] = to_column(mass) * x_ref[:rows, :].astype(F32) - part


def col_part(keep_ref, near_ref, far_ref, x0_ref, x1_ref, cols):
    near = near_ref.shape[1]
    part = jnp.dot(keep_ref[cols, :], x0_ref[...], preferred_element_type=F32)
    part = part + jnp.dot(near_ref[cols, :], x1_ref[:near, :], preferred_element_type=F32)
    return part + jnp.dot(far_ref[cols, :], x1_ref[near:, :], preferred_element_type=F32)


def col_send_kernel(cols, *refs):
    *refs, out_ref = refs
    out_ref[...] = col_part(*refs, cols).astype(BF16)


def col_keep_kernel(*refs):
    *refs, out_ref = refs
    out_ref[...] = col_part(*refs, slice(0, out_ref.shape[0]))


def target_rows(factor, cols, own_ref, other_ref, mass_ref, y_ref, out_ref, held_ref, sem_ref):
    count = cols.stop - cols.start
    mass = mass_ref[:, cols]
    copies = []
    for n, t in enumerate(slice(i, i + 128) for i in range(0, count, 128)):
        here = slice(cols.start + t.start, cols.start + t.stop)
        part = own_ref[here, :] + other_ref[t, :].astype(F32)
        held_ref[t, :] = factor * (to_column(mass[:, t]) * y_ref[here, :].astype(F32) - part)
        copies.append(pltpu.make_async_copy(held_ref.at[t], out_ref.at[here], sem_ref.at[n]))
        copies[-1].start()
    return copies


def target_kernel(factor, cols, *refs):
    for copy in target_rows(factor, cols, *refs):
        copy.wait()


def last_kernel(factor, cols, *refs):
    target_ins, (_, own_ref, near_ref, far_ref, x_ref), refs = refs[:4], refs[4:9], refs[9:]
    target_out, source_out, held_target, sem_target, held_source, sem_source = refs
    source_kernel(own_ref, near_ref, far_ref, x_ref, held_source)
    first = pltpu.make_async_copy(held_source, source_out, sem_source)
    first.start()
    copies = target_rows(factor, cols, *target_ins, target_out, held_target, sem_target)
    for copy in [first, *copies]:
        copy.wait()


def per_device(source_feats, target_feats, source_logits, target_logits):
    count = lax.axis_size(AXIS)
    me = lax.axis_index(AXIS)
    rows, width = source_feats.shape
    cols = target_feats.shape[0]
    source_count = rows * count
    target_count = cols * count
    scale = 1.0 / math.sqrt(width)
    direct = count == 16
    blocks = count // 2
    lines = blocks // 2
    mine = source_count // 2
    half = mine // 2
    parts = [slice(0, cols * 3 // 4), slice(cols * 3 // 4, cols)]
    masks = [4 * k + c for c in range(2) for k in range(lines)]
    order = jnp.bitwise_xor(me, jnp.array(masks))

    if direct:
        far = swap(source_feats, 8)
        line = [source_feats, swap(source_feats, 4), far]
    crossed = [swap(target_feats, 2)]
    logits_here = target_logits.reshape(1, cols)
    logits_there = swap(logits_here, 2)
    logits = jnp.concatenate([logits_here, logits_there], axis=1)
    here = me.astype(jnp.int32).reshape(1, 1)
    (source_log,) = call(
        functools.partial(prep_kernel, count),
        "prep",
        [here, source_logits.reshape(1, source_count)],
        [shape((1, mine))],
        scalar=True,
    )
    logits_here, source_log = lax.optimization_barrier((logits_here, source_log))
    pack = jnp.concatenate([jnp.full((1, mine), LOW, F32), jnp.zeros((2, mine), F32)])

    s_shape, x_shape = shape((2 * cols, half)), shape((half, width), BF16)
    here_cols, there_cols = slice(0, cols), slice(cols, 2 * cols)
    lift_shape = shape((cols, 1))

    def cost(xs, ys, sides, where, line, store, pack, copy=False, fresh=False):
        ins = [*xs, *ys, *sides, pack]
        return call(
            functools.partial(cost_kernel, scale, copy, fresh, fresh, where, line),
            "cost",
            ins + store,
            [s_shape] * 2 + [x_shape] * 2 * copy + [shape(pack.shape)] + [lift_shape] * fresh,
            input_output_aliases={len(ins) + i: i for i in range(len(store))},
        )

    if direct:
        store = []
        for k in (0, 2, 1, 3):
            x, ours, sides, where = line[k], [target_feats], [], [here_cols]
            if k == 0:
                sides = [logits_here]
            if k == 3:
                x, *_ = lax.optimization_barrier((x, logits_there, pack))
                s0, s1, pack, lift_there = cost(
                    store[2:],
                    crossed,
                    [logits_there],
                    [there_cols],
                    slice(0, k * rows),
                    store[:2],
                    pack,
                    fresh=True,
                )
                store = [s0, s1, *store[2:]]
                ours, where = [target_feats, *crossed], [here_cols, there_cols]
                sides = [lift, lift_there]
            *store, pack = cost(
                [x, swap(x, 1)],
                ours,
                sides or [lift],
                where,
                slice(k * rows, (k + 1) * rows),
                store,
                pack,
                copy=True,
                fresh=k == 0,
            )
            if k == 0:
                *store, pack, lift = [*store, pack]
                line[2], y, _ = lax.optimization_barrier((line[2], target_feats, pack))
                line.append(swap(line[2], 4))
                ys = [target_feats, swap(y, 1)]
        s0, s1, x0, x1 = store
    else:
        gathered = lax.all_gather(source_feats, AXIS, axis=0)[order].reshape(2, half, width)
        x0, x1 = gathered[0], gathered[1]
        store = []
        for y, logit, where in (
            (target_feats, logits_here, here_cols),
            (crossed[0], logits_there, there_cols),
        ):
            *store, pack, _ = cost(
                [x0, x1], [y], [logit], [where], slice(0, half), store, pack, fresh=True
            )
        s0, s1 = store

    *levels, last = row_levels(count)
    last_masks = (0, *last)
    for level in levels:
        packs = [pack] + [swap(pack, m) for m in level]
        (pack,) = call(
            functools.partial(merge_kernel, (0, *level), blocks),
            "merge",
            packs,
            [shape(pack.shape)],
        )
    packs = [pack] + [swap(pack, m) for m in last]

    flat_shape, lane_shape = shape((1, mine)), shape((1, 2 * cols))
    e_shape = shape((2 * cols, mine))

    e, col, q, h = call(
        functools.partial(first_kernel, last_masks, blocks),
        "first",
        [*packs, s0, s1, source_log],
        [e_shape, shape((2, 2 * cols)), flat_shape, shape((2, mine))],
    )
    col_other = swap(col, 2)
    if direct:
        crossed, _ = lax.optimization_barrier((crossed, pack))
        ys = [ys[0], crossed[0], ys[1], swap(crossed[0], 1)]
        col_other, *ys = lax.optimization_barrier((col_other, *ys))
    row, phi, g = call(
        first_row_kernel,
        "first_row",
        [e, col, col_other, logits],
        [flat_shape, lane_shape, lane_shape],
    )

    def columns(row, *base):
        for level in levels:
            row = row + sum(flip(swap(row, m), m, blocks) for m in level)
        sums = [row] + [swap(row, m) for m in last]
        return call(
            functools.partial(column_kernel, last_masks, blocks),
            "column",
            [*sums, e, h, phi, *base],
            [shape((1 + len(base), 2 * cols))] + [flat_shape] * len(base),
        )

    for _ in range(ITERS - 2):
        (col,) = columns(row)
        (row,) = call(
            row_kernel,
            "row",
            [e, col, swap(col, 2), logits, phi],
            [flat_shape],
        )
    assert mine == 2 * cols
    source_sq = scale * jnp.concatenate(
        [jnp.sum(jnp.square(x.astype(F32)), axis=1) for x in (x0, x1)]
    )
    base = q - source_log + source_sq.reshape(1, mine)
    col, a = columns(row, base)
    col_other = swap(col, 2)
    keep, *sends, mass, logb = call(
        functools.partial(plan_kernel, source_count),
        "plan",
        [e, a, h, col, col_other, logits, phi],
        [shape((2 * cols, half), BF16)]
        + [shape((2 * cols, size), BF16) for size in (half * 3 // 4, half // 4)]
        + [lane_shape, lane_shape],
    )

    def col_send(p, keep):
        piece = slice(cols + parts[p].start, cols + parts[p].stop)
        (out,) = call(
            functools.partial(col_send_kernel, piece),
            "col_send",
            [keep, *sends, x0, x1],
            [shape((parts[p].stop - parts[p].start, width), BF16)],
        )
        return out

    out = col_send(0, keep)
    back = [swap(out, 2)]
    if direct:
        others = [None, swap(sends[1], 1)]
        others[0] = swap(sends[0], 1)
        block, block_out = shape((rows + TAIL, width)), shape((rows + TAIL, width), BF16)

        def row_parts(far, gate):
            plan, other, _ = lax.optimization_barrier((keep, others[far], gate))
            outs = [block_out] if far else [block, block_out, block]
            lanes = slice(3 * rows, half) if far else slice(0, 3 * rows)
            return call(
                functools.partial(row_part_kernel, lanes, len(outs)),
                "row_part",
                [plan, other, *ys],
                outs,
            )

        (out3,) = row_parts(True, out)
        near3 = swap(out3, 4)
        keep_gated, _ = lax.optimization_barrier((keep, out3))
        out = col_send(1, keep_gated)
        back.append(swap(out, 2))
        own0, out1, own2 = row_parts(False, out)
        near1 = swap(out1, 4)
        (out2,) = call(line_kernel, "line", [own2, near3], [block_out])
        far2 = swap(out2, 8)
        ends = [own0, near1, far2, x0]
        gate = near1
    else:
        out = col_send(1, keep)
        back.append(swap(out, 2))
        gate = out
        plan = jnp.concatenate([keep, *sends], axis=1)
        both = jnp.concatenate([target_feats, *crossed], axis=0)
        full = lax.dot_general(
            plan, both, (((0,), (0,)), ((), ())), preferred_element_type=F32
        ).reshape(blocks, rows, width)
        row_mass = jnp.sum(plan.astype(F32), axis=0).reshape(blocks, rows)
        full = jnp.zeros((count, rows, width), F32).at[order].set(full)
        row_mass = jnp.zeros((count, rows), F32).at[order].set(row_mass)
        grad_source = lax.psum_scatter(row_mass, AXIS, scatter_dimension=0)[:, None] * (
            source_feats.astype(F32)
        ) - lax.psum_scatter(full, AXIS, scatter_dimension=0)

    logb, _ = lax.optimization_barrier((logb, gate))
    potential_src, potential_tgt = call(
        functools.partial(potential_kernel, count, scale),
        "potential",
        [here, col, col_other, g, logb, target_feats],
        [shape((1, source_count)), shape((1, cols))],
        scalar=True,
    )
    keep_later, _ = lax.optimization_barrier((keep, potential_tgt))
    (own_col,) = call(
        col_keep_kernel,
        "col_keep",
        [keep_later, *sends, x0, x1],
        [shape((cols, width))],
    )
    factor = target_count / source_count

    def held(p):
        size = parts[p].stop - parts[p].start
        return [pltpu.VMEM((size, width), F32), pltpu.SemaphoreType.DMA((size // 128,))]

    ins = [own_col, back[0], mass, target_feats]
    (grad_target,) = call(
        functools.partial(target_kernel, factor, parts[0]),
        "target",
        ins,
        [shape((cols, width))],
        size=4 * cols * width,
        out_hbm=True,
        scratch_shapes=held(0),
    )
    ins = [own_col, back[1], mass, target_feats, grad_target]
    kw = dict(size=cols * width, in_hbm=(4,), out_hbm=True, input_output_aliases={4: 0})
    if direct:
        grad_target, grad_source = call(
            functools.partial(last_kernel, factor, parts[1]),
            "last",
            ins + ends,
            [shape((cols, width)), shape((rows, width))],
            scratch_shapes=held(1) + [pltpu.VMEM((rows, width), F32), pltpu.SemaphoreType.DMA],
            **kw,
        )
    else:
        (grad_target,) = call(
            lambda *refs: target_kernel(factor, parts[1], *refs[:4], *refs[5:]),
            "target",
            ins,
            [shape((cols, width))],
            scratch_shapes=held(1),
            **kw,
        )

    potential_src = potential_src.reshape(source_count)
    potential_tgt = potential_tgt.reshape(cols)
    return (grad_source, grad_target, potential_src, potential_tgt)


def solution(mesh):
    return jax.shard_map(
        per_device,
        mesh=mesh,
        in_specs=(
            P(("groups", "tgt"), None),
            P(("groups", "tgt"), None),
            P("groups"),
            P(("groups", "tgt")),
        ),
        out_specs=(
            P(("groups", "tgt"), None),
            P(("groups", "tgt"), None),
            P("groups"),
            P(("groups", "tgt")),
        ),
        check_vma=False,
    )
```

```python
import functools
import math

import jax
import jax.numpy as jnp
from jax import lax
from jax.experimental import pallas as pl
from jax.experimental.pallas import tpu as pltpu
from jax.sharding import PartitionSpec as P

ITERS = 3
AXIS = "tgt"
F32 = jnp.float32
BF16 = jnp.bfloat16
TAIL = 8
LOW = -1e30


def call(body, name, ins, outs, size=1, in_hbm=(), out_hbm=False, scalar=False, **kw):
    held, away = pl.BlockSpec(memory_space=pltpu.VMEM), pl.BlockSpec(memory_space=pl.ANY)
    specs = [away if i in in_hbm else held for i in range(len(ins))]
    if scalar:
        specs[0] = pl.BlockSpec(memory_space=pltpu.SMEM)
    return pl.pallas_call(
        body,
        name=name,
        out_shape=outs,
        in_specs=specs,
        out_specs=[away if out_hbm else held] * len(outs),
        compiler_params=pltpu.CompilerParams(vmem_limit_bytes=12 << 20),
        cost_estimate=pl.CostEstimate(flops=1, bytes_accessed=size, transcendentals=0),
        **kw,
    )(*ins)


def tiles(count):
    step = min(count, 128)
    return [slice(i, i + step) for i in range(0, count, step)]


def shape(dims, dtype=F32):
    return jax.ShapeDtypeStruct(dims, dtype)


def swap(value, mask):
    count = lax.axis_size(AXIS)
    return lax.ppermute(value, AXIS, [(i, i ^ mask) for i in range(count)])


def row_levels(count):
    levels, step = [(1,)], 4
    while step < count:
        if step * 4 <= count:
            levels.append((3 * step, 2 * step, step))
            step *= 4
        else:
            levels.append((step,))
            step *= 2
    return levels


def flip(value, mask, blocks):
    move = (mask & 1) * (blocks // 2) + (mask >> 2)
    if not move:
        return value
    width = value.shape[-1] // blocks
    parts = [value[..., (r ^ move) * width : ((r ^ move) + 1) * width] for r in range(blocks)]
    return jnp.concatenate(parts, axis=-1)


def by_index(value, me, blocks):
    width = value.shape[1] // blocks
    bit = 1
    while bit < blocks:
        parts = [value[:, (r ^ bit) * width : ((r ^ bit) + 1) * width] for r in range(blocks)]
        value = jnp.where((me & bit) != 0, jnp.concatenate(parts, axis=1), value)
        bit *= 2
    return value


def prep_kernel(count, me_ref, logit_ref, rel_ref):
    logit = logit_ref[...]
    logit = logit - jnp.log(jnp.sum(jnp.exp(logit), axis=1, keepdims=True))
    value = by_index(logit, me_ref[0, 0], count)
    rows = logit.shape[1] // count
    lines = count // 4
    for c in range(2):
        for k in range(lines):
            here, there = (c * lines + k) * rows, (4 * k + c) * rows
            rel_ref[:, here : here + rows] = value[:, there : there + rows]


def potential_kernel(
    count, scale, me_ref, own_ref, other_ref, g_ref, logb_ref, y_ref, source_ref, target_ref
):
    rows = source_ref.shape[1] // count
    lines = count // 4
    parts = []
    for r in range(count):
        start = ((r & 1) * lines + (r >> 2)) * rows
        ref = other_ref if r & 2 else own_ref
        parts.append(ref[1:2, start : start + rows])
    source_ref[...] = by_index(jnp.concatenate(parts, axis=1), me_ref[0, 0], count)
    cols = target_ref.shape[1]
    wide = y_ref[...].astype(F32)
    square = to_row(jnp.sum(wide * wide, axis=1, keepdims=True))
    target_ref[...] = g_ref[:, :cols] + logb_ref[:, :cols] + scale * square


def diagonal():
    return lax.broadcasted_iota(jnp.int32, (128, 128), 0) == lax.broadcasted_iota(
        jnp.int32, (128, 128), 1
    )


def to_column(row):
    same = diagonal()
    parts = [
        jnp.sum(
            jnp.where(same, jnp.broadcast_to(row[:, i : i + 128], (128, 128)), 0.0),
            axis=1,
            keepdims=True,
        )
        for i in range(0, row.shape[1], 128)
    ]
    return jnp.concatenate(parts, axis=0)


def to_row(column):
    same = diagonal()
    parts = [
        jnp.sum(
            jnp.where(same, jnp.broadcast_to(column[i : i + 128, :], (128, 128)), 0.0),
            axis=0,
            keepdims=True,
        )
        for i in range(0, column.shape[0], 128)
    ]
    return jnp.concatenate(parts, axis=1)


def cost_kernel(scale, copy, fresh, add_mass, cols, line, *refs):
    count = len(cols)
    x_refs, y_refs, side_refs = refs[:2], refs[2 : 2 + count], refs[2 + count : 2 + 2 * count]
    pack_ref = refs[2 + 2 * count]
    outs = refs[-(3 + 2 * copy + fresh) :]
    s_outs, pack_out = outs[:2], outs[2 + 2 * copy]
    half = s_outs[0].shape[1]
    pack_out[...] = pack_ref[...]
    lifts = [side[...] for side in side_refs]
    if fresh:
        logit = lifts[0]
        wide = y_refs[0][...].astype(F32)
        lifts = [to_column(logit) - scale * jnp.sum(wide * wide, axis=1, keepdims=True)]
        outs[-1][...] = lifts[0]
        if add_mass:
            mass = jnp.sum(jnp.exp(logit), axis=1, keepdims=True)
            pack_out[2:3, :] = pack_ref[2:3, :] + mass
    for c in range(2):
        x = x_refs[c][...] if copy else x_refs[c][line, :]
        if copy:
            outs[2 + c][line, :] = x
        lanes = slice(c * half + line.start, c * half + line.stop)
        top, total = pack_ref[0:1, lanes], pack_ref[1:2, lanes]
        for y_ref, lift, here in zip(y_refs, lifts, cols):
            s = (2.0 * scale) * lax.dot_general(
                y_ref[...], x, (((1,), (1,)), ((), ())), preferred_element_type=F32
            )
            s_outs[c][here, line] = s
            s = s + lift
            old, top = top, jnp.maximum(top, jnp.max(s, axis=0, keepdims=True))
            total = total * jnp.exp(old - top) + jnp.sum(jnp.exp(s - top), axis=0, keepdims=True)
        pack_out[0:1, lanes] = top
        pack_out[1:2, lanes] = total


def merge(packs, masks, blocks):
    packs = [flip(p, m, blocks) for p, m in zip(packs, masks)]
    top = functools.reduce(jnp.maximum, [p[0:1] for p in packs])
    total = sum(p[1:2] * jnp.exp(p[0:1] - top) for p in packs)
    return top, total, sum(p[2:3] for p in packs)


def merge_kernel(masks, blocks, *refs):
    top, total, mass = merge([r[...] for r in refs[:-1]], masks, blocks)
    refs[-1][0:1, :] = top
    refs[-1][1:2, :] = total
    refs[-1][2:3, :] = mass


def first_kernel(masks, blocks, *refs):
    pack_refs, refs = refs[: len(masks)], refs[len(masks) :]
    s_refs, refs = refs[:2], refs[2:]
    log_ref, e_ref, col_ref, q_ref, h_ref = refs
    top, total, mass = merge([r[...] for r in pack_refs], masks, blocks)
    h = log_ref[...] + jnp.log(mass)
    h_ref[0:1, :] = h
    h_ref[1:2, :] = mass
    q = h - top - jnp.log(total)
    q_ref[...] = q
    half = s_refs[0].shape[1]
    for t in tiles(e_ref.shape[0]):
        parts = [s_refs[c][t, :] + q[:, c * half : (c + 1) * half] for c in range(2)]
        top = jnp.maximum(*[jnp.max(p, axis=1, keepdims=True) for p in parts])
        total = jnp.zeros_like(top)
        for c in range(2):
            e = jnp.exp(parts[c] - top)
            e_ref[t, c * half : (c + 1) * half] = e
            total = total + jnp.sum(e, axis=1, keepdims=True)
        col_ref[0:1, t] = to_row(top)
        col_ref[1:2, t] = to_row(total)


def turn(value):
    half = value.shape[1] // 2
    return jnp.concatenate([value[:, half:], value[:, :half]], axis=1)


def weighted_rows(e_ref, weight):
    return sum(
        jnp.sum(e_ref[t, :] * to_column(weight[:, t]), axis=0, keepdims=True)
        for t in tiles(e_ref.shape[0])
    )


def first_row_kernel(e_ref, own_ref, other_ref, logit_ref, row_ref, phi_ref, g_ref):
    own, other = own_ref[...], turn(other_ref[...])
    top = jnp.maximum(own[0:1, :], other[0:1, :])
    total = own[1:2, :] * jnp.exp(own[0:1, :] - top) + other[1:2, :] * jnp.exp(other[0:1, :] - top)
    g_ref[...] = -(top + jnp.log(total))
    phi = jnp.exp(own[0:1, :] - top) / total
    phi_ref[...] = phi
    row_ref[...] = weighted_rows(e_ref, jnp.exp(logit_ref[...]) * phi)


def row_kernel(e_ref, own_ref, other_ref, logit_ref, phi_ref, row_ref):
    c = own_ref[...] + turn(other_ref[...])
    row_ref[...] = weighted_rows(e_ref, jnp.exp(logit_ref[...]) * phi_ref[...] / c)


def column_kernel(masks, blocks, *refs):
    sum_refs, refs = refs[: len(masks)], refs[len(masks) :]
    (e_ref, h_ref, phi_ref), rest = refs[:3], refs[3:]
    col_ref = rest[-2] if len(rest) > 1 else rest[0]
    total = sum(flip(r[...], m, blocks) for r, m in zip(sum_refs, masks))
    a = jnp.exp(h_ref[0:1, :]) / total
    for t in tiles(e_ref.shape[0]):
        total = jnp.sum(e_ref[t, :] * a, axis=1, keepdims=True)
        col_ref[0:1, t] = to_row(total) * phi_ref[:, t]
    if len(rest) > 1:
        rest[-1][...] = a
        col_ref[1:2, :] = rest[0][...] + jnp.log(a)


def plan_kernel(source_count, *refs):
    e_ref, a_ref, h_ref, own_ref, other_ref, logit_ref, phi_ref = refs[:7]
    keep_ref, near_ref, far_ref, mass_ref, logb_ref = refs[7:]
    c = own_ref[0:1, :] + turn(other_ref[0:1, :])
    logb_ref[...] = -jnp.log(c)
    mass = jnp.exp(logit_ref[...]) * (source_count / h_ref[1:2, :1])
    mass_ref[...] = mass
    share = mass * phi_ref[...] / c
    half = keep_ref.shape[1]
    split = half + near_ref.shape[1]
    a = a_ref[...]
    for t in tiles(e_ref.shape[0]):
        plan = ((e_ref[t, :] * a) * to_column(share[:, t])).astype(BF16)
        keep_ref[t, :] = plan[:, :half]
        near_ref[t, :] = plan[:, half:split]
        far_ref[t, :] = plan[:, split:]


def split_mass(mass, width):
    mass = jnp.concatenate([mass, jnp.zeros((1, width - mass.shape[1]), F32)], axis=1)
    high = mass.astype(BF16).astype(F32)
    rest = mass - high
    middle = rest.astype(BF16).astype(F32)
    row = lax.broadcasted_iota(jnp.int32, (TAIL, width), 0)
    out = jnp.where(row == 0, high, jnp.where(row == 1, middle, rest - middle))
    return jnp.where(row < 3, out, 0.0).astype(BF16)


def joined_mass(ref, width):
    return jnp.sum(ref[ref.shape[0] - TAIL :, :width].astype(F32), axis=0, keepdims=True)


def row_part_kernel(lanes, count, keep_ref, other_ref, *refs):
    y_refs, out_refs = refs[:-count], refs[-count:]
    group = len(y_refs) // 2
    part = mass = 0.0
    for plan_ref, part_lanes, ys in (
        (keep_ref, lanes, y_refs[:group]),
        (other_ref, slice(None), y_refs[group:]),
    ):
        start = 0
        for y in ys:
            block = plan_ref[start : start + y.shape[0], part_lanes]
            start += y.shape[0]
            part = part + lax.dot_general(
                block, y[...], (((0,), (0,)), ((), ())), preferred_element_type=F32
            )
            mass = mass + jnp.sum(block.astype(F32), axis=0, keepdims=True)
    rows, width = out_refs[0].shape[0] - TAIL, out_refs[0].shape[1]
    for n, ref in enumerate(out_refs):
        here = slice(n * rows, (n + 1) * rows)
        ref[:rows, :] = part[here, :].astype(ref.dtype)
        if ref.dtype == BF16:
            ref[rows:, :] = split_mass(mass[:, here], width)
        else:
            ref[rows:, :rows] = jnp.broadcast_to(mass[:, here], (TAIL, rows))
            ref[rows:, rows:] = jnp.zeros((TAIL, width - rows), F32)


def line_kernel(own_ref, other_ref, out_ref):
    rows, width = out_ref.shape[0] - TAIL, out_ref.shape[1]
    out_ref[:rows, :] = (own_ref[:rows, :] + other_ref[:rows, :].astype(F32)).astype(BF16)
    mass = own_ref[rows : rows + 1, :rows] + joined_mass(other_ref, rows)
    out_ref[rows:, :] = split_mass(mass, width)


def source_kernel(own_ref, near_ref, far_ref, x_ref, out_ref):
    rows = out_ref.shape[0]
    part = own_ref[:rows, :] + near_ref[:rows, :].astype(F32) + far_ref[:rows, :].astype(F32)
    mass = own_ref[rows : rows + 1, :rows] + joined_mass(near_ref, rows)
    mass = mass + joined_mass(far_ref, rows)
    out_ref[...] = to_column(mass) * x_ref[:rows, :].astype(F32) - part


def col_part(keep_ref, near_ref, far_ref, x0_ref, x1_ref, cols):
    near = near_ref.shape[1]
    part = jnp.dot(keep_ref[cols, :], x0_ref[...], preferred_element_type=F32)
    part = part + jnp.dot(near_ref[cols, :], x1_ref[:near, :], preferred_element_type=F32)
    return part + jnp.dot(far_ref[cols, :], x1_ref[near:, :], preferred_element_type=F32)


def col_send_kernel(cols, *refs):
    *refs, out_ref = refs
    out_ref[...] = col_part(*refs, cols).astype(BF16)


def col_keep_kernel(*refs):
    *refs, out_ref = refs
    out_ref[...] = col_part(*refs, slice(0, out_ref.shape[0]))


def target_rows(factor, cols, own_ref, other_ref, mass_ref, y_ref, out_ref, held_ref, sem_ref):
    count = cols.stop - cols.start
    mass = mass_ref[:, cols]
    copies = []
    for n, t in enumerate(slice(i, i + 128) for i in range(0, count, 128)):
        here = slice(cols.start + t.start, cols.start + t.stop)
        part = own_ref[here, :] + other_ref[t, :].astype(F32)
        held_ref[t, :] = factor * (to_column(mass[:, t]) * y_ref[here, :].astype(F32) - part)
        copies.append(pltpu.make_async_copy(held_ref.at[t], out_ref.at[here], sem_ref.at[n]))
        copies[-1].start()
    return copies


def target_kernel(factor, cols, *refs):
    for copy in target_rows(factor, cols, *refs):
        copy.wait()


def last_kernel(factor, cols, *refs):
    target_ins, (_, own_ref, near_ref, far_ref, x_ref), refs = refs[:4], refs[4:9], refs[9:]
    target_out, source_out, held_target, sem_target, held_source, sem_source = refs
    source_kernel(own_ref, near_ref, far_ref, x_ref, held_source)
    first = pltpu.make_async_copy(held_source, source_out, sem_source)
    first.start()
    copies = target_rows(factor, cols, *target_ins, target_out, held_target, sem_target)
    for copy in [first, *copies]:
        copy.wait()


def per_device(source_feats, target_feats, source_logits, target_logits):
    count = lax.axis_size(AXIS)
    me = lax.axis_index(AXIS)
    rows, width = source_feats.shape
    cols = target_feats.shape[0]
    source_count = rows * count
    target_count = cols * count
    scale = 1.0 / math.sqrt(width)
    direct = count == 16
    blocks = count // 2
    lines = blocks // 2
    mine = source_count // 2
    half = mine // 2
    parts = [slice(0, cols * 3 // 4), slice(cols * 3 // 4, cols)]
    masks = [4 * k + c for c in range(2) for k in range(lines)]
    order = jnp.bitwise_xor(me, jnp.array(masks))

    if direct:
        far = swap(source_feats, 8)
        line = [source_feats, swap(source_feats, 4), far]
    crossed = [swap(target_feats, 2)]
    logits_here = target_logits.reshape(1, cols)
    logits_there = swap(logits_here, 2)
    logits = jnp.concatenate([logits_here, logits_there], axis=1)
    here = me.astype(jnp.int32).reshape(1, 1)
    (source_log,) = call(
        functools.partial(prep_kernel, count),
        "prep",
        [here, source_logits.reshape(1, source_count)],
        [shape((1, mine))],
        scalar=True,
    )
    logits_here, source_log = lax.optimization_barrier((logits_here, source_log))
    pack = jnp.concatenate([jnp.full((1, mine), LOW, F32), jnp.zeros((2, mine), F32)])

    s_shape, x_shape = shape((2 * cols, half)), shape((half, width), BF16)
    here_cols, there_cols = slice(0, cols), slice(cols, 2 * cols)
    lift_shape = shape((cols, 1))

    def cost(xs, ys, sides, where, line, store, pack, copy=False, fresh=False):
        ins = [*xs, *ys, *sides, pack]
        return call(
            functools.partial(cost_kernel, scale, copy, fresh, fresh, where, line),
            "cost",
            ins + store,
            [s_shape] * 2 + [x_shape] * 2 * copy + [shape(pack.shape)] + [lift_shape] * fresh,
            input_output_aliases={len(ins) + i: i for i in range(len(store))},
        )

    if direct:
        store = []
        for k in (0, 2, 1, 3):
            x, ours, sides, where = line[k], [target_feats], [], [here_cols]
            if k == 0:
                sides = [logits_here]
            if k == 3:
                x, *_ = lax.optimization_barrier((x, logits_there, pack))
                s0, s1, pack, lift_there = cost(
                    store[2:],
                    crossed,
                    [logits_there],
                    [there_cols],
                    slice(0, k * rows),
                    store[:2],
                    pack,
                    fresh=True,
                )
                store = [s0, s1, *store[2:]]
                ours, where = [target_feats, *crossed], [here_cols, there_cols]
                sides = [lift, lift_there]
            *store, pack = cost(
                [x, swap(x, 1)],
                ours,
                sides or [lift],
                where,
                slice(k * rows, (k + 1) * rows),
                store,
                pack,
                copy=True,
                fresh=k == 0,
            )
            if k == 0:
                *store, pack, lift = [*store, pack]
                line[2], y, _ = lax.optimization_barrier((line[2], target_feats, pack))
                line.append(swap(line[2], 4))
                ys = [target_feats, swap(y, 1)]
        s0, s1, x0, x1 = store
    else:
        gathered = lax.all_gather(source_feats, AXIS, axis=0)[order].reshape(2, half, width)
        x0, x1 = gathered[0], gathered[1]
        store = []
        for y, logit, where in (
            (target_feats, logits_here, here_cols),
            (crossed[0], logits_there, there_cols),
        ):
            *store, pack, _ = cost(
                [x0, x1], [y], [logit], [where], slice(0, half), store, pack, fresh=True
            )
        s0, s1 = store

    *levels, last = row_levels(count)
    last_masks = (0, *last)
    for level in levels:
        packs = [pack] + [swap(pack, m) for m in level]
        (pack,) = call(
            functools.partial(merge_kernel, (0, *level), blocks),
            "merge",
            packs,
            [shape(pack.shape)],
        )
    packs = [pack] + [swap(pack, m) for m in last]

    flat_shape, lane_shape = shape((1, mine)), shape((1, 2 * cols))
    e_shape = shape((2 * cols, mine))

    e, col, q, h = call(
        functools.partial(first_kernel, last_masks, blocks),
        "first",
        [*packs, s0, s1, source_log],
        [e_shape, shape((2, 2 * cols)), flat_shape, shape((2, mine))],
    )
    col_other = swap(col, 2)
    if direct:
        crossed, _ = lax.optimization_barrier((crossed, h))
        ys = [ys[0], crossed[0], ys[1], swap(crossed[0], 1)]
    row, phi, g = call(
        first_row_kernel,
        "first_row",
        [e, col, col_other, logits],
        [flat_shape, lane_shape, lane_shape],
    )

    if direct:
        row, *ys = lax.optimization_barrier((row, *ys))

    def columns(row, *base):
        for level in levels:
            row = row + sum(flip(swap(row, m), m, blocks) for m in level)
        sums = [row] + [swap(row, m) for m in last]
        return call(
            functools.partial(column_kernel, last_masks, blocks),
            "column",
            [*sums, e, h, phi, *base],
            [shape((1 + len(base), 2 * cols))] + [flat_shape] * len(base),
        )

    for _ in range(ITERS - 2):
        (col,) = columns(row)
        (row,) = call(
            row_kernel,
            "row",
            [e, col, swap(col, 2), logits, phi],
            [flat_shape],
        )
    assert mine == 2 * cols
    source_sq = scale * jnp.concatenate(
        [jnp.sum(jnp.square(x.astype(F32)), axis=1) for x in (x0, x1)]
    )
    base = q - source_log + source_sq.reshape(1, mine)
    col, a = columns(row, base)
    col_other = swap(col, 2)
    keep, *sends, mass, logb = call(
        functools.partial(plan_kernel, source_count),
        "plan",
        [e, a, h, col, col_other, logits, phi],
        [shape((2 * cols, half), BF16)]
        + [shape((2 * cols, size), BF16) for size in (half * 3 // 4, half // 4)]
        + [lane_shape, lane_shape],
    )

    def col_send(p, keep):
        piece = slice(cols + parts[p].start, cols + parts[p].stop)
        (out,) = call(
            functools.partial(col_send_kernel, piece),
            "col_send",
            [keep, *sends, x0, x1],
            [shape((parts[p].stop - parts[p].start, width), BF16)],
        )
        return out

    out = col_send(0, keep)
    back = [swap(out, 2)]
    if direct:
        others = [None, swap(sends[1], 1)]
        others[0] = swap(sends[0], 1)
        block, block_out = shape((rows + TAIL, width)), shape((rows + TAIL, width), BF16)

        def row_parts(far, gate):
            plan, other, _ = lax.optimization_barrier((keep, others[far], gate))
            outs = [block_out] if far else [block, block_out, block]
            lanes = slice(3 * rows, half) if far else slice(0, 3 * rows)
            return call(
                functools.partial(row_part_kernel, lanes, len(outs)),
                "row_part",
                [plan, other, *ys],
                outs,
            )

        (out3,) = row_parts(True, out)
        near3 = swap(out3, 4)
        keep_gated, _ = lax.optimization_barrier((keep, out3))
        out = col_send(1, keep_gated)
        back.append(swap(out, 2))
        own0, out1, own2 = row_parts(False, out)
        near1 = swap(out1, 4)
        (out2,) = call(line_kernel, "line", [own2, near3], [block_out])
        far2 = swap(out2, 8)
        ends = [own0, near1, far2, x0]
        gate = near1
    else:
        out = col_send(1, keep)
        back.append(swap(out, 2))
        gate = out
        plan = jnp.concatenate([keep, *sends], axis=1)
        both = jnp.concatenate([target_feats, *crossed], axis=0)
        full = lax.dot_general(
            plan, both, (((0,), (0,)), ((), ())), preferred_element_type=F32
        ).reshape(blocks, rows, width)
        row_mass = jnp.sum(plan.astype(F32), axis=0).reshape(blocks, rows)
        full = jnp.zeros((count, rows, width), F32).at[order].set(full)
        row_mass = jnp.zeros((count, rows), F32).at[order].set(row_mass)
        grad_source = lax.psum_scatter(row_mass, AXIS, scatter_dimension=0)[:, None] * (
            source_feats.astype(F32)
        ) - lax.psum_scatter(full, AXIS, scatter_dimension=0)

    logb, _ = lax.optimization_barrier((logb, gate))
    potential_src, potential_tgt = call(
        functools.partial(potential_kernel, count, scale),
        "potential",
        [here, col, col_other, g, logb, target_feats],
        [shape((1, source_count)), shape((1, cols))],
        scalar=True,
    )
    keep_later, _ = lax.optimization_barrier((keep, potential_tgt))
    (own_col,) = call(
        col_keep_kernel,
        "col_keep",
        [keep_later, *sends, x0, x1],
        [shape((cols, width))],
    )
    factor = target_count / source_count

    def held(p):
        size = parts[p].stop - parts[p].start
        return [pltpu.VMEM((size, width), F32), pltpu.SemaphoreType.DMA((size // 128,))]

    ins = [own_col, back[0], mass, target_feats]
    (grad_target,) = call(
        functools.partial(target_kernel, factor, parts[0]),
        "target",
        ins,
        [shape((cols, width))],
        size=4 * cols * width,
        out_hbm=True,
        scratch_shapes=held(0),
    )
    ins = [own_col, back[1], mass, target_feats, grad_target]
    kw = dict(size=cols * width, in_hbm=(4,), out_hbm=True, input_output_aliases={4: 0})
    if direct:
        grad_target, grad_source = call(
            functools.partial(last_kernel, factor, parts[1]),
            "last",
            ins + ends,
            [shape((cols, width)), shape((rows, width))],
            scratch_shapes=held(1) + [pltpu.VMEM((rows, width), F32), pltpu.SemaphoreType.DMA],
            **kw,
        )
    else:
        (grad_target,) = call(
            lambda *refs: target_kernel(factor, parts[1], *refs[:4], *refs[5:]),
            "target",
            ins,
            [shape((cols, width))],
            scratch_shapes=held(1),
            **kw,
        )

    potential_src = potential_src.reshape(source_count)
    potential_tgt = potential_tgt.reshape(cols)
    return (grad_source, grad_target, potential_src, potential_tgt)


def solution(mesh):
    return jax.shard_map(
        per_device,
        mesh=mesh,
        in_specs=(
            P(("groups", "tgt"), None),
            P(("groups", "tgt"), None),
            P("groups"),
            P(("groups", "tgt")),
        ),
        out_specs=(
            P(("groups", "tgt"), None),
            P(("groups", "tgt"), None),
            P("groups"),
            P(("groups", "tgt")),
        ),
        check_vma=False,
    )
```

```python
import functools
import math

import jax
import jax.numpy as jnp
from jax import lax
from jax.experimental import pallas as pl
from jax.experimental.pallas import tpu as pltpu
from jax.sharding import PartitionSpec as P

ITERS = 3
AXIS = "tgt"
F32 = jnp.float32
BF16 = jnp.bfloat16
TAIL = 8
LOW = -1e30


def call(body, name, ins, outs, size=1, in_hbm=(), out_hbm=False, scalar=False, **kw):
    held, away = pl.BlockSpec(memory_space=pltpu.VMEM), pl.BlockSpec(memory_space=pl.ANY)
    specs = [away if i in in_hbm else held for i in range(len(ins))]
    if scalar:
        specs[0] = pl.BlockSpec(memory_space=pltpu.SMEM)
    return pl.pallas_call(
        body,
        name=name,
        out_shape=outs,
        in_specs=specs,
        out_specs=[away if out_hbm else held] * len(outs),
        compiler_params=pltpu.CompilerParams(vmem_limit_bytes=12 << 20),
        cost_estimate=pl.CostEstimate(flops=1, bytes_accessed=size, transcendentals=0),
        **kw,
    )(*ins)


def tiles(count):
    step = min(count, 128)
    return [slice(i, i + step) for i in range(0, count, step)]


def shape(dims, dtype=F32):
    return jax.ShapeDtypeStruct(dims, dtype)


def swap(value, mask):
    count = lax.axis_size(AXIS)
    return lax.ppermute(value, AXIS, [(i, i ^ mask) for i in range(count)])


def row_levels(count):
    levels, step = [(1,)], 4
    while step < count:
        if step * 4 <= count:
            levels.append((3 * step, 2 * step, step))
            step *= 4
        else:
            levels.append((step,))
            step *= 2
    return levels


def flip(value, mask, blocks):
    move = (mask & 1) * (blocks // 2) + (mask >> 2)
    if not move:
        return value
    width = value.shape[-1] // blocks
    parts = [value[..., (r ^ move) * width : ((r ^ move) + 1) * width] for r in range(blocks)]
    return jnp.concatenate(parts, axis=-1)


def by_index(value, me, blocks):
    width = value.shape[1] // blocks
    bit = 1
    while bit < blocks:
        parts = [value[:, (r ^ bit) * width : ((r ^ bit) + 1) * width] for r in range(blocks)]
        value = jnp.where((me & bit) != 0, jnp.concatenate(parts, axis=1), value)
        bit *= 2
    return value


def prep_kernel(count, me_ref, logit_ref, rel_ref):
    logit = logit_ref[...]
    logit = logit - jnp.log(jnp.sum(jnp.exp(logit), axis=1, keepdims=True))
    value = by_index(logit, me_ref[0, 0], count)
    rows = logit.shape[1] // count
    lines = count // 4
    for c in range(2):
        for k in range(lines):
            here, there = (c * lines + k) * rows, (4 * k + c) * rows
            rel_ref[:, here : here + rows] = value[:, there : there + rows]


def potential_kernel(
    count, scale, me_ref, own_ref, other_ref, g_ref, last_ref, y_ref, source_ref, target_ref
):
    rows = source_ref.shape[1] // count
    lines = count // 4
    parts = []
    for r in range(count):
        start = ((r & 1) * lines + (r >> 2)) * rows
        ref = other_ref if r & 2 else own_ref
        parts.append(ref[1:2, start : start + rows])
    source_ref[...] = by_index(jnp.concatenate(parts, axis=1), me_ref[0, 0], count)
    cols = target_ref.shape[1]
    wide = y_ref[...].astype(F32)
    square = to_row(jnp.sum(wide * wide, axis=1, keepdims=True))
    target_ref[...] = g_ref[:, :cols] + jnp.log(last_ref[:, :cols]) + scale * square


def diagonal():
    return lax.broadcasted_iota(jnp.int32, (128, 128), 0) == lax.broadcasted_iota(
        jnp.int32, (128, 128), 1
    )


def to_column(row):
    same = diagonal()
    parts = [
        jnp.sum(
            jnp.where(same, jnp.broadcast_to(row[:, i : i + 128], (128, 128)), 0.0),
            axis=1,
            keepdims=True,
        )
        for i in range(0, row.shape[1], 128)
    ]
    return jnp.concatenate(parts, axis=0)


def to_row(column):
    same = diagonal()
    parts = [
        jnp.sum(
            jnp.where(same, jnp.broadcast_to(column[i : i + 128, :], (128, 128)), 0.0),
            axis=0,
            keepdims=True,
        )
        for i in range(0, column.shape[0], 128)
    ]
    return jnp.concatenate(parts, axis=1)


def cost_kernel(scale, copy, fresh, add_mass, cols, line, *refs):
    count = len(cols)
    x_refs, y_refs, side_refs = refs[:2], refs[2 : 2 + count], refs[2 + count : 2 + 2 * count]
    pack_ref = refs[2 + 2 * count]
    outs = refs[-(3 + 2 * copy + fresh) :]
    s_outs, pack_out = outs[:2], outs[2 + 2 * copy]
    half = s_outs[0].shape[1]
    pack_out[...] = pack_ref[...]
    lifts = [side[...] for side in side_refs]
    if fresh:
        logit = lifts[0]
        wide = y_refs[0][...].astype(F32)
        lifts = [to_column(logit) - scale * jnp.sum(wide * wide, axis=1, keepdims=True)]
        outs[-1][...] = lifts[0]
        if add_mass:
            mass = jnp.sum(jnp.exp(logit), axis=1, keepdims=True)
            pack_out[2:3, :] = pack_ref[2:3, :] + mass
    for c in range(2):
        x = x_refs[c][...] if copy else x_refs[c][line, :]
        if copy:
            outs[2 + c][line, :] = x
        lanes = slice(c * half + line.start, c * half + line.stop)
        top, total = pack_ref[0:1, lanes], pack_ref[1:2, lanes]
        for y_ref, lift, here in zip(y_refs, lifts, cols):
            s = (2.0 * scale) * lax.dot_general(
                y_ref[...], x, (((1,), (1,)), ((), ())), preferred_element_type=F32
            )
            s_outs[c][here, line] = s
            s = s + lift
            old, top = top, jnp.maximum(top, jnp.max(s, axis=0, keepdims=True))
            total = total * jnp.exp(old - top) + jnp.sum(jnp.exp(s - top), axis=0, keepdims=True)
        pack_out[0:1, lanes] = top
        pack_out[1:2, lanes] = total


def merge(packs, masks, blocks):
    packs = [flip(p, m, blocks) for p, m in zip(packs, masks)]
    top = functools.reduce(jnp.maximum, [p[0:1] for p in packs])
    total = sum(p[1:2] * jnp.exp(p[0:1] - top) for p in packs)
    return top, total, sum(p[2:3] for p in packs)


def merge_kernel(masks, blocks, *refs):
    top, total, mass = merge([r[...] for r in refs[:-1]], masks, blocks)
    refs[-1][0:1, :] = top
    refs[-1][1:2, :] = total
    refs[-1][2:3, :] = mass


def first_kernel(masks, blocks, *refs):
    pack_refs, refs = refs[: len(masks)], refs[len(masks) :]
    s_refs, refs = refs[:2], refs[2:]
    log_ref, e_ref, col_ref, q_ref, h_ref = refs
    top, total, mass = merge([r[...] for r in pack_refs], masks, blocks)
    h = log_ref[...] + jnp.log(mass)
    h_ref[0:1, :] = h
    h_ref[1:2, :] = mass
    q = h - top - jnp.log(total)
    q_ref[...] = q
    half = s_refs[0].shape[1]
    for t in tiles(e_ref.shape[0]):
        parts = [s_refs[c][t, :] + q[:, c * half : (c + 1) * half] for c in range(2)]
        top = jnp.maximum(*[jnp.max(p, axis=1, keepdims=True) for p in parts])
        total = jnp.zeros_like(top)
        for c in range(2):
            e = jnp.exp(parts[c] - top)
            e_ref[t, c * half : (c + 1) * half] = e
            total = total + jnp.sum(e, axis=1, keepdims=True)
        col_ref[0:1, t] = to_row(top)
        col_ref[1:2, t] = to_row(total)


def turn(value):
    half = value.shape[1] // 2
    return jnp.concatenate([value[:, half:], value[:, :half]], axis=1)


def weighted_rows(e_ref, weight):
    return sum(
        jnp.sum(e_ref[t, :] * to_column(weight[:, t]), axis=0, keepdims=True)
        for t in tiles(e_ref.shape[0])
    )


def first_row_kernel(e_ref, own_ref, other_ref, logit_ref, row_ref, phi_ref, g_ref):
    own, other = own_ref[...], turn(other_ref[...])
    top = jnp.maximum(own[0:1, :], other[0:1, :])
    total = own[1:2, :] * jnp.exp(own[0:1, :] - top) + other[1:2, :] * jnp.exp(other[0:1, :] - top)
    g_ref[...] = -(top + jnp.log(total))
    phi = jnp.exp(own[0:1, :] - top) / total
    phi_ref[...] = phi
    row_ref[...] = weighted_rows(e_ref, jnp.exp(logit_ref[...]) * phi)


def row_kernel(e_ref, own_ref, other_ref, logit_ref, phi_ref, row_ref):
    c = own_ref[...] + turn(other_ref[...])
    row_ref[...] = weighted_rows(e_ref, jnp.exp(logit_ref[...]) * phi_ref[...] / c)


def column_kernel(masks, blocks, *refs):
    sum_refs, refs = refs[: len(masks)], refs[len(masks) :]
    (e_ref, h_ref, phi_ref), rest = refs[:3], refs[3:]
    col_ref = rest[-2] if len(rest) > 1 else rest[0]
    total = sum(flip(r[...], m, blocks) for r, m in zip(sum_refs, masks))
    a = jnp.exp(h_ref[0:1, :]) / total
    for t in tiles(e_ref.shape[0]):
        total = jnp.sum(e_ref[t, :] * a, axis=1, keepdims=True)
        col_ref[0:1, t] = to_row(total) * phi_ref[:, t]
    if len(rest) > 1:
        rest[-1][...] = a
        col_ref[1:2, :] = rest[0][...] + jnp.log(a)


def store_plan(e_ref, a, share, outs):
    for t in tiles(e_ref.shape[0]):
        plan = ((e_ref[t, :] * a) * to_column(share[:, t])).astype(BF16)
        start = 0
        for ref in outs:
            ref[t, :] = plan[:, start : start + ref.shape[1]]
            start += ref.shape[1]


def early_plan_kernel(source_count, e_ref, a_ref, h_ref, logit_ref, phi_ref, *outs):
    *outs, mass_ref = outs
    mass = jnp.exp(logit_ref[...]) * (source_count / h_ref[1:2, :1])
    mass_ref[...] = mass
    store_plan(e_ref, a_ref[...], mass * phi_ref[...], outs)


def plan_kernel(e_ref, a_ref, mass_ref, own_ref, other_ref, phi_ref, *outs):
    *outs, last_ref = outs
    last = 1.0 / (own_ref[0:1, :] + turn(other_ref[0:1, :]))
    last_ref[...] = last
    store_plan(e_ref, a_ref[...], mass_ref[...] * phi_ref[...] * last, outs)


def split_mass(mass, width):
    mass = jnp.concatenate([mass, jnp.zeros((1, width - mass.shape[1]), F32)], axis=1)
    high = mass.astype(BF16).astype(F32)
    rest = mass - high
    middle = rest.astype(BF16).astype(F32)
    row = lax.broadcasted_iota(jnp.int32, (TAIL, width), 0)
    out = jnp.where(row == 0, high, jnp.where(row == 1, middle, rest - middle))
    return jnp.where(row < 3, out, 0.0).astype(BF16)


def joined_mass(ref, width):
    return jnp.sum(ref[ref.shape[0] - TAIL :, :width].astype(F32), axis=0, keepdims=True)


def row_part_kernel(lanes, count, keep_ref, other_ref, *refs):
    y_refs, out_refs = refs[:-count], refs[-count:]
    group = len(y_refs) // 2
    part = mass = 0.0
    for plan_ref, part_lanes, ys in (
        (keep_ref, lanes, y_refs[:group]),
        (other_ref, slice(None), y_refs[group:]),
    ):
        start = 0
        for y in ys:
            block = plan_ref[start : start + y.shape[0], part_lanes]
            start += y.shape[0]
            part = part + lax.dot_general(
                block, y[...], (((0,), (0,)), ((), ())), preferred_element_type=F32
            )
            mass = mass + jnp.sum(block.astype(F32), axis=0, keepdims=True)
    rows, width = out_refs[0].shape[0] - TAIL, out_refs[0].shape[1]
    for n, ref in enumerate(out_refs):
        here = slice(n * rows, (n + 1) * rows)
        ref[:rows, :] = part[here, :].astype(ref.dtype)
        if ref.dtype == BF16:
            ref[rows:, :] = split_mass(mass[:, here], width)
        else:
            ref[rows:, :rows] = jnp.broadcast_to(mass[:, here], (TAIL, rows))
            ref[rows:, rows:] = jnp.zeros((TAIL, width - rows), F32)


def line_kernel(own_ref, other_ref, out_ref):
    rows, width = out_ref.shape[0] - TAIL, out_ref.shape[1]
    out_ref[:rows, :] = (own_ref[:rows, :] + other_ref[:rows, :].astype(F32)).astype(BF16)
    mass = own_ref[rows : rows + 1, :rows] + joined_mass(other_ref, rows)
    out_ref[rows:, :] = split_mass(mass, width)


def source_kernel(own_ref, near_ref, far_ref, x_ref, out_ref):
    rows = out_ref.shape[0]
    part = own_ref[:rows, :] + near_ref[:rows, :].astype(F32) + far_ref[:rows, :].astype(F32)
    mass = own_ref[rows : rows + 1, :rows] + joined_mass(near_ref, rows)
    mass = mass + joined_mass(far_ref, rows)
    out_ref[...] = to_column(mass) * x_ref[:rows, :].astype(F32) - part


def col_part(keep_ref, near_ref, far_ref, x0_ref, x1_ref, cols):
    near = near_ref.shape[1]
    part = jnp.dot(keep_ref[cols, :], x0_ref[...], preferred_element_type=F32)
    part = part + jnp.dot(near_ref[cols, :], x1_ref[:near, :], preferred_element_type=F32)
    return part + jnp.dot(far_ref[cols, :], x1_ref[near:, :], preferred_element_type=F32)


def col_send_kernel(cols, *refs):
    *refs, out_ref = refs
    out_ref[...] = col_part(*refs, cols).astype(BF16)


def col_keep_kernel(*refs):
    *refs, out_ref = refs
    out_ref[...] = col_part(*refs, slice(0, out_ref.shape[0]))


def target_rows(
    factor, cols, own_ref, other_ref, mass_ref, last_ref, y_ref, out_ref, held_ref, sem_ref
):
    count = cols.stop - cols.start
    mass, last = mass_ref[:, cols], last_ref[:, cols]
    copies = []
    for n, t in enumerate(slice(i, i + 128) for i in range(0, count, 128)):
        here = slice(cols.start + t.start, cols.start + t.stop)
        part = own_ref[here, :] + other_ref[t, :].astype(F32)
        part = to_column(last[:, t]) * part
        held_ref[t, :] = factor * (to_column(mass[:, t]) * y_ref[here, :].astype(F32) - part)
        copies.append(pltpu.make_async_copy(held_ref.at[t], out_ref.at[here], sem_ref.at[n]))
        copies[-1].start()
    return copies


def target_kernel(factor, cols, *refs):
    for copy in target_rows(factor, cols, *refs):
        copy.wait()


def last_kernel(factor, cols, *refs):
    target_ins, (_, own_ref, near_ref, far_ref, x_ref), refs = refs[:5], refs[5:10], refs[10:]
    target_out, source_out, held_target, sem_target, held_source, sem_source = refs
    source_kernel(own_ref, near_ref, far_ref, x_ref, held_source)
    first = pltpu.make_async_copy(held_source, source_out, sem_source)
    first.start()
    copies = target_rows(factor, cols, *target_ins, target_out, held_target, sem_target)
    for copy in [first, *copies]:
        copy.wait()


def per_device(source_feats, target_feats, source_logits, target_logits):
    count = lax.axis_size(AXIS)
    me = lax.axis_index(AXIS)
    rows, width = source_feats.shape
    cols = target_feats.shape[0]
    source_count = rows * count
    target_count = cols * count
    scale = 1.0 / math.sqrt(width)
    direct = count == 16
    blocks = count // 2
    lines = blocks // 2
    mine = source_count // 2
    half = mine // 2
    parts = [slice(0, cols * 3 // 4), slice(cols * 3 // 4, cols)]
    masks = [4 * k + c for c in range(2) for k in range(lines)]
    order = jnp.bitwise_xor(me, jnp.array(masks))

    if direct:
        far = swap(source_feats, 8)
        line = [source_feats, swap(source_feats, 4), far]
    crossed = [swap(target_feats, 2)]
    logits_here = target_logits.reshape(1, cols)
    logits_there = swap(logits_here, 2)
    logits = jnp.concatenate([logits_here, logits_there], axis=1)
    here = me.astype(jnp.int32).reshape(1, 1)
    (source_log,) = call(
        functools.partial(prep_kernel, count),
        "prep",
        [here, source_logits.reshape(1, source_count)],
        [shape((1, mine))],
        scalar=True,
    )
    logits_here, source_log = lax.optimization_barrier((logits_here, source_log))
    pack = jnp.concatenate([jnp.full((1, mine), LOW, F32), jnp.zeros((2, mine), F32)])

    s_shape, x_shape = shape((2 * cols, half)), shape((half, width), BF16)
    here_cols, there_cols = slice(0, cols), slice(cols, 2 * cols)
    lift_shape = shape((cols, 1))

    def cost(xs, ys, sides, where, line, store, pack, copy=False, fresh=False):
        ins = [*xs, *ys, *sides, pack]
        return call(
            functools.partial(cost_kernel, scale, copy, fresh, fresh, where, line),
            "cost",
            ins + store,
            [s_shape] * 2 + [x_shape] * 2 * copy + [shape(pack.shape)] + [lift_shape] * fresh,
            input_output_aliases={len(ins) + i: i for i in range(len(store))},
        )

    if direct:
        store = []
        for k in (0, 2, 1, 3):
            x, ours, sides, where = line[k], [target_feats], [], [here_cols]
            if k == 0:
                sides = [logits_here]
            if k == 3:
                x, *_ = lax.optimization_barrier((x, logits_there, pack))
                s0, s1, pack, lift_there = cost(
                    store[2:],
                    crossed,
                    [logits_there],
                    [there_cols],
                    slice(0, k * rows),
                    store[:2],
                    pack,
                    fresh=True,
                )
                store = [s0, s1, *store[2:]]
                ours, where = [target_feats, *crossed], [here_cols, there_cols]
                sides = [lift, lift_there]
            *store, pack = cost(
                [x, swap(x, 1)],
                ours,
                sides or [lift],
                where,
                slice(k * rows, (k + 1) * rows),
                store,
                pack,
                copy=True,
                fresh=k == 0,
            )
            if k == 0:
                *store, pack, lift = [*store, pack]
                line[2], y, _ = lax.optimization_barrier((line[2], target_feats, pack))
                line.append(swap(line[2], 4))
                ys = [target_feats, swap(y, 1)]
        s0, s1, x0, x1 = store
    else:
        gathered = lax.all_gather(source_feats, AXIS, axis=0)[order].reshape(2, half, width)
        x0, x1 = gathered[0], gathered[1]
        store = []
        for y, logit, where in (
            (target_feats, logits_here, here_cols),
            (crossed[0], logits_there, there_cols),
        ):
            *store, pack, _ = cost(
                [x0, x1], [y], [logit], [where], slice(0, half), store, pack, fresh=True
            )
        s0, s1 = store

    *levels, last = row_levels(count)
    last_masks = (0, *last)
    for level in levels:
        packs = [pack] + [swap(pack, m) for m in level]
        (pack,) = call(
            functools.partial(merge_kernel, (0, *level), blocks),
            "merge",
            packs,
            [shape(pack.shape)],
        )
    packs = [pack] + [swap(pack, m) for m in last]

    flat_shape, lane_shape = shape((1, mine)), shape((1, 2 * cols))
    e_shape = shape((2 * cols, mine))

    e, col, q, h = call(
        functools.partial(first_kernel, last_masks, blocks),
        "first",
        [*packs, s0, s1, source_log],
        [e_shape, shape((2, 2 * cols)), flat_shape, shape((2, mine))],
    )
    col_other = swap(col, 2)
    if direct:
        crossed, _ = lax.optimization_barrier((crossed, h))
        ys = [ys[0], crossed[0], ys[1], swap(crossed[0], 1)]
    row, phi, g = call(
        first_row_kernel,
        "first_row",
        [e, col, col_other, logits],
        [flat_shape, lane_shape, lane_shape],
    )

    if direct:
        row, *ys = lax.optimization_barrier((row, *ys))

    def columns(row, *base):
        for level in levels:
            row = row + sum(flip(swap(row, m), m, blocks) for m in level)
        sums = [row] + [swap(row, m) for m in last]
        return call(
            functools.partial(column_kernel, last_masks, blocks),
            "column",
            [*sums, e, h, phi, *base],
            [shape((1 + len(base), 2 * cols))] + [flat_shape] * len(base),
        )

    for _ in range(ITERS - 2):
        (col,) = columns(row)
        (row,) = call(
            row_kernel,
            "row",
            [e, col, swap(col, 2), logits, phi],
            [flat_shape],
        )
    assert mine == 2 * cols
    source_sq = scale * jnp.concatenate(
        [jnp.sum(jnp.square(x.astype(F32)), axis=1) for x in (x0, x1)]
    )
    base = q - source_log + source_sq.reshape(1, mine)
    col, a = columns(row, base)
    col_other = swap(col, 2)
    plan_shapes = [shape((2 * cols, n), BF16) for n in (half, half * 3 // 4, half // 4)]
    *early, mass = call(
        functools.partial(early_plan_kernel, source_count),
        "early_plan",
        [e, a, h, logits, phi],
        plan_shapes + [lane_shape],
    )

    def col_send(p, first):
        piece = slice(cols + parts[p].start, cols + parts[p].stop)
        (out,) = call(
            functools.partial(col_send_kernel, piece),
            "col_send",
            [first, *early[1:], x0, x1],
            [shape((parts[p].stop - parts[p].start, width), BF16)],
        )
        return out

    out = col_send(0, early[0])
    back = [swap(out, 2)]
    col_last, _ = lax.optimization_barrier((col_other, out))
    keep, *sends, final = call(
        plan_kernel,
        "plan",
        [e, a, mass, col, col_last, phi],
        plan_shapes + [lane_shape],
    )
    if direct:
        others = [None, swap(sends[1], 1)]
        others[0] = swap(sends[0], 1)
        block, block_out = shape((rows + TAIL, width)), shape((rows + TAIL, width), BF16)

        def row_parts(far, gate):
            plan, other, _ = lax.optimization_barrier((keep, others[far], gate))
            outs = [block_out] if far else [block, block_out, block]
            lanes = slice(3 * rows, half) if far else slice(0, 3 * rows)
            return call(
                functools.partial(row_part_kernel, lanes, len(outs)),
                "row_part",
                [plan, other, *ys],
                outs,
            )

        (out3,) = row_parts(True, keep)
        near3 = swap(out3, 4)
        first, _ = lax.optimization_barrier((early[0], out3))
        out = col_send(1, first)
        back.append(swap(out, 2))
        own0, out1, own2 = row_parts(False, out)
        near1 = swap(out1, 4)
        (out2,) = call(line_kernel, "line", [own2, near3], [block_out])
        far2 = swap(out2, 8)
        ends = [own0, near1, far2, x0]
        gate = near1
    else:
        out = col_send(1, early[0])
        back.append(swap(out, 2))
        gate = out
        plan = jnp.concatenate([keep, *sends], axis=1)
        both = jnp.concatenate([target_feats, *crossed], axis=0)
        full = lax.dot_general(
            plan, both, (((0,), (0,)), ((), ())), preferred_element_type=F32
        ).reshape(blocks, rows, width)
        row_mass = jnp.sum(plan.astype(F32), axis=0).reshape(blocks, rows)
        full = jnp.zeros((count, rows, width), F32).at[order].set(full)
        row_mass = jnp.zeros((count, rows), F32).at[order].set(row_mass)
        grad_source = lax.psum_scatter(row_mass, AXIS, scatter_dimension=0)[:, None] * (
            source_feats.astype(F32)
        ) - lax.psum_scatter(full, AXIS, scatter_dimension=0)

    final, _ = lax.optimization_barrier((final, gate))
    potential_src, potential_tgt = call(
        functools.partial(potential_kernel, count, scale),
        "potential",
        [here, col, col_other, g, final, target_feats],
        [shape((1, source_count)), shape((1, cols))],
        scalar=True,
    )
    first, _ = lax.optimization_barrier((early[0], potential_tgt))
    (own_col,) = call(
        col_keep_kernel,
        "col_keep",
        [first, *early[1:], x0, x1],
        [shape((cols, width))],
    )
    factor = target_count / source_count

    def held(p):
        size = parts[p].stop - parts[p].start
        return [pltpu.VMEM((size, width), F32), pltpu.SemaphoreType.DMA((size // 128,))]

    ins = [own_col, back[0], mass, final, target_feats]
    (grad_target,) = call(
        functools.partial(target_kernel, factor, parts[0]),
        "target",
        ins,
        [shape((cols, width))],
        size=4 * cols * width,
        out_hbm=True,
        scratch_shapes=held(0),
    )
    ins = [own_col, back[1], mass, final, target_feats, grad_target]
    kw = dict(size=cols * width, in_hbm=(5,), out_hbm=True, input_output_aliases={5: 0})
    if direct:
        grad_target, grad_source = call(
            functools.partial(last_kernel, factor, parts[1]),
            "last",
            ins + ends,
            [shape((cols, width)), shape((rows, width))],
            scratch_shapes=held(1) + [pltpu.VMEM((rows, width), F32), pltpu.SemaphoreType.DMA],
            **kw,
        )
    else:
        (grad_target,) = call(
            lambda *refs: target_kernel(factor, parts[1], *refs[:5], *refs[6:]),
            "target",
            ins,
            [shape((cols, width))],
            scratch_shapes=held(1),
            **kw,
        )

    potential_src = potential_src.reshape(source_count)
    potential_tgt = potential_tgt.reshape(cols)
    return (grad_source, grad_target, potential_src, potential_tgt)


def solution(mesh):
    return jax.shard_map(
        per_device,
        mesh=mesh,
        in_specs=(
            P(("groups", "tgt"), None),
            P(("groups", "tgt"), None),
            P("groups"),
            P(("groups", "tgt")),
        ),
        out_specs=(
            P(("groups", "tgt"), None),
            P(("groups", "tgt"), None),
            P("groups"),
            P(("groups", "tgt")),
        ),
        check_vma=False,
    )
```

```python
import functools
import math

import jax
import jax.numpy as jnp
from jax import lax
from jax.experimental import pallas as pl
from jax.experimental.pallas import tpu as pltpu
from jax.sharding import PartitionSpec as P

ITERS = 3
AXIS = "tgt"
F32 = jnp.float32
BF16 = jnp.bfloat16
TAIL = 8
LOW = -1e30


def call(body, name, ins, outs, size=1, in_hbm=(), out_hbm=False, scalar=False, **kw):
    held, away = pl.BlockSpec(memory_space=pltpu.VMEM), pl.BlockSpec(memory_space=pl.ANY)
    specs = [away if i in in_hbm else held for i in range(len(ins))]
    if scalar:
        specs[0] = pl.BlockSpec(memory_space=pltpu.SMEM)
    return pl.pallas_call(
        body,
        name=name,
        out_shape=outs,
        in_specs=specs,
        out_specs=[away if out_hbm else held] * len(outs),
        compiler_params=pltpu.CompilerParams(vmem_limit_bytes=12 << 20),
        cost_estimate=pl.CostEstimate(flops=1, bytes_accessed=size, transcendentals=0),
        **kw,
    )(*ins)


def tiles(count):
    step = min(count, 128)
    return [slice(i, i + step) for i in range(0, count, step)]


def shape(dims, dtype=F32):
    return jax.ShapeDtypeStruct(dims, dtype)


def swap(value, mask):
    count = lax.axis_size(AXIS)
    return lax.ppermute(value, AXIS, [(i, i ^ mask) for i in range(count)])


def row_levels(count):
    levels, step = [(1,)], 4
    while step < count:
        if step * 4 <= count:
            levels.append((3 * step, 2 * step, step))
            step *= 4
        else:
            levels.append((step,))
            step *= 2
    return levels


def flip(value, mask, blocks):
    move = (mask & 1) * (blocks // 2) + (mask >> 2)
    if not move:
        return value
    width = value.shape[-1] // blocks
    parts = [value[..., (r ^ move) * width : ((r ^ move) + 1) * width] for r in range(blocks)]
    return jnp.concatenate(parts, axis=-1)


def by_index(value, me, blocks):
    width = value.shape[1] // blocks
    bit = 1
    while bit < blocks:
        parts = [value[:, (r ^ bit) * width : ((r ^ bit) + 1) * width] for r in range(blocks)]
        value = jnp.where((me & bit) != 0, jnp.concatenate(parts, axis=1), value)
        bit *= 2
    return value


def prep_kernel(count, me_ref, logit_ref, rel_ref):
    logit = logit_ref[...]
    logit = logit - jnp.log(jnp.sum(jnp.exp(logit), axis=1, keepdims=True))
    value = by_index(logit, me_ref[0, 0], count)
    rows = logit.shape[1] // count
    lines = count // 4
    for c in range(2):
        for k in range(lines):
            here, there = (c * lines + k) * rows, (4 * k + c) * rows
            rel_ref[:, here : here + rows] = value[:, there : there + rows]


def potential_kernel(
    count, scale, me_ref, own_ref, other_ref, g_ref, last_ref, y_ref, source_ref, target_ref
):
    rows = source_ref.shape[1] // count
    lines = count // 4
    parts = []
    for r in range(count):
        start = ((r & 1) * lines + (r >> 2)) * rows
        ref = other_ref if r & 2 else own_ref
        parts.append(ref[1:2, start : start + rows])
    source_ref[...] = by_index(jnp.concatenate(parts, axis=1), me_ref[0, 0], count)
    cols = target_ref.shape[1]
    wide = y_ref[...].astype(F32)
    square = to_row(jnp.sum(wide * wide, axis=1, keepdims=True))
    target_ref[...] = g_ref[:, :cols] + jnp.log(last_ref[:, :cols]) + scale * square


def diagonal():
    return lax.broadcasted_iota(jnp.int32, (128, 128), 0) == lax.broadcasted_iota(
        jnp.int32, (128, 128), 1
    )


def to_column(row):
    same = diagonal()
    parts = [
        jnp.sum(
            jnp.where(same, jnp.broadcast_to(row[:, i : i + 128], (128, 128)), 0.0),
            axis=1,
            keepdims=True,
        )
        for i in range(0, row.shape[1], 128)
    ]
    return jnp.concatenate(parts, axis=0)


def to_row(column):
    same = diagonal()
    parts = [
        jnp.sum(
            jnp.where(same, jnp.broadcast_to(column[i : i + 128, :], (128, 128)), 0.0),
            axis=0,
            keepdims=True,
        )
        for i in range(0, column.shape[0], 128)
    ]
    return jnp.concatenate(parts, axis=1)


def cost_kernel(scale, copy, fresh, add_mass, cols, line, *refs):
    count = len(cols)
    x_refs, y_refs, side_refs = refs[:2], refs[2 : 2 + count], refs[2 + count : 2 + 2 * count]
    pack_ref = refs[2 + 2 * count]
    outs = refs[-(3 + 2 * copy + fresh) :]
    s_outs, pack_out = outs[:2], outs[2 + 2 * copy]
    half = s_outs[0].shape[1]
    pack_out[...] = pack_ref[...]
    lifts = [side[...] for side in side_refs]
    if fresh:
        logit = lifts[0]
        wide = y_refs[0][...].astype(F32)
        lifts = [to_column(logit) - scale * jnp.sum(wide * wide, axis=1, keepdims=True)]
        outs[-1][...] = lifts[0]
        if add_mass:
            mass = jnp.sum(jnp.exp(logit), axis=1, keepdims=True)
            pack_out[2:3, :] = pack_ref[2:3, :] + mass
    for c in range(2):
        x = x_refs[c][...] if copy else x_refs[c][line, :]
        if copy:
            outs[2 + c][line, :] = x
        lanes = slice(c * half + line.start, c * half + line.stop)
        top, total = pack_ref[0:1, lanes], pack_ref[1:2, lanes]
        for y_ref, lift, here in zip(y_refs, lifts, cols):
            s = (2.0 * scale) * lax.dot_general(
                y_ref[...], x, (((1,), (1,)), ((), ())), preferred_element_type=F32
            )
            s_outs[c][here, line] = s
            s = s + lift
            old, top = top, jnp.maximum(top, jnp.max(s, axis=0, keepdims=True))
            total = total * jnp.exp(old - top) + jnp.sum(jnp.exp(s - top), axis=0, keepdims=True)
        pack_out[0:1, lanes] = top
        pack_out[1:2, lanes] = total


def merge(packs, masks, blocks):
    packs = [flip(p, m, blocks) for p, m in zip(packs, masks)]
    top = functools.reduce(jnp.maximum, [p[0:1] for p in packs])
    total = sum(p[1:2] * jnp.exp(p[0:1] - top) for p in packs)
    return top, total, sum(p[2:3] for p in packs)


def merge_kernel(masks, blocks, *refs):
    top, total, mass = merge([r[...] for r in refs[:-1]], masks, blocks)
    refs[-1][0:1, :] = top
    refs[-1][1:2, :] = total
    refs[-1][2:3, :] = mass


def first_kernel(masks, blocks, *refs):
    pack_refs, refs = refs[: len(masks)], refs[len(masks) :]
    s_refs, refs = refs[:2], refs[2:]
    log_ref, e_ref, col_ref, q_ref, h_ref = refs
    top, total, mass = merge([r[...] for r in pack_refs], masks, blocks)
    h = log_ref[...] + jnp.log(mass)
    h_ref[0:1, :] = h
    h_ref[1:2, :] = mass
    q = h - top - jnp.log(total)
    q_ref[...] = q
    half = s_refs[0].shape[1]
    for t in tiles(e_ref.shape[0]):
        parts = [s_refs[c][t, :] + q[:, c * half : (c + 1) * half] for c in range(2)]
        top = jnp.maximum(*[jnp.max(p, axis=1, keepdims=True) for p in parts])
        total = jnp.zeros_like(top)
        for c in range(2):
            e = jnp.exp(parts[c] - top)
            e_ref[t, c * half : (c + 1) * half] = e
            total = total + jnp.sum(e, axis=1, keepdims=True)
        col_ref[0:1, t] = to_row(top)
        col_ref[1:2, t] = to_row(total)


def turn(value):
    half = value.shape[1] // 2
    return jnp.concatenate([value[:, half:], value[:, :half]], axis=1)


def weighted_rows(e_ref, weight):
    return sum(
        jnp.sum(e_ref[t, :] * to_column(weight[:, t]), axis=0, keepdims=True)
        for t in tiles(e_ref.shape[0])
    )


def first_row_kernel(e_ref, own_ref, other_ref, logit_ref, row_ref, phi_ref, g_ref):
    own, other = own_ref[...], turn(other_ref[...])
    top = jnp.maximum(own[0:1, :], other[0:1, :])
    total = own[1:2, :] * jnp.exp(own[0:1, :] - top) + other[1:2, :] * jnp.exp(other[0:1, :] - top)
    g_ref[...] = -(top + jnp.log(total))
    phi = jnp.exp(own[0:1, :] - top) / total
    phi_ref[...] = phi
    row_ref[...] = weighted_rows(e_ref, jnp.exp(logit_ref[...]) * phi)


def row_kernel(e_ref, own_ref, other_ref, logit_ref, phi_ref, row_ref):
    c = own_ref[...] + turn(other_ref[...])
    row_ref[...] = weighted_rows(e_ref, jnp.exp(logit_ref[...]) * phi_ref[...] / c)


def column_kernel(masks, blocks, *refs):
    sum_refs, refs = refs[: len(masks)], refs[len(masks) :]
    (e_ref, h_ref, phi_ref), rest = refs[:3], refs[3:]
    col_ref = rest[-2] if len(rest) > 1 else rest[0]
    total = sum(flip(r[...], m, blocks) for r, m in zip(sum_refs, masks))
    a = jnp.exp(h_ref[0:1, :]) / total
    for t in tiles(e_ref.shape[0]):
        total = jnp.sum(e_ref[t, :] * a, axis=1, keepdims=True)
        col_ref[0:1, t] = to_row(total) * phi_ref[:, t]
    if len(rest) > 1:
        rest[-1][...] = a
        col_ref[1:2, :] = rest[0][...] + jnp.log(a)


def store_plan(e_ref, a, share, outs):
    for t in tiles(e_ref.shape[0]):
        plan = ((e_ref[t, :] * a) * to_column(share[:, t])).astype(BF16)
        start = 0
        for ref in outs:
            ref[t, :] = plan[:, start : start + ref.shape[1]]
            start += ref.shape[1]


def early_plan_kernel(source_count, e_ref, a_ref, h_ref, logit_ref, phi_ref, *outs):
    *outs, mass_ref = outs
    mass = jnp.exp(logit_ref[...]) * (source_count / h_ref[1:2, :1])
    mass_ref[...] = mass
    store_plan(e_ref, a_ref[...], mass * phi_ref[...], outs)


def plan_kernel(e_ref, a_ref, mass_ref, own_ref, other_ref, phi_ref, *outs):
    *outs, last_ref = outs
    last = 1.0 / (own_ref[0:1, :] + turn(other_ref[0:1, :]))
    last_ref[...] = last
    store_plan(e_ref, a_ref[...], mass_ref[...] * phi_ref[...] * last, outs)


def split_mass(mass, width):
    mass = jnp.concatenate([mass, jnp.zeros((1, width - mass.shape[1]), F32)], axis=1)
    high = mass.astype(BF16).astype(F32)
    rest = mass - high
    middle = rest.astype(BF16).astype(F32)
    row = lax.broadcasted_iota(jnp.int32, (TAIL, width), 0)
    out = jnp.where(row == 0, high, jnp.where(row == 1, middle, rest - middle))
    return jnp.where(row < 3, out, 0.0).astype(BF16)


def joined_mass(ref, width):
    return jnp.sum(ref[ref.shape[0] - TAIL :, :width].astype(F32), axis=0, keepdims=True)


def row_part_kernel(lanes, count, keep_ref, other_ref, *refs):
    y_refs, out_refs = refs[:-count], refs[-count:]
    group = len(y_refs) // 2
    part = mass = 0.0
    for plan_ref, part_lanes, ys in (
        (keep_ref, lanes, y_refs[:group]),
        (other_ref, slice(None), y_refs[group:]),
    ):
        start = 0
        for y in ys:
            block = plan_ref[start : start + y.shape[0], part_lanes]
            start += y.shape[0]
            part = part + lax.dot_general(
                block, y[...], (((0,), (0,)), ((), ())), preferred_element_type=F32
            )
            mass = mass + jnp.sum(block.astype(F32), axis=0, keepdims=True)
    rows, width = out_refs[0].shape[0] - TAIL, out_refs[0].shape[1]
    for n, ref in enumerate(out_refs):
        here = slice(n * rows, (n + 1) * rows)
        ref[:rows, :] = part[here, :].astype(ref.dtype)
        if ref.dtype == BF16:
            ref[rows:, :] = split_mass(mass[:, here], width)
        else:
            ref[rows:, :rows] = jnp.broadcast_to(mass[:, here], (TAIL, rows))
            ref[rows:, rows:] = jnp.zeros((TAIL, width - rows), F32)


def contract(plan_ref, lanes, y_refs):
    part = mass = 0.0
    start = 0
    for y in y_refs:
        block = plan_ref[start : start + y.shape[0], lanes]
        start += y.shape[0]
        part = part + lax.dot_general(
            block, y[...], (((0,), (0,)), ((), ())), preferred_element_type=F32
        )
        mass = mass + jnp.sum(block.astype(F32), axis=0, keepdims=True)
    return part, mass


def far_own_kernel(lanes, plan_ref, *refs):
    *y_refs, out_ref = refs
    part, mass = contract(plan_ref, lanes, y_refs)
    rows, width = part.shape
    out_ref[:rows, :] = part
    out_ref[rows:, :rows] = jnp.broadcast_to(mass, (TAIL, rows))
    out_ref[rows:, rows:] = jnp.zeros((TAIL, width - rows), F32)


def far_send_kernel(own_ref, plan_ref, *refs):
    *y_refs, out_ref = refs
    part, mass = contract(plan_ref, slice(None), y_refs)
    rows, width = part.shape
    out_ref[:rows, :] = (own_ref[:rows, :] + part).astype(BF16)
    out_ref[rows:, :] = split_mass(own_ref[rows : rows + 1, :rows] + mass, width)


def line_kernel(own_ref, other_ref, out_ref):
    rows, width = out_ref.shape[0] - TAIL, out_ref.shape[1]
    out_ref[:rows, :] = (own_ref[:rows, :] + other_ref[:rows, :].astype(F32)).astype(BF16)
    mass = own_ref[rows : rows + 1, :rows] + joined_mass(other_ref, rows)
    out_ref[rows:, :] = split_mass(mass, width)


def source_kernel(own_ref, near_ref, far_ref, x_ref, out_ref):
    rows = out_ref.shape[0]
    part = own_ref[:rows, :] + near_ref[:rows, :].astype(F32) + far_ref[:rows, :].astype(F32)
    mass = own_ref[rows : rows + 1, :rows] + joined_mass(near_ref, rows)
    mass = mass + joined_mass(far_ref, rows)
    out_ref[...] = to_column(mass) * x_ref[:rows, :].astype(F32) - part


def col_part(keep_ref, near_ref, far_ref, x0_ref, x1_ref, cols):
    near = near_ref.shape[1]
    part = jnp.dot(keep_ref[cols, :], x0_ref[...], preferred_element_type=F32)
    part = part + jnp.dot(near_ref[cols, :], x1_ref[:near, :], preferred_element_type=F32)
    return part + jnp.dot(far_ref[cols, :], x1_ref[near:, :], preferred_element_type=F32)


def col_send_kernel(cols, *refs):
    *refs, out_ref = refs
    out_ref[...] = col_part(*refs, cols).astype(BF16)


def col_keep_kernel(*refs):
    *refs, out_ref = refs
    out_ref[...] = col_part(*refs, slice(0, out_ref.shape[0]))


def target_rows(
    factor, cols, own_ref, other_ref, mass_ref, last_ref, y_ref, out_ref, held_ref, sem_ref
):
    count = cols.stop - cols.start
    mass, last = mass_ref[:, cols], last_ref[:, cols]
    copies = []
    for n, t in enumerate(slice(i, i + 128) for i in range(0, count, 128)):
        here = slice(cols.start + t.start, cols.start + t.stop)
        part = own_ref[here, :] + other_ref[t, :].astype(F32)
        part = to_column(last[:, t]) * part
        held_ref[t, :] = factor * (to_column(mass[:, t]) * y_ref[here, :].astype(F32) - part)
        copies.append(pltpu.make_async_copy(held_ref.at[t], out_ref.at[here], sem_ref.at[n]))
        copies[-1].start()
    return copies


def target_kernel(factor, cols, *refs):
    for copy in target_rows(factor, cols, *refs):
        copy.wait()


def last_kernel(factor, cols, *refs):
    target_ins, (_, own_ref, near_ref, far_ref, x_ref), refs = refs[:5], refs[5:10], refs[10:]
    target_out, source_out, held_target, sem_target, held_source, sem_source = refs
    source_kernel(own_ref, near_ref, far_ref, x_ref, held_source)
    first = pltpu.make_async_copy(held_source, source_out, sem_source)
    first.start()
    copies = target_rows(factor, cols, *target_ins, target_out, held_target, sem_target)
    for copy in [first, *copies]:
        copy.wait()


def per_device(source_feats, target_feats, source_logits, target_logits):
    count = lax.axis_size(AXIS)
    me = lax.axis_index(AXIS)
    rows, width = source_feats.shape
    cols = target_feats.shape[0]
    source_count = rows * count
    target_count = cols * count
    scale = 1.0 / math.sqrt(width)
    direct = count == 16
    blocks = count // 2
    lines = blocks // 2
    mine = source_count // 2
    half = mine // 2
    parts = [slice(0, cols * 3 // 4), slice(cols * 3 // 4, cols)]
    masks = [4 * k + c for c in range(2) for k in range(lines)]
    order = jnp.bitwise_xor(me, jnp.array(masks))

    if direct:
        far = swap(source_feats, 8)
        line = [source_feats, swap(source_feats, 4), far]
    crossed = [swap(target_feats, 2)]
    logits_here = target_logits.reshape(1, cols)
    logits_there = swap(logits_here, 2)
    logits = jnp.concatenate([logits_here, logits_there], axis=1)
    here = me.astype(jnp.int32).reshape(1, 1)
    (source_log,) = call(
        functools.partial(prep_kernel, count),
        "prep",
        [here, source_logits.reshape(1, source_count)],
        [shape((1, mine))],
        scalar=True,
    )
    logits_here, source_log = lax.optimization_barrier((logits_here, source_log))
    pack = jnp.concatenate([jnp.full((1, mine), LOW, F32), jnp.zeros((2, mine), F32)])

    s_shape, x_shape = shape((2 * cols, half)), shape((half, width), BF16)
    here_cols, there_cols = slice(0, cols), slice(cols, 2 * cols)
    lift_shape = shape((cols, 1))

    def cost(xs, ys, sides, where, line, store, pack, copy=False, fresh=False):
        ins = [*xs, *ys, *sides, pack]
        return call(
            functools.partial(cost_kernel, scale, copy, fresh, fresh, where, line),
            "cost",
            ins + store,
            [s_shape] * 2 + [x_shape] * 2 * copy + [shape(pack.shape)] + [lift_shape] * fresh,
            input_output_aliases={len(ins) + i: i for i in range(len(store))},
        )

    if direct:
        store = []
        for k in (0, 2, 1, 3):
            x, ours, sides, where = line[k], [target_feats], [], [here_cols]
            if k == 0:
                sides = [logits_here]
            if k == 3:
                x, *_ = lax.optimization_barrier((x, logits_there, pack))
                s0, s1, pack, lift_there = cost(
                    store[2:],
                    crossed,
                    [logits_there],
                    [there_cols],
                    slice(0, k * rows),
                    store[:2],
                    pack,
                    fresh=True,
                )
                store = [s0, s1, *store[2:]]
                ours, where = [target_feats, *crossed], [here_cols, there_cols]
                sides = [lift, lift_there]
            *store, pack = cost(
                [x, swap(x, 1)],
                ours,
                sides or [lift],
                where,
                slice(k * rows, (k + 1) * rows),
                store,
                pack,
                copy=True,
                fresh=k == 0,
            )
            if k == 0:
                *store, pack, lift = [*store, pack]
                line[2], y, _ = lax.optimization_barrier((line[2], target_feats, pack))
                line.append(swap(line[2], 4))
                ys = [target_feats, swap(y, 1)]
        s0, s1, x0, x1 = store
    else:
        gathered = lax.all_gather(source_feats, AXIS, axis=0)[order].reshape(2, half, width)
        x0, x1 = gathered[0], gathered[1]
        store = []
        for y, logit, where in (
            (target_feats, logits_here, here_cols),
            (crossed[0], logits_there, there_cols),
        ):
            *store, pack, _ = cost(
                [x0, x1], [y], [logit], [where], slice(0, half), store, pack, fresh=True
            )
        s0, s1 = store

    *levels, last = row_levels(count)
    last_masks = (0, *last)
    for level in levels:
        packs = [pack] + [swap(pack, m) for m in level]
        (pack,) = call(
            functools.partial(merge_kernel, (0, *level), blocks),
            "merge",
            packs,
            [shape(pack.shape)],
        )
    packs = [pack] + [swap(pack, m) for m in last]

    flat_shape, lane_shape = shape((1, mine)), shape((1, 2 * cols))
    e_shape = shape((2 * cols, mine))

    e, col, q, h = call(
        functools.partial(first_kernel, last_masks, blocks),
        "first",
        [*packs, s0, s1, source_log],
        [e_shape, shape((2, 2 * cols)), flat_shape, shape((2, mine))],
    )
    col_other = swap(col, 2)
    if direct:
        crossed, _ = lax.optimization_barrier((crossed, h))
        ys = [ys[0], crossed[0], ys[1], swap(crossed[0], 1)]
    row, phi, g = call(
        first_row_kernel,
        "first_row",
        [e, col, col_other, logits],
        [flat_shape, lane_shape, lane_shape],
    )

    if direct:
        row, *ys = lax.optimization_barrier((row, *ys))

    def columns(row, *base):
        for level in levels:
            row = row + sum(flip(swap(row, m), m, blocks) for m in level)
        sums = [row] + [swap(row, m) for m in last]
        return call(
            functools.partial(column_kernel, last_masks, blocks),
            "column",
            [*sums, e, h, phi, *base],
            [shape((1 + len(base), 2 * cols))] + [flat_shape] * len(base),
        )

    for _ in range(ITERS - 2):
        (col,) = columns(row)
        (row,) = call(
            row_kernel,
            "row",
            [e, col, swap(col, 2), logits, phi],
            [flat_shape],
        )
    assert mine == 2 * cols
    source_sq = scale * jnp.concatenate(
        [jnp.sum(jnp.square(x.astype(F32)), axis=1) for x in (x0, x1)]
    )
    base = q - source_log + source_sq.reshape(1, mine)
    col, a = columns(row, base)
    col_other = swap(col, 2)
    plan_shapes = [shape((2 * cols, n), BF16) for n in (half, half * 3 // 4, half // 4)]
    *early, mass = call(
        functools.partial(early_plan_kernel, source_count),
        "early_plan",
        [e, a, h, logits, phi],
        plan_shapes + [lane_shape],
    )

    def col_send(p, first):
        piece = slice(cols + parts[p].start, cols + parts[p].stop)
        (out,) = call(
            functools.partial(col_send_kernel, piece),
            "col_send",
            [first, *early[1:], x0, x1],
            [shape((parts[p].stop - parts[p].start, width), BF16)],
        )
        return out

    out = col_send(0, early[0])
    back = [swap(out, 2)]
    col_last, _ = lax.optimization_barrier((col_other, out))
    keep, *sends, final = call(
        plan_kernel,
        "plan",
        [e, a, mass, col, col_last, phi],
        plan_shapes + [lane_shape],
    )
    if direct:
        others = [None, swap(sends[1], 1)]
        others[0] = swap(sends[0], 1)
        block, block_out = shape((rows + TAIL, width)), shape((rows + TAIL, width), BF16)

        far = slice(3 * rows, half)
        (own3,) = call(
            functools.partial(far_own_kernel, far), "far_own", [keep, *ys[:2]], [block]
        )
        (out3,) = call(far_send_kernel, "far_send", [own3, others[1], *ys[2:]], [block_out])
        near3 = swap(out3, 4)
        first, _ = lax.optimization_barrier((early[0], out3))
        out = col_send(1, first)
        back.append(swap(out, 2))
        rest, _ = lax.optimization_barrier((keep, out))
        own0, out1, own2 = call(
            functools.partial(row_part_kernel, slice(0, 3 * rows), 3),
            "row_part",
            [rest, others[0], *ys],
            [block, block_out, block],
        )
        near1 = swap(out1, 4)
        (out2,) = call(line_kernel, "line", [own2, near3], [block_out])
        far2 = swap(out2, 8)
        ends = [own0, near1, far2, x0]
        gate = near1
    else:
        out = col_send(1, early[0])
        back.append(swap(out, 2))
        gate = out
        plan = jnp.concatenate([keep, *sends], axis=1)
        both = jnp.concatenate([target_feats, *crossed], axis=0)
        full = lax.dot_general(
            plan, both, (((0,), (0,)), ((), ())), preferred_element_type=F32
        ).reshape(blocks, rows, width)
        row_mass = jnp.sum(plan.astype(F32), axis=0).reshape(blocks, rows)
        full = jnp.zeros((count, rows, width), F32).at[order].set(full)
        row_mass = jnp.zeros((count, rows), F32).at[order].set(row_mass)
        grad_source = lax.psum_scatter(row_mass, AXIS, scatter_dimension=0)[:, None] * (
            source_feats.astype(F32)
        ) - lax.psum_scatter(full, AXIS, scatter_dimension=0)

    final, _ = lax.optimization_barrier((final, gate))
    potential_src, potential_tgt = call(
        functools.partial(potential_kernel, count, scale),
        "potential",
        [here, col, col_other, g, final, target_feats],
        [shape((1, source_count)), shape((1, cols))],
        scalar=True,
    )
    first, _ = lax.optimization_barrier((early[0], potential_tgt))
    (own_col,) = call(
        col_keep_kernel,
        "col_keep",
        [first, *early[1:], x0, x1],
        [shape((cols, width))],
    )
    factor = target_count / source_count

    def held(p):
        size = parts[p].stop - parts[p].start
        return [pltpu.VMEM((size, width), F32), pltpu.SemaphoreType.DMA((size // 128,))]

    ins = [own_col, back[0], mass, final, target_feats]
    (grad_target,) = call(
        functools.partial(target_kernel, factor, parts[0]),
        "target",
        ins,
        [shape((cols, width))],
        size=4 * cols * width,
        out_hbm=True,
        scratch_shapes=held(0),
    )
    ins = [own_col, back[1], mass, final, target_feats, grad_target]
    kw = dict(size=cols * width, in_hbm=(5,), out_hbm=True, input_output_aliases={5: 0})
    if direct:
        grad_target, grad_source = call(
            functools.partial(last_kernel, factor, parts[1]),
            "last",
            ins + ends,
            [shape((cols, width)), shape((rows, width))],
            scratch_shapes=held(1) + [pltpu.VMEM((rows, width), F32), pltpu.SemaphoreType.DMA],
            **kw,
        )
    else:
        (grad_target,) = call(
            lambda *refs: target_kernel(factor, parts[1], *refs[:5], *refs[6:]),
            "target",
            ins,
            [shape((cols, width))],
            scratch_shapes=held(1),
            **kw,
        )

    potential_src = potential_src.reshape(source_count)
    potential_tgt = potential_tgt.reshape(cols)
    return (grad_source, grad_target, potential_src, potential_tgt)


def solution(mesh):
    return jax.shard_map(
        per_device,
        mesh=mesh,
        in_specs=(
            P(("groups", "tgt"), None),
            P(("groups", "tgt"), None),
            P("groups"),
            P(("groups", "tgt")),
        ),
        out_specs=(
            P(("groups", "tgt"), None),
            P(("groups", "tgt"), None),
            P("groups"),
            P(("groups", "tgt")),
        ),
        check_vma=False,
    )
```
